32 devices in a mesh: gx: 8 (over z, core), gy: 2 (over y), vert: 2 (over x).
Axes of the slice: x: 2, y: 2, z: 4, core: 2. Of those that a mesh axis runs over, the one named last changes fastest.
Arguments:
- vectors: float32 [16, 64, 16, 128], P('vert', 'gx', 'gy'), may hold values from -6 to 6
- conductivity: float32 [64, 16, 128], P('gx', 'gy'), may hold values from 0.3 to 3
- c_points: int32 [64, 16, 16], P('gx', 'gy'), may hold values from -1 to 127, as said below
Outputs:
- interp: float32 [64, 16, 16, 128], P('gx', 'gy')
- coarse: float32 [64, 16, 9, 256], P('gx', 'gy')
The draws below stay inside these ranges and needn't reach their ends.
Inputs may be any that keep to these rules, and one draw needn't show every extreme that they name: `c_points`: in each tile column the used slots come first, hold distinct positions in increasing order, and number at least 8; some column uses all 16 slots.
All inputs are finite; a program needn't handle non-finite values.
Results may differ from the reference program's by a relative error of at most 0.0003.
Values sent between devices are 32-bit elements; how exact they have to be, the bound alone decides.
A program may use at most 64 MiB of HBM per device.

```python
import math
import jax
import jax.numpy as jnp
from jax import lax

NZ = 128
VECS = 16
CPTS = 16
SWEEPS = 3
NX = 64
NY = 16


def draw_c_points(key, part):
    columns = NX * NY
    keys = jax.random.split(jax.random.fold_in(key, 11), columns)
    chosen = jax.vmap(lambda single: jax.random.permutation(single, NZ)[:CPTS])(keys)
    chosen = jnp.sort(chosen.astype(jnp.int32), axis=1)
    counts = jax.random.randint(jax.random.fold_in(key, 23), (columns,), CPTS // 2, CPTS + 1)
    counts = counts.at[0].set(CPTS)
    slots = jnp.arange(CPTS, dtype=jnp.int32)[None, :]
    result = jnp.where(slots < counts[:, None], chosen, -1)
    return result.reshape(NX, NY, CPTS).astype(jnp.int32)


def level_of(stream_key, dims, pieces, least, largest):
    gain = 1.0
    for dim, parts in pieces:
        heights = jax.random.uniform(jax.random.fold_in(jax.random.fold_in(stream_key, 6), dim), (parts,), jnp.float32, least / len(pieces), largest / len(pieces))
        gain = gain * jnp.repeat(jnp.exp(heights), dims[dim] // parts).reshape((-1,) + (1,) * (len(dims) - 1 - dim))
    return gain


def scatter_about(rng, extent, spread, most, cuts=(), kind=jnp.bfloat16):
    loudness = level_of(rng, extent, cuts, -0.22, 0.18) if cuts else 1.0
    values = jax.random.normal(rng, extent, jnp.float32) * spread * loudness
    return jnp.minimum(jnp.maximum(values, -most), most).astype(kind)


def setup_inputs(seed: int = 0) -> dict:
    streams_of = jax.random.split(jax.random.key(seed), 4)
    return {
        "vectors": scatter_about(streams_of[0], (VECS, NX, NY, NZ), 1.0, 6.0, ((0, 2), (1, 8), (2, 2)), jnp.float32),
        "conductivity": jnp.clip(jnp.exp(math.log(3.0) - 2.3025851 * jax.random.uniform(streams_of[1], (NX, NY, NZ), jnp.float32) ** level_of(streams_of[1], (NX, NY, NZ), ((0, 8), (1, 2)), -0.2, 0.2)), 0.3, 3.0),
        "c_points": draw_c_points(jax.random.fold_in(streams_of[3], 71), 0),
    }


ANISOTROPY = (1.0, 0.6, 0.15)
OMEGA = 0.6
SHIFT = 0.5
RIDGE = 0.1

def stencil_offsets():
    result = []
    for move_x in (-1, 0, 1):
        for move_y in (-1, 0, 1):
            for move_z in (-1, 0, 1):
                if move_x != 0 or move_y != 0 or move_z != 0:
                    result.append((move_x, move_y, move_z))
    return result

def coupling(move):
    weight = 1.0
    for axis_no in range(3):
        if move[axis_no] != 0:
            weight = weight * ANISOTROPY[axis_no]
    return weight

def window_of(move, shape):
    return tuple((slice(1 + move[axis_no], 1 + move[axis_no] + shape[axis_no]) for axis_no in range(3)))

def operator_apply(padded, kpad):
    shape = (kpad.shape[0] - 2, kpad.shape[1] - 2, kpad.shape[2] - 2)
    interior = kpad[1:-1, 1:-1, 1:-1]
    centre = padded[:, 1:-1, 1:-1, 1:-1]
    diagonal = SHIFT * interior * interior
    nearby = jnp.zeros_like(centre)
    for move in stencil_offsets():
        window = window_of(move, shape)
        couple = coupling(move) * interior * kpad[window]
        diagonal = diagonal + couple
        nearby = nearby + couple * padded[(slice(None),) + window]
    return (diagonal * centre - nearby, diagonal, centre)

def jacobi(padded, kpad):
    image, diagonal, centre = operator_apply(padded, kpad)
    alive = diagonal > 0.0
    guarded = jnp.where(alive, diagonal, 1.0)
    return jnp.where(alive, centre - OMEGA * image / guarded, 0.0)

def gram_terms(field, c_points):
    depth = field.shape[-1]
    onehot = (c_points[..., None] == jnp.arange(depth, dtype=jnp.int32)).astype(jnp.float32)
    cvals = jnp.einsum('vxyz,xyjz->vxyj', field, onehot, precision=lax.Precision.HIGHEST)
    right = jnp.einsum('vxyz,vxyj->xyjz', field, cvals, precision=lax.Precision.HIGHEST)
    gram = jnp.einsum('vxyi,vxyj->xyij', cvals, cvals, precision=lax.Precision.HIGHEST)
    return (right, gram, onehot)

def solve_interp(right, gram, onehot):
    slots = gram.shape[-1]
    ridge = RIDGE * jnp.trace(gram, axis1=2, axis2=3) / slots + 1e-06
    system = gram + ridge[:, :, None, None] * jnp.eye(slots, dtype=jnp.float32)
    lower = jnp.linalg.cholesky(system)
    weights = jax.scipy.linalg.cho_solve((lower, True), right)
    c_row = jnp.sum(onehot, axis=2)
    return weights * (1.0 - c_row[:, :, None, :]) + onehot

def galerkin(interp, ppad, kpad):
    shape = (kpad.shape[0] - 2, kpad.shape[1] - 2, kpad.shape[2] - 2)
    interior = kpad[1:-1, 1:-1, 1:-1]
    diagonal = SHIFT * interior * interior
    for move in stencil_offsets():
        diagonal = diagonal + coupling(move) * interior * kpad[window_of(move, shape)]
    blocks = []
    slots = interp.shape[2]
    for move_x in (-1, 0, 1):
        for move_y in (-1, 0, 1):
            if move_x == 0 and move_y == 0:
                image = diagonal[:, :, None, :] * interp
            else:
                image = jnp.zeros_like(interp)
            for move_z in (-1, 0, 1):
                if move_x == 0 and move_y == 0 and (move_z == 0):
                    continue
                move = (move_x, move_y, move_z)
                window = window_of(move, shape)
                couple = coupling(move) * interior * kpad[window]
                source = ppad[window[0], window[1], :, window[2]]
                image = image - couple[:, :, None, :] * source
            block = jnp.einsum('xyiz,xyjz->xyij', interp, image, precision=lax.Precision.HIGHEST)
            blocks.append(block.reshape(shape[0], shape[1], slots * slots))
    return jnp.stack(blocks, axis=2)

def reference(vectors, conductivity, c_points):
    kpad = jnp.pad(conductivity, 1)
    field = vectors
    for turn in range(SWEEPS):
        field = jacobi(jnp.pad(field, ((0, 0), (1, 1), (1, 1), (1, 1))), kpad)
    right, gram, onehot = gram_terms(field, c_points)
    interp = solve_interp(right, gram, onehot)
    ppad = jnp.pad(interp, ((1, 1), (1, 1), (0, 0), (1, 1)))
    coarse = galerkin(interp, ppad, kpad)
    return (interp, coarse)
```

```python
import functools

import jax
import jax.numpy as jnp
from jax import lax
from jax.experimental import pallas as pl
from jax.experimental.pallas import tpu as pltpu
from jax.sharding import PartitionSpec as P

SWEEPS = 3
ANISOTROPY = (1.0, 0.6, 0.15)
OMEGA = 0.6
SHIFT = 0.5
RIDGE = 0.1
HALO = SWEEPS
GROUP = 8
BATCH = 13
BATCH_2 = 2
MESH = pl.DeviceIdType.MESH
F32 = jnp.float32
BF16 = jnp.bfloat16


def smear_z(x):
    axis = x.ndim - 1
    depth = x.shape[axis]
    lane = lax.broadcasted_iota(jnp.int32, x.shape, axis)
    below = jnp.where(lane == 0, 0.0, pltpu.roll(x, 1, axis))
    above = jnp.where(lane == depth - 1, 0.0, pltpu.roll(x, depth - 1, axis))
    return x + ANISOTROPY[2] * (below + above)


def smear_xy(ref, row, col, pick):
    return pick(ref, row, col) + ANISOTROPY[0] * (pick(ref, row - 1, col) + pick(ref, row + 1, col))


def smear_row(ref, row, first, last, pick):
    across = {col: smear_xy(ref, row, col, pick) for col in range(first - 1, last + 1)}
    return [
        smear_z(across[col] + ANISOTROPY[1] * (across[col - 1] + across[col + 1]))
        for col in range(first, last)
    ]


def span(move, size):
    if move == 0:
        return pl.ds(0, size), pl.ds(HALO, size)
    if move > 0:
        return pl.ds(size - HALO, HALO), pl.ds(0, HALO)
    return pl.ds(0, HALO), pl.ds(size + HALO, HALO)


def hole(move, size):
    if move == 0:
        return pl.ds(HALO, size)
    return pl.ds(size + HALO, HALO) if move > 0 else pl.ds(0, HALO)


def rim(move, size):
    if move == 0:
        return pl.ds(1, size)
    return pl.ds(size + 1, 1) if move > 0 else pl.ds(0, 1)


def smooth_kernel(
    nx, ny, nv, raw_ref, k_ref, c_ref, out_ref, knots_ref, spots_ref,
    one, two, gain, wide_k, wide_c, ksend, krecv, csend, crecv, vsend, vrecv,
    fsend, frecv, hsend, hrecv, v_ref, turn, load,
):
    size_x, size_y, vecs, depth = v_ref.shape
    wide_x, wide_y = size_x + 2 * HALO, size_y + 2 * HALO
    gx, gy, gv = lax.axis_index("gx"), lax.axis_index("gy"), lax.axis_index("vert")
    moves = [(mx, my) for mx in (-1, 0, 1) for my in (-1, 0, 1) if (mx, my) != (0, 0)]

    def inside(mx, my):
        ok_x = jnp.logical_and(gx + mx >= 0, gx + mx < nx)
        ok_y = jnp.logical_and(gy + my >= 0, gy + my < ny)
        return jnp.logical_and(ok_x, ok_y)

    inner = pl.ds(HALO, size_x), pl.ds(HALO, size_y)
    loads = [
        pltpu.make_async_copy(source, target.at[inner], load.at[no])
        for no, (source, target) in enumerate(((k_ref, wide_k), (c_ref, wide_c)))
    ]
    for copy in loads:
        copy.start()
    turns = [
        pltpu.make_async_copy(raw_ref.at[vec], v_ref.at[:, :, vec], turn.at[vec])
        for vec in range(vecs)
    ]
    for copy in turns:
        copy.start()

    barrier = pltpu.get_barrier_semaphore()
    total = jnp.int32(nv - 1)
    for mx, my in moves:
        here = inside(mx, my)

        @pl.when(here)
        def _():
            pl.semaphore_signal(
                barrier, inc=1, device_id=(gx + mx, gy + my, gv), device_id_type=MESH
            )

        total = total + here.astype(jnp.int32)
    for step in range(1, nv):
        pl.semaphore_signal(
            barrier, inc=1, device_id=(gx, gy, lax.rem(gv + step, nv)), device_id_type=MESH
        )
    pl.semaphore_wait(barrier, total)

    kinds = (
        (wide_k.at[inner], wide_k, ksend, krecv), (v_ref, one, vsend, vrecv),
        (wide_c.at[inner], wide_c, csend, crecv),
    )
    for copy in loads:
        copy.wait()

    def departure(kind, no):
        mx, my = moves[no]
        source, target, send, recv = kinds[kind]
        from_x, to_x = span(mx, size_x)
        from_y, to_y = span(my, size_y)
        return pltpu.make_async_remote_copy(
            src_ref=source.at[from_x, from_y], dst_ref=target.at[to_x, to_y],
            send_sem=send.at[no], recv_sem=recv.at[no],
            device_id=(gx + mx, gy + my, gv), device_id_type=MESH,
        )

    def arrival(kind, no):
        mx, my = moves[no]
        other = moves.index((-mx, -my))
        _, target, send, recv = kinds[kind]
        place = target.at[hole(mx, size_x), hole(my, size_y)]
        return pltpu.make_async_remote_copy(
            src_ref=place, dst_ref=place, send_sem=send.at[other], recv_sem=recv.at[other],
            device_id=(gx + mx, gy + my, gv), device_id_type=MESH,
        )

    for no, (mx, my) in enumerate(moves):

        @pl.when(inside(mx, my))
        def _():
            departure(0, no).start()

        @pl.when(jnp.logical_not(inside(mx, my)))
        def _():
            at_x, at_y = hole(mx, size_x), hole(my, size_y)
            for source, target, _, _ in kinds:
                target[at_x, at_y] = jnp.zeros(
                    (at_x.size, at_y.size) + source.shape[2:], source.dtype
                )
            rim_x, rim_y = rim(mx, size_x), rim(my, size_y)
            out_ref[:, rim_x, rim_y] = jnp.zeros((nv, rim_x.size, rim_y.size, vecs, depth), F32)

    for copy in turns:
        copy.wait()
    for kind in (1, 2):
        for no, (mx, my) in enumerate(moves):

            @pl.when(inside(mx, my))
            def _():
                departure(kind, no).start()

    one[inner] = v_ref[...]

    for no, (mx, my) in enumerate(moves):

        @pl.when(inside(mx, my))
        def _():
            arrival(0, no).wait_recv()

    def pick_k(ref, row, col):
        return ref[row, col, 0:1, :]

    def pick_u(ref, row, col):
        return ref[row, col]

    def gains(row, carry):
        around = smear_row(wide_k, row, 1, wide_y - 1, pick_k)
        for col in range(1, wide_y - 1):
            mid = pick_k(wide_k, row, col)
            below = around[col - 1] - (1.0 - SHIFT) * mid
            alive = mid > 0.0
            value = jnp.where(alive, OMEGA * mid / jnp.where(alive, below, 1.0), 0.0)
            gain[row, col] = jnp.broadcast_to(value, (vecs, depth))
        return carry

    lax.fori_loop(1, wide_x - 1, gains, 0, unroll=2)

    for no, (mx, my) in enumerate(moves):

        @pl.when(inside(mx, my))
        def _():
            arrival(1, no).wait_recv()

    def scale(row, carry):
        for col in range(wide_y):
            one[row, col] = one[row, col] * jnp.broadcast_to(pick_k(wide_k, row, col), (vecs, depth))
        return carry

    lax.fori_loop(0, wide_x, scale, 0, unroll=2)

    def relaxed(ref, row, first, last):
        around = smear_row(ref, row, first, last, pick_u)
        result = []
        for col in range(first, last):
            factor = gain[row, col]
            result.append((1.0 - OMEGA - factor) * ref[row, col] + factor * around[col - first])
        return result

    source, target = one, two
    for sweep in range(1, SWEEPS):

        def step(row, carry, source=source, target=target, sweep=sweep):
            for no, value in enumerate(relaxed(source, row, sweep, wide_y - sweep)):
                target[row, sweep + no] = value
            return carry

        lax.fori_loop(sweep, wide_x - sweep, step, 0, unroll=2)
        source, target = target, source

    def last_sweep(row, carry):
        for no, value in enumerate(relaxed(source, row, SWEEPS, wide_y - SWEEPS)):
            out_ref[gv, row - SWEEPS + 1, no + 1] = value
        return carry

    lax.fori_loop(SWEEPS, wide_x - SWEEPS, last_sweep, 0, unroll=2)

    pieces = (
        (pl.ds(1, 1), pl.ds(1, size_y)),
        (pl.ds(size_x, 1), pl.ds(1, size_y)),
        (pl.ds(2, size_x - 2), pl.ds(1, 1)),
        (pl.ds(2, size_x - 2), pl.ds(size_y, 1)),
        (pl.ds(2, size_x - 2), pl.ds(2, size_y - 2)),
    )

    def piece_copy(no, step, half):
        place = out_ref.at[(half,) + pieces[no]]
        return pltpu.make_async_remote_copy(
            src_ref=place, dst_ref=place,
            send_sem=fsend.at[step - 1, no], recv_sem=frecv.at[step - 1, no],
            device_id=(gx, gy, lax.rem(gv + step, nv)), device_id_type=MESH,
        )

    def edge(move, size):
        if move == 0:
            return pl.ds(1, size), pl.ds(1, size)
        if move > 0:
            return pl.ds(size, 1), pl.ds(0, 1)
        return pl.ds(1, 1), pl.ds(size + 1, 1)

    def rim_departure(step, half, no):
        mx, my = moves[no]
        from_x, to_x = edge(mx, size_x)
        from_y, to_y = edge(my, size_y)
        return pltpu.make_async_remote_copy(
            src_ref=out_ref.at[half, from_x, from_y], dst_ref=out_ref.at[half, to_x, to_y],
            send_sem=hsend.at[step, no], recv_sem=hrecv.at[step, no],
            device_id=(gx + mx, gy + my, gv), device_id_type=MESH,
        )

    def rim_arrival(step, half, no):
        mx, my = moves[no]
        other = moves.index((-mx, -my))
        place = out_ref.at[half, edge(-mx, size_x)[1], edge(-my, size_y)[1]]
        return pltpu.make_async_remote_copy(
            src_ref=place, dst_ref=place,
            send_sem=hsend.at[step, other], recv_sem=hrecv.at[step, other],
            device_id=(gx + mx, gy + my, gv), device_id_type=MESH,
        )

    for no in range(len(pieces)):
        for step in range(1, nv):
            piece_copy(no, step, gv).start()
    for step in range(nv):
        half = lax.rem(gv - step + nv, nv)
        if step > 0:
            for no in range(len(pieces) - 1):
                piece_copy(no, step, half).wait_recv()
        for no, (mx, my) in enumerate(moves):

            @pl.when(inside(mx, my))
            def _():
                rim_departure(step, half, no).start()

    for no, (mx, my) in enumerate(moves):

        @pl.when(inside(mx, my))
        def _():
            arrival(2, no).wait_recv()

    rim_x, rim_y = pl.ds(HALO - 1, size_x + 2), pl.ds(HALO - 1, size_y + 2)
    knots_ref[...] = wide_k[rim_x, rim_y]
    spots_ref[...] = wide_c[rim_x, rim_y]

    for step in range(1, nv):
        piece_copy(len(pieces) - 1, step, lax.rem(gv - step + nv, nv)).wait_recv()
        for no in range(len(pieces)):
            piece_copy(no, step, gv).wait_send()
    for no, (mx, my) in enumerate(moves):

        @pl.when(inside(mx, my))
        def _():
            for kind in range(3):
                departure(kind, no).wait_send()
            for step in range(nv):
                half = lax.rem(gv - step + nv, nv)
                rim_arrival(step, half, no).wait_recv()
                rim_departure(step, half, no).wait_send()


def split(x):
    high = x.astype(BF16)
    return high, (x - high.astype(F32)).astype(BF16)


NT = (((1,), (1,)), ((), ()))
NN = (((1,), (0,)), ((), ()))


def dot(a, b, dims):
    return lax.dot_general(a, b, dims, preferred_element_type=F32)


def dot3(a, b, dims):
    return dot(a[0], b[0], dims) + dot(a[0], b[1], dims) + dot(a[1], b[0], dims)


def coarse_kernel(
    size_x, size_y, slots, f_ref, k_ref, c_ref, interp_ref, coarse_ref,
    hot, right_h, right_l, gram_s, lh, ll, rh, rl, ch, tiles, leave,
):
    nv, cols, vecs, depth = f_ref.shape
    wide_y = size_y + 2
    rows = GROUP * slots
    members = GROUP * nv * vecs
    count = gram_s.shape[0]
    padded = -(-wide_y // GROUP) * GROUP
    band = size_y * slots

    def lanes(shape):
        return lax.broadcasted_iota(jnp.int32, shape, len(shape) - 1)

    def subs(shape):
        return lax.broadcasted_iota(jnp.int32, shape, len(shape) - 2)

    same = subs((rows, members)) // slots == lanes((rows, members)) // (nv * vecs)
    same_slots = subs((rows, rows)) // slots == lanes((rows, rows)) // slots
    own_lane = subs((rows, slots)) % slots == lanes((rows, slots))
    ones = jnp.ones((slots, depth), BF16)

    def start_of(no):
        return jnp.minimum(no * GROUP, cols - GROUP)

    def gather(batch):
        fields, spreads = [], []
        for no in batch:
            start = min(no * GROUP, cols - GROUP)
            knots = k_ref[pl.ds(start, GROUP)]
            alive = knots > 0.0
            inverse = jnp.where(alive, 1.0 / jnp.where(alive, knots, 1.0), 0.0)
            field = jnp.concatenate(
                [f_ref[half, pl.ds(start, GROUP)] * inverse for half in range(nv)], axis=1
            ).reshape(members, depth)
            fields.append(split(field))
            spots = jnp.broadcast_to(
                c_ref[pl.ds(start, GROUP)].astype(F32), (GROUP, slots, slots)
            ).reshape(rows, slots)
            spreads.append(dot(jnp.where(own_lane, spots, 0.0).astype(BF16), ones, NN))
        pairs = []
        for no, spread, (high, low) in zip(batch, spreads, fields):
            onehot = jnp.where(spread == lanes((rows, depth)).astype(F32), 1.0, 0.0).astype(BF16)
            hot[no] = onehot
            pairs.append(dot(onehot, high, NT) + dot(onehot, low, NT))
        pairs = [split(jnp.where(same, cvals, 0.0)) for cvals in pairs]
        grams = [dot3(pair, pair, NT) for pair in pairs]
        rights = [dot3(pair, field, NN) for pair, field in zip(pairs, fields)]
        for no, gram, right in zip(batch, grams, rights):
            gram_s[no] = jnp.sum(gram.reshape(GROUP, slots, rows), axis=0)
            high, low = split(right)
            right_h[no] = high
            right_l[no] = low

    for first in range(0, count, BATCH):
        gather(range(first, min(first + BATCH, count)))

    shape = (count, slots, rows)
    lane = lanes(shape) % slots
    sub = subs(shape)
    system = gram_s[...]
    diagonal = jnp.sum(jnp.where(lane == sub, system, 0.0), axis=1)
    block = jnp.where(same_slots, 1.0, 0.0).astype(BF16)
    first = diagonal.astype(BF16)
    rest = diagonal - first.astype(F32)
    second = rest.astype(BF16)
    third = (rest - second.astype(F32)).astype(BF16)
    trace = dot(first, block, NN) + dot(second, block, NN) + dot(third, block, NN)
    ridge = RIDGE * trace / slots + 1e-06
    system = system + jnp.where(lane == sub, ridge[:, None, :], 0.0)
    flat = (count * slots, rows)
    base = lanes(flat) // slots * slots
    for pivot in range(slots):
        column = jnp.take_along_axis(
            system.reshape(flat), base + pivot, axis=1, mode="promise_in_bounds"
        ).reshape(shape)
        line = system[:, pivot : pivot + 1, :]
        here = lane[:, 0:1, :] == pivot
        line = jnp.where(here, 1.0, line) / column[:, pivot : pivot + 1, :]
        system = jnp.where(
            sub == pivot, line, jnp.where(lane == pivot, 0.0, system) - column * line
        )
    gram_s[...] = system

    def weigh(batch):
        inverses = [
            split(
                jnp.where(
                    same_slots,
                    jnp.broadcast_to(gram_s[no][None], (GROUP, slots, rows)).reshape(rows, rows),
                    0.0,
                )
            )
            for no in batch
        ]
        solved = [
            dot3(inverse, (right_h[no], right_l[no]), NN) for no, inverse in zip(batch, inverses)
        ]
        for no, weights in zip(batch, solved):
            here = pl.ds(min(no * GROUP, cols - GROUP), GROUP)
            onehot = hot[no].astype(F32).reshape(GROUP, slots, depth)
            crow = jnp.sum(onehot, axis=1, keepdims=True)
            value = weights.reshape(GROUP, slots, depth) * (1.0 - crow) + onehot
            ch[here] = value
            left = value * k_ref[here]
            high, low = split(left)
            lh[here] = high
            ll[here] = low
            high, low = split(smear_z(left.reshape(rows, depth)))
            rh[here] = high.reshape(GROUP, slots, depth)
            rl[here] = low.reshape(GROUP, slots, depth)

    for first in range(0, count, BATCH_2):
        weigh(range(first, min(first + BATCH_2, count)))

    half = GROUP * slots
    groups = slots * slots // half
    tall = (GROUP, half)
    pick_row = lanes(tall) // slots
    out_row = subs(tall)

    def merge(tiles):
        hop = GROUP // 2
        while hop >= 1:
            up = out_row // hop % 2 == 1
            straight = up == (pick_row // hop % 2 == 1)
            merged = []
            for no in range(hop):
                one, two = tiles[no], tiles[no + hop]
                same_place = jnp.where(up, two, one)
                moved = jnp.where(up, one, two)
                down = pltpu.roll(moved, hop, 0)
                if 2 * hop != GROUP:
                    down = jnp.where(up, down, pltpu.roll(moved, GROUP - hop, 0))
                merged.append(jnp.where(straight, same_place, down))
            tiles = merged
            hop //= 2
        return tiles[0]

    block_lane = lanes((slots, half)) % slots

    def galerkin(row):
        at = (row + 1) * wide_y
        mine = pl.ds(at + 1, size_y)
        own = ch[mine]
        away[row][0].start()
        across = k_ref[pl.ds(at, wide_y)] + ANISOTROPY[0] * (
            k_ref[pl.ds(at - wide_y, wide_y)] + k_ref[pl.ds(at + wide_y, wide_y)]
        )
        along = across[1 : size_y + 1] + ANISOTROPY[1] * (across[0:size_y] + across[2:])
        whole = smear_z(along.reshape(size_y, depth)).reshape(size_y, 1, depth)
        left = (lh[mine].reshape(band, depth), ll[mine].reshape(band, depth))
        right = rh[mine].astype(F32) + rl[mine].astype(F32)
        centre = right - own * (whole + SHIFT * k_ref[mine])
        middle = dot3(left, split(centre.reshape(band, depth)), NT)
        for move_x in (-1, 0, 1):
            there = pl.ds(at + move_x * wide_y, padded)
            other = (
                rh[there].reshape(padded * slots, depth),
                rl[there].reshape(padded * slots, depth),
            )
            product = dot3(left, other, NT)
            for move_y in (-1, 0, 1):
                weight = 1.0
                if move_x != 0:
                    weight = weight * ANISOTROPY[0]
                if move_y != 0:
                    weight = weight * ANISOTROPY[1]
                order = 3 * (move_x + 1) + move_y + 1
                for chunk in range(0, size_y, GROUP):
                    spread = []
                    for col in range(chunk, chunk + GROUP):
                        central = move_x == 0 and move_y == 0
                        origin = middle if central else product
                        place = col if central else col + 1 + move_y
                        first_lane = place // GROUP * half
                        values = origin[
                            col * slots : (col + 1) * slots, first_lane : first_lane + half
                        ]
                        spread.append(
                            jnp.take_along_axis(
                                values, block_lane + place % GROUP * slots, axis=1,
                                mode="promise_in_bounds",
                            )
                        )
                    parts = [
                        merge([tile[g * GROUP : (g + 1) * GROUP] for tile in spread])
                        for g in range(groups)
                    ]
                    tiles[row, order, chunk : chunk + GROUP, :] = -weight * jnp.concatenate(
                        parts, axis=1
                    )
        away[row][1].start()

    away = [
        (
            pltpu.make_async_copy(
                ch.at[pl.ds((row + 1) * wide_y + 1, size_y)], interp_ref.at[row], leave.at[0, row]
            ),
            pltpu.make_async_copy(tiles.at[row], coarse_ref.at[row], leave.at[1, row]),
        )
        for row in range(size_x)
    ]
    for row in range(size_x):
        galerkin(row)
    for pair in away:
        for copy in pair:
            copy.wait()


def stay(x):
    return pltpu.with_memory_space_constraint(x, pltpu.VMEM)


def body(nx, ny, nv, vectors, conductivity, c_points):
    vecs, size_x, size_y, depth = vectors.shape
    slots = c_points.shape[-1]
    wide_x, wide_y = size_x + 2 * HALO, size_y + 2 * HALO
    cols = (size_x + 2) * (size_y + 2)
    vmem = pl.BlockSpec(memory_space=pltpu.VMEM)
    hbm = pl.BlockSpec(memory_space=pl.ANY)
    dma = pltpu.SemaphoreType.DMA
    field, knots, spots = pl.pallas_call(
        functools.partial(smooth_kernel, nx, ny, nv),
        out_shape=(
            pltpu.VMEM((nv, size_x + 2, size_y + 2, vecs, depth), F32),
            pltpu.VMEM((size_x + 2, size_y + 2, 1, depth), F32),
            pltpu.VMEM((size_x + 2, size_y + 2, 1, slots), jnp.int32),
        ),
        in_specs=[hbm] * 3,
        out_specs=(vmem,) * 3,
        scratch_shapes=[
            pltpu.VMEM((wide_x, wide_y, vecs, depth), F32),
            pltpu.VMEM((wide_x, wide_y, vecs, depth), F32),
            pltpu.VMEM((wide_x, wide_y, vecs, depth), F32),
            pltpu.VMEM((wide_x, wide_y, 1, depth), F32),
            pltpu.VMEM((wide_x, wide_y, 1, slots), jnp.int32),
            dma((8,)), dma((8,)), dma((8,)), dma((8,)), dma((8,)), dma((8,)),
            dma((nv, 5)), dma((nv, 5)), dma((nv, 8)), dma((nv, 8)),
            pltpu.VMEM((size_x, size_y, vecs, depth), F32), dma((vecs,)), dma((2,)),
        ],
        compiler_params=pltpu.CompilerParams(collective_id=0, has_side_effects=True),
        name="smooth",
    )(vectors, conductivity[:, :, None, :], c_points[:, :, None, :])
    count = -(-cols // GROUP)
    rows = GROUP * slots
    more = cols + 2 * GROUP
    interp, coarse = pl.pallas_call(
        functools.partial(coarse_kernel, size_x, size_y, slots),
        out_shape=(
            jax.ShapeDtypeStruct((size_x, size_y, slots, depth), F32),
            jax.ShapeDtypeStruct((size_x, 9, size_y, slots * slots), F32),
        ),
        in_specs=[vmem] * 3,
        out_specs=(hbm, hbm),
        scratch_shapes=[
            pltpu.VMEM((count, rows, depth), BF16),
            pltpu.VMEM((count, rows, depth), BF16),
            pltpu.VMEM((count, rows, depth), BF16),
            pltpu.VMEM((count, slots, rows), F32),
            pltpu.VMEM((more, slots, depth), BF16),
            pltpu.VMEM((more, slots, depth), BF16),
            pltpu.VMEM((more, slots, depth), BF16),
            pltpu.VMEM((more, slots, depth), BF16),
            pltpu.VMEM((more, slots, depth), F32),
            pltpu.VMEM((size_x, 9, size_y, slots * slots), F32),
            dma((2, size_x)),
        ],
        name="coarse",
    )(
        stay(field.reshape(nv, cols, vecs, depth)),
        stay(knots.reshape(cols, 1, depth)),
        stay(spots.reshape(cols, 1, slots)),
    )
    return interp, jnp.transpose(coarse, (0, 2, 1, 3))


def solution(mesh):
    placed = (P("vert", "gx", "gy", None), P("gx", "gy", None), P("gx", "gy", None))
    return jax.shard_map(
        functools.partial(body, mesh.shape["gx"], mesh.shape["gy"], mesh.shape["vert"]),
        mesh=mesh,
        in_specs=placed,
        out_specs=(P("gx", "gy", None, None), P("gx", "gy", None, None)),
        check_vma=False,
    )
```

```python
import functools

import jax
import jax.numpy as jnp
from jax import lax
from jax.experimental import pallas as pl
from jax.experimental.pallas import tpu as pltpu
from jax.sharding import PartitionSpec as P

SWEEPS = 3
ANISOTROPY = (1.0, 0.6, 0.15)
OMEGA = 0.6
SHIFT = 0.5
RIDGE = 0.1
HALO = SWEEPS
GROUP = 8
BATCH = 13
BATCH_2 = 2
MESH = pl.DeviceIdType.MESH
F32 = jnp.float32
BF16 = jnp.bfloat16


def smear_z(x):
    axis = x.ndim - 1
    depth = x.shape[axis]
    lane = lax.broadcasted_iota(jnp.int32, x.shape, axis)
    below = jnp.where(lane == 0, 0.0, pltpu.roll(x, 1, axis))
    above = jnp.where(lane == depth - 1, 0.0, pltpu.roll(x, depth - 1, axis))
    return x + ANISOTROPY[2] * (below + above)


def smear_line(get, count, across, along):
    summed = [get(0, no) + across * (get(-1, no) + get(1, no)) for no in range(-1, count + 1)]
    return [
        smear_z(summed[no + 1] + along * (summed[no] + summed[no + 2])) for no in range(count)
    ]


def pick(low, first, second):
    return jnp.where(low, jnp.int32(first), jnp.int32(second))


def smooth_kernel(
    nx, ny, nv, raw_ref, k_ref, c_ref, out_ref, knots_ref, spots_ref,
    one, two, three, gain, wide_k, wide_c, hsend, hrecv, fsend, frecv, rsend, rrecv, turn, load,
):
    size_x, size_y, depth = k_ref.shape[0], k_ref.shape[1], k_ref.shape[3]
    vecs = raw_ref.shape[0]
    wide_x, wide_y = size_x + 2 * HALO, size_y + 2 * HALO
    gx, gy, gv = lax.axis_index("gx"), lax.axis_index("gy"), lax.axis_index("vert")
    near = 1 - 2 * lax.rem(gx, 2)
    far_x = -near
    far_y = pick(gy > 0, -1, 1)
    low_x, low_y = far_x < 0, far_y < 0
    sides_x, sides_y = (0, near, far_x), (0, -far_y, far_y)
    middle, close, far = 0, 1, 2
    moves = [(mx, my) for mx in range(3) for my in range(3) if (mx, my) != (0, 0)]
    if ny <= 2:
        missing = [move for move in moves if move[1] == close]
        moves = [move for move in moves if move[1] != close]
    else:
        missing = []

    inner = pl.ds(HALO, size_x), pl.ds(HALO, size_y)
    loads = [
        pltpu.make_async_copy(source, target.at[inner], load.at[no])
        for no, (source, target) in enumerate(((k_ref, wide_k), (c_ref, wide_c)))
    ]
    turns = [
        pltpu.make_async_copy(raw_ref.at[vec], one.at[inner[0], inner[1], vec], turn.at[vec])
        for vec in range(vecs)
    ]
    for copy in loads + turns:
        copy.start()

    def inside(move):
        at_x, at_y = gx + sides_x[move[0]], gy + sides_y[move[1]]
        ok_x = jnp.logical_and(at_x >= 0, at_x < nx)
        return jnp.logical_and(ok_x, jnp.logical_and(at_y >= 0, at_y < ny))

    def device(move, step=0):
        return (gx + sides_x[move[0]], gy + sides_y[move[1]], lax.rem(gv + step, nv))

    def number(move):
        return 3 * (sides_x[move[0]] + 1) + sides_y[move[1]] + 1

    def opposite(move):
        return 3 * (1 - sides_x[move[0]]) + 1 - sides_y[move[1]]

    barrier = pltpu.get_barrier_semaphore()
    total = jnp.int32(nv - 1)
    for move in moves:
        here = inside(move)

        @pl.when(here)
        def _():
            pl.semaphore_signal(barrier, inc=1, device_id=device(move), device_id_type=MESH)

        total = total + here.astype(jnp.int32)
    for step in range(1, nv):
        pl.semaphore_signal(
            barrier, inc=1, device_id=device((0, 0), step), device_id_type=MESH
        )

    def side(sides, which, size, width, out):
        if which == middle:
            return pl.ds(0 if out else width, size), pl.ds(width, size)
        base = 0 if out else width
        low = sides[which] < 0
        return (
            pl.ds(base + pick(low, 0, size - width), width),
            pl.ds(pick(low, size + width, 0), width),
        )

    def hole(sides, which, size, width):
        if which == middle:
            return pl.ds(width, size)
        return pl.ds(pick(sides[which] < 0, 0, size + width), width)

    fills = ((wide_k, F32), (wide_c, jnp.int32), (one, F32))

    def clear(move):
        at_x, at_y = hole(sides_x, move[0], size_x, HALO), hole(sides_y, move[1], size_y, HALO)
        for target, kind in fills:
            target[at_x, at_y] = jnp.zeros((at_x.size, at_y.size) + target.shape[2:], kind)
        at_x, at_y = hole(sides_x, move[0], size_x, 1), hole(sides_y, move[1], size_y, 1)
        out_ref[:, at_x, at_y] = jnp.zeros((nv, at_x.size, at_y.size, vecs, depth), F32)

    for move in missing:
        clear(move)
    for move in moves:

        @pl.when(jnp.logical_not(inside(move)))
        def _():
            clear(move)

    for copy in loads + turns:
        copy.wait()

    def scale(row, carry):
        for col in range(HALO, HALO + size_y):
            factor = jnp.broadcast_to(wide_k[row, col], (vecs, depth))
            one[row, col] = one[row, col] * factor
        return carry

    lax.fori_loop(HALO, HALO + size_x, scale, 0, unroll=2)
    pl.semaphore_wait(barrier, total)

    kinds = (wide_k, one, wide_c)

    def departure(kind, move):
        from_x, to_x = side(sides_x, move[0], size_x, HALO, False)
        from_y, to_y = side(sides_y, move[1], size_y, HALO, False)
        no = number(move)
        return pltpu.make_async_remote_copy(
            src_ref=kinds[kind].at[from_x, from_y], dst_ref=kinds[kind].at[to_x, to_y],
            send_sem=hsend.at[kind, no], recv_sem=hrecv.at[kind, no],
            device_id=device(move), device_id_type=MESH,
        )

    def arrival(kind, move):
        no = opposite(move)
        place = kinds[kind].at[
            hole(sides_x, move[0], size_x, HALO), hole(sides_y, move[1], size_y, HALO)
        ]
        return pltpu.make_async_remote_copy(
            src_ref=place, dst_ref=place, send_sem=hsend.at[kind, no], recv_sem=hrecv.at[kind, no],
            device_id=device(move), device_id_type=MESH,
        )

    def for_each(some, act):
        for move in some:
            if move in moves:

                @pl.when(inside(move))
                def _():
                    act(move)

    first = [(close, middle), (middle, close), (close, close)]
    second = [(far, middle), (far, close)]
    third = [(middle, far), (close, far), (far, far)]

    def leave(move):
        departure(0, move).start()
        departure(1, move).start()

    for_each(first[:1] + third[:1] + second[:1] + third[1:] + first[1:] + second[1:], leave)

    def start(low, sweep, wide, whole):
        if whole:
            return pick(low, HALO + sweep, sweep)
        return pick(low, sweep, wide - HALO - sweep)

    def region_rows(sweep, part):
        if part == 2:
            return sweep, wide_x - 2 * sweep
        if part == 1:
            return start(low_x, sweep, wide_x, False), HALO
        return start(low_x, sweep, wide_x, True), wide_x - HALO - 2 * sweep

    def region_cols(sweep, part):
        if part == 2:
            return start(low_y, sweep, wide_y, False), HALO
        return start(low_y, sweep, wide_y, True), wide_y - HALO - 2 * sweep

    def sweep_lines(sweep, part, act):
        row, rows = region_rows(sweep, part)
        col, cols = region_cols(sweep, part)
        if part == 2:

            def step(no, carry):
                act(lambda i, j: (row + j, col + no + i), rows, ANISOTROPY[1], ANISOTROPY[0])
                return carry

            lax.fori_loop(0, cols, step, 0, unroll=True)
        else:

            def step(no, carry):
                act(lambda i, j: (row + no + i, col + j), cols, ANISOTROPY[0], ANISOTROPY[1])
                return carry

            lax.fori_loop(0, rows, step, 0, unroll=True if part == 1 else 3)

    def gains(at, count, across, along):
        around = smear_line(lambda i, j: wide_k[at(i, j)], count, across, along)
        for no in range(count):
            mid = wide_k[at(0, no)]
            below = around[no] - (1.0 - SHIFT) * mid
            alive = mid > 0.0
            value = jnp.where(alive, OMEGA * mid / jnp.where(alive, below, 1.0), 0.0)
            gain[at(0, no)] = jnp.broadcast_to(value, (vecs, depth))

    def relax(source, target, at, count, across, along):
        around = smear_line(lambda i, j: source[at(i, j)], count, across, along)
        for no in range(count):
            factor = gain[at(0, no)]
            target(at(0, no), (1.0 - OMEGA - factor) * source[at(0, no)] + factor * around[no])

    def keep(ref):
        def store(at, value):
            ref[at] = value

        return store

    def final(at, value):
        out_ref[gv, at[0] - HALO + 1, at[1] - HALO + 1] = value

    def smooth(part):
        buffers = (one, two, three)
        for sweep in range(1, SWEEPS + 1):
            source = buffers[(sweep - 1) % 3]
            target = final if sweep == SWEEPS else keep(buffers[sweep % 3])
            sweep_lines(sweep, part, functools.partial(relax, source, target))

    def block_copy(step, part, half):
        row, rows = region_rows(SWEEPS, part)
        col, cols = region_cols(SWEEPS, part)
        place = out_ref.at[half, pl.ds(row - HALO + 1, rows), pl.ds(col - HALO + 1, cols)]
        return pltpu.make_async_remote_copy(
            src_ref=place, dst_ref=place,
            send_sem=fsend.at[step - 1, part], recv_sem=frecv.at[step - 1, part],
            device_id=device((0, 0), step), device_id_type=MESH,
        )

    def edge(sides, which, size):
        if which == middle:
            return pl.ds(1, size), pl.ds(1, size), pl.ds(1, size)
        low = sides[which] < 0
        return (
            pl.ds(pick(low, 1, size), 1), pl.ds(pick(low, size + 1, 0), 1),
            pl.ds(pick(low, 0, size + 1), 1),
        )

    def rim_span(piece):
        mx, my, part = piece
        over_x, over_y = edge(sides_x, mx, size_x), edge(sides_y, my, size_y)
        if my == middle:
            col, cols = region_cols(SWEEPS, part)
            over_y = (pl.ds(col - HALO + 1, cols),) * 3
        return over_x, over_y

    def rim_departure(step, piece):
        (from_x, to_x, _), (from_y, to_y, _) = rim_span(piece)
        no = number(piece)
        return pltpu.make_async_remote_copy(
            src_ref=out_ref.at[gv, from_x, from_y], dst_ref=out_ref.at[gv, to_x, to_y],
            send_sem=rsend.at[step, no, piece[2] // 2], recv_sem=rrecv.at[step, no, piece[2] // 2],
            device_id=device(piece, step), device_id_type=MESH,
        )

    def rim_arrival(step, piece):
        (_, _, at_x), (_, _, at_y) = rim_span(piece)
        no = opposite(piece)
        half = lax.rem(gv - step + nv, nv)
        place = out_ref.at[half, at_x, at_y]
        return pltpu.make_async_remote_copy(
            src_ref=place, dst_ref=place,
            send_sem=rsend.at[step, no, piece[2] // 2], recv_sem=rrecv.at[step, no, piece[2] // 2],
            device_id=device(piece, -step + nv), device_id_type=MESH,
        )

    rims = (
        [(close, middle, 0)],
        [(far, middle, 0)],
        [
            (far, far, 2), (close, far, 2), (middle, far, 2), (far, middle, 2), (close, middle, 2),
            (middle, close, 2), (close, close, 2), (far, close, 2),
        ],
    )

    def for_rims(pieces, act):
        for piece in pieces:
            if piece[:2] in moves:

                @pl.when(inside(piece))
                def _():
                    act(piece)

    for part, group in enumerate((first, second, third)):
        for_each(group, lambda move: arrival(0, move).wait_recv())
        sweep_lines(1, part, gains)
        for_each(group, lambda move: arrival(1, move).wait_recv())
        smooth(part)
        for step in range(1, nv):
            if part == 2:
                for_rims(rims[part], lambda piece: rim_departure(step, piece).start())
            block_copy(step, part, gv).start()
            if part < 2:
                for_rims(rims[part], lambda piece: rim_departure(step, piece).start())
        for_rims(rims[part], lambda piece: rim_departure(0, piece).start())
        if part == 0:
            for_each(moves, lambda move: departure(2, move).start())

    for_each(moves, lambda move: arrival(2, move).wait_recv())
    rim_x, rim_y = pl.ds(HALO - 1, size_x + 2), pl.ds(HALO - 1, size_y + 2)
    knots_ref[...] = wide_k[rim_x, rim_y]
    spots_ref[...] = wide_c[rim_x, rim_y]

    for step in range(1, nv):
        for part in range(3):
            block_copy(step, part, lax.rem(gv - step + nv, nv)).wait_recv()
    for step in range(nv):
        for part in range(3):
            for_rims(rims[part], lambda piece: rim_arrival(step, piece).wait_recv())
    for step in range(1, nv):
        for part in range(3):
            block_copy(step, part, gv).wait_send()
    for step in range(nv):
        for part in range(3):
            for_rims(rims[part], lambda piece: rim_departure(step, piece).wait_send())
    for kind in range(3):
        for_each(moves, lambda move: departure(kind, move).wait_send())


def split(x):
    high = x.astype(BF16)
    return high, (x - high.astype(F32)).astype(BF16)


NT = (((1,), (1,)), ((), ()))
NN = (((1,), (0,)), ((), ()))


def dot(a, b, dims):
    return lax.dot_general(a, b, dims, preferred_element_type=F32)


def dot3(a, b, dims):
    return dot(a[0], b[0], dims) + dot(a[0], b[1], dims) + dot(a[1], b[0], dims)


def coarse_kernel(
    size_x, size_y, slots, f_ref, k_ref, c_ref, interp_ref, coarse_ref,
    hot, right_h, right_l, gram_s, lh, ll, rh, rl, ch, tiles, leave,
):
    nv, cols, vecs, depth = f_ref.shape
    wide_y = size_y + 2
    rows = GROUP * slots
    members = GROUP * nv * vecs
    count = gram_s.shape[0]
    padded = -(-wide_y // GROUP) * GROUP
    band = size_y * slots

    def lanes(shape):
        return lax.broadcasted_iota(jnp.int32, shape, len(shape) - 1)

    def subs(shape):
        return lax.broadcasted_iota(jnp.int32, shape, len(shape) - 2)

    same = subs((rows, members)) // slots == lanes((rows, members)) // (nv * vecs)
    same_slots = subs((rows, rows)) // slots == lanes((rows, rows)) // slots
    own_lane = subs((rows, slots)) % slots == lanes((rows, slots))
    ones = jnp.ones((slots, depth), BF16)

    def start_of(no):
        return jnp.minimum(no * GROUP, cols - GROUP)

    def gather(batch):
        fields, spreads = [], []
        for no in batch:
            start = min(no * GROUP, cols - GROUP)
            knots = k_ref[pl.ds(start, GROUP)]
            alive = knots > 0.0
            inverse = jnp.where(alive, 1.0 / jnp.where(alive, knots, 1.0), 0.0)
            field = jnp.concatenate(
                [f_ref[half, pl.ds(start, GROUP)] * inverse for half in range(nv)], axis=1
            ).reshape(members, depth)
            fields.append(split(field))
            spots = jnp.broadcast_to(
                c_ref[pl.ds(start, GROUP)].astype(F32), (GROUP, slots, slots)
            ).reshape(rows, slots)
            spreads.append(dot(jnp.where(own_lane, spots, 0.0).astype(BF16), ones, NN))
        pairs = []
        for no, spread, (high, low) in zip(batch, spreads, fields):
            onehot = jnp.where(spread == lanes((rows, depth)).astype(F32), 1.0, 0.0).astype(BF16)
            hot[no] = onehot
            pairs.append(dot(onehot, high, NT) + dot(onehot, low, NT))
        pairs = [split(jnp.where(same, cvals, 0.0)) for cvals in pairs]
        grams = [dot3(pair, pair, NT) for pair in pairs]
        rights = [dot3(pair, field, NN) for pair, field in zip(pairs, fields)]
        for no, gram, right in zip(batch, grams, rights):
            gram_s[no] = jnp.sum(gram.reshape(GROUP, slots, rows), axis=0)
            high, low = split(right)
            right_h[no] = high
            right_l[no] = low

    for first in range(0, count, BATCH):
        gather(range(first, min(first + BATCH, count)))

    shape = (count, slots, rows)
    lane = lanes(shape) % slots
    sub = subs(shape)
    system = gram_s[...]
    diagonal = jnp.sum(jnp.where(lane == sub, system, 0.0), axis=1)
    block = jnp.where(same_slots, 1.0, 0.0).astype(BF16)
    first = diagonal.astype(BF16)
    rest = diagonal - first.astype(F32)
    second = rest.astype(BF16)
    third = (rest - second.astype(F32)).astype(BF16)
    trace = dot(first, block, NN) + dot(second, block, NN) + dot(third, block, NN)
    ridge = RIDGE * trace / slots + 1e-06
    system = system + jnp.where(lane == sub, ridge[:, None, :], 0.0)
    flat = (count * slots, rows)
    base = lanes(flat) // slots * slots
    for pivot in range(slots):
        column = jnp.take_along_axis(
            system.reshape(flat), base + pivot, axis=1, mode="promise_in_bounds"
        ).reshape(shape)
        line = system[:, pivot : pivot + 1, :]
        here = lane[:, 0:1, :] == pivot
        line = jnp.where(here, 1.0, line) / column[:, pivot : pivot + 1, :]
        system = jnp.where(
            sub == pivot, line, jnp.where(lane == pivot, 0.0, system) - column * line
        )
    gram_s[...] = system

    def weigh(batch):
        inverses = [
            split(
                jnp.where(
                    same_slots,
                    jnp.broadcast_to(gram_s[no][None], (GROUP, slots, rows)).reshape(rows, rows),
                    0.0,
                )
            )
            for no in batch
        ]
        solved = [
            dot3(inverse, (right_h[no], right_l[no]), NN) for no, inverse in zip(batch, inverses)
        ]
        for no, weights in zip(batch, solved):
            here = pl.ds(min(no * GROUP, cols - GROUP), GROUP)
            onehot = hot[no].astype(F32).reshape(GROUP, slots, depth)
            crow = jnp.sum(onehot, axis=1, keepdims=True)
            value = weights.reshape(GROUP, slots, depth) * (1.0 - crow) + onehot
            ch[here] = value
            left = value * k_ref[here]
            high, low = split(left)
            lh[here] = high
            ll[here] = low
            high, low = split(smear_z(left.reshape(rows, depth)))
            rh[here] = high.reshape(GROUP, slots, depth)
            rl[here] = low.reshape(GROUP, slots, depth)

    for first in range(0, count, BATCH_2):
        weigh(range(first, min(first + BATCH_2, count)))

    half = GROUP * slots
    groups = slots * slots // half
    tall = (GROUP, half)
    pick_row = lanes(tall) // slots
    out_row = subs(tall)

    def merge(tiles):
        hop = GROUP // 2
        while hop >= 1:
            up = out_row // hop % 2 == 1
            straight = up == (pick_row // hop % 2 == 1)
            merged = []
            for no in range(hop):
                one, two = tiles[no], tiles[no + hop]
                same_place = jnp.where(up, two, one)
                moved = jnp.where(up, one, two)
                down = pltpu.roll(moved, hop, 0)
                if 2 * hop != GROUP:
                    down = jnp.where(up, down, pltpu.roll(moved, GROUP - hop, 0))
                merged.append(jnp.where(straight, same_place, down))
            tiles = merged
            hop //= 2
        return tiles[0]

    block_lane = lanes((slots, half)) % slots

    def galerkin(row):
        at = (row + 1) * wide_y
        mine = pl.ds(at + 1, size_y)
        own = ch[mine]
        away[row][0].start()
        across = k_ref[pl.ds(at, wide_y)] + ANISOTROPY[0] * (
            k_ref[pl.ds(at - wide_y, wide_y)] + k_ref[pl.ds(at + wide_y, wide_y)]
        )
        along = across[1 : size_y + 1] + ANISOTROPY[1] * (across[0:size_y] + across[2:])
        whole = smear_z(along.reshape(size_y, depth)).reshape(size_y, 1, depth)
        left = (lh[mine].reshape(band, depth), ll[mine].reshape(band, depth))
        right = rh[mine].astype(F32) + rl[mine].astype(F32)
        centre = right - own * (whole + SHIFT * k_ref[mine])
        middle = dot3(left, split(centre.reshape(band, depth)), NT)
        for move_x in (-1, 0, 1):
            there = pl.ds(at + move_x * wide_y, padded)
            other = (
                rh[there].reshape(padded * slots, depth),
                rl[there].reshape(padded * slots, depth),
            )
            product = dot3(left, other, NT)
            for move_y in (-1, 0, 1):
                weight = 1.0
                if move_x != 0:
                    weight = weight * ANISOTROPY[0]
                if move_y != 0:
                    weight = weight * ANISOTROPY[1]
                order = 3 * (move_x + 1) + move_y + 1
                for chunk in range(0, size_y, GROUP):
                    spread = []
                    for col in range(chunk, chunk + GROUP):
                        central = move_x == 0 and move_y == 0
                        origin = middle if central else product
                        place = col if central else col + 1 + move_y
                        first_lane = place // GROUP * half
                        values = origin[
                            col * slots : (col + 1) * slots, first_lane : first_lane + half
                        ]
                        spread.append(
                            jnp.take_along_axis(
                                values, block_lane + place % GROUP * slots, axis=1,
                                mode="promise_in_bounds",
                            )
                        )
                    parts = [
                        merge([tile[g * GROUP : (g + 1) * GROUP] for tile in spread])
                        for g in range(groups)
                    ]
                    tiles[row, order, chunk : chunk + GROUP, :] = -weight * jnp.concatenate(
                        parts, axis=1
                    )
        away[row][1].start()

    away = [
        (
            pltpu.make_async_copy(
                ch.at[pl.ds((row + 1) * wide_y + 1, size_y)], interp_ref.at[row], leave.at[0, row]
            ),
            pltpu.make_async_copy(tiles.at[row], coarse_ref.at[row], leave.at[1, row]),
        )
        for row in range(size_x)
    ]
    for row in range(size_x):
        galerkin(row)
    for pair in away:
        for copy in pair:
            copy.wait()


def stay(x):
    return pltpu.with_memory_space_constraint(x, pltpu.VMEM)


def body(nx, ny, nv, vectors, conductivity, c_points):
    vecs, size_x, size_y, depth = vectors.shape
    slots = c_points.shape[-1]
    wide_x, wide_y = size_x + 2 * HALO, size_y + 2 * HALO
    cols = (size_x + 2) * (size_y + 2)
    vmem = pl.BlockSpec(memory_space=pltpu.VMEM)
    hbm = pl.BlockSpec(memory_space=pl.ANY)
    dma = pltpu.SemaphoreType.DMA
    field, knots, spots = pl.pallas_call(
        functools.partial(smooth_kernel, nx, ny, nv),
        out_shape=(
            pltpu.VMEM((nv, size_x + 2, size_y + 2, vecs, depth), F32),
            pltpu.VMEM((size_x + 2, size_y + 2, 1, depth), F32),
            pltpu.VMEM((size_x + 2, size_y + 2, 1, slots), jnp.int32),
        ),
        in_specs=[hbm] * 3,
        out_specs=(vmem,) * 3,
        scratch_shapes=[
            pltpu.VMEM((wide_x, wide_y, vecs, depth), F32),
            pltpu.VMEM((wide_x, wide_y, vecs, depth), F32),
            pltpu.VMEM((wide_x, wide_y, vecs, depth), F32),
            pltpu.VMEM((wide_x, wide_y, vecs, depth), F32),
            pltpu.VMEM((wide_x, wide_y, 1, depth), F32),
            pltpu.VMEM((wide_x, wide_y, 1, slots), jnp.int32),
            dma((3, 9)), dma((3, 9)), dma((nv, 3)), dma((nv, 3)), dma((nv, 9, 2)), dma((nv, 9, 2)),
            dma((vecs,)), dma((2,)),
        ],
        compiler_params=pltpu.CompilerParams(collective_id=0, has_side_effects=True),
        name="smooth",
    )(vectors, conductivity[:, :, None, :], c_points[:, :, None, :])
    count = -(-cols // GROUP)
    rows = GROUP * slots
    more = cols + 2 * GROUP
    interp, coarse = pl.pallas_call(
        functools.partial(coarse_kernel, size_x, size_y, slots),
        out_shape=(
            jax.ShapeDtypeStruct((size_x, size_y, slots, depth), F32),
            jax.ShapeDtypeStruct((size_x, 9, size_y, slots * slots), F32),
        ),
        in_specs=[vmem] * 3,
        out_specs=(hbm, hbm),
        scratch_shapes=[
            pltpu.VMEM((count, rows, depth), BF16),
            pltpu.VMEM((count, rows, depth), BF16),
            pltpu.VMEM((count, rows, depth), BF16),
            pltpu.VMEM((count, slots, rows), F32),
            pltpu.VMEM((more, slots, depth), BF16),
            pltpu.VMEM((more, slots, depth), BF16),
            pltpu.VMEM((more, slots, depth), BF16),
            pltpu.VMEM((more, slots, depth), BF16),
            pltpu.VMEM((more, slots, depth), F32),
            pltpu.VMEM((size_x, 9, size_y, slots * slots), F32),
            dma((2, size_x)),
        ],
        name="coarse",
    )(
        stay(field.reshape(nv, cols, vecs, depth)),
        stay(knots.reshape(cols, 1, depth)),
        stay(spots.reshape(cols, 1, slots)),
    )
    return interp, jnp.transpose(coarse, (0, 2, 1, 3))


def solution(mesh):
    placed = (P("vert", "gx", "gy", None), P("gx", "gy", None), P("gx", "gy", None))
    return jax.shard_map(
        functools.partial(body, mesh.shape["gx"], mesh.shape["gy"], mesh.shape["vert"]),
        mesh=mesh,
        in_specs=placed,
        out_specs=(P("gx", "gy", None, None), P("gx", "gy", None, None)),
        check_vma=False,
    )
```

```python
import functools

import jax
import jax.numpy as jnp
from jax import lax
from jax.experimental import pallas as pl
from jax.experimental.pallas import tpu as pltpu
from jax.sharding import PartitionSpec as P

SWEEPS = 3
ANISOTROPY = (1.0, 0.6, 0.15)
OMEGA = 0.6
SHIFT = 0.5
RIDGE = 0.1
HALO = SWEEPS
GROUP = 8
BATCH = 13
BATCH_2 = 2
MESH = pl.DeviceIdType.MESH
F32 = jnp.float32
BF16 = jnp.bfloat16


def smear_z(x):
    axis = x.ndim - 1
    depth = x.shape[axis]
    lane = lax.broadcasted_iota(jnp.int32, x.shape, axis)
    below = jnp.where(lane == 0, 0.0, pltpu.roll(x, 1, axis))
    above = jnp.where(lane == depth - 1, 0.0, pltpu.roll(x, depth - 1, axis))
    return x + ANISOTROPY[2] * (below + above)


def smear_line(get, count, across, along):
    summed = [get(0, no) + across * (get(-1, no) + get(1, no)) for no in range(-1, count + 1)]
    return [
        smear_z(summed[no + 1] + along * (summed[no] + summed[no + 2])) for no in range(count)
    ]


def pick(low, first, second):
    return jnp.where(low, jnp.int32(first), jnp.int32(second))


def smooth_kernel(
    nx, ny, nv, raw_ref, k_ref, c_ref, out_ref, knots_ref, spots_ref,
    one, two, three, gain, wide_k, wide_c, hsend, hrecv, fsend, frecv, rsend, rrecv, turn, load,
):
    size_x, size_y, depth = k_ref.shape[0], k_ref.shape[1], k_ref.shape[3]
    vecs = raw_ref.shape[0]
    wide_x, wide_y = size_x + 2 * HALO, size_y + 2 * HALO
    gx, gy, gv = lax.axis_index("gx"), lax.axis_index("gy"), lax.axis_index("vert")
    near = 1 - 2 * lax.rem(gx, 2)
    far_x = -near
    far_y = pick(gy > 0, -1, 1)
    low_x, low_y = far_x < 0, far_y < 0
    sides_x, sides_y = (0, near, far_x), (0, -far_y, far_y)
    middle, close, far = 0, 1, 2
    moves = [(mx, my) for mx in range(3) for my in range(3) if (mx, my) != (0, 0)]
    if ny <= 2:
        missing = [move for move in moves if move[1] == close]
        moves = [move for move in moves if move[1] != close]
    else:
        missing = []

    inner = pl.ds(HALO, size_x), pl.ds(HALO, size_y)
    loads = [
        pltpu.make_async_copy(source, target.at[inner], load.at[no])
        for no, (source, target) in enumerate(((k_ref, wide_k), (c_ref, wide_c)))
    ]
    turns = [
        pltpu.make_async_copy(raw_ref.at[vec], one.at[inner[0], inner[1], vec], turn.at[vec])
        for vec in range(vecs)
    ]
    for copy in loads + turns:
        copy.start()

    def inside(move):
        at_x, at_y = gx + sides_x[move[0]], gy + sides_y[move[1]]
        ok_x = jnp.logical_and(at_x >= 0, at_x < nx)
        return jnp.logical_and(ok_x, jnp.logical_and(at_y >= 0, at_y < ny))

    def device(move, step=0):
        return (gx + sides_x[move[0]], gy + sides_y[move[1]], lax.rem(gv + step, nv))

    def number(move):
        return 3 * (sides_x[move[0]] + 1) + sides_y[move[1]] + 1

    def opposite(move):
        return 3 * (1 - sides_x[move[0]]) + 1 - sides_y[move[1]]

    barrier = pltpu.get_barrier_semaphore()
    total = jnp.int32(nv - 1)
    for move in moves:
        here = inside(move)

        @pl.when(here)
        def _():
            pl.semaphore_signal(barrier, inc=1, device_id=device(move), device_id_type=MESH)

        total = total + here.astype(jnp.int32)
    for step in range(1, nv):
        pl.semaphore_signal(
            barrier, inc=1, device_id=device((0, 0), step), device_id_type=MESH
        )

    def side(sides, which, size, width, out):
        if which == middle:
            return pl.ds(0 if out else width, size), pl.ds(width, size)
        base = 0 if out else width
        low = sides[which] < 0
        return (
            pl.ds(base + pick(low, 0, size - width), width),
            pl.ds(pick(low, size + width, 0), width),
        )

    def hole(sides, which, size, width):
        if which == middle:
            return pl.ds(width, size)
        return pl.ds(pick(sides[which] < 0, 0, size + width), width)

    fills = ((wide_k, F32), (wide_c, jnp.int32), (one, F32))

    def clear(move):
        at_x, at_y = hole(sides_x, move[0], size_x, HALO), hole(sides_y, move[1], size_y, HALO)
        for target, kind in fills:
            target[at_x, at_y] = jnp.zeros((at_x.size, at_y.size) + target.shape[2:], kind)
        at_x, at_y = hole(sides_x, move[0], size_x, 1), hole(sides_y, move[1], size_y, 1)
        out_ref[:, at_x, at_y] = jnp.zeros((nv, at_x.size, at_y.size, vecs, depth), F32)

    for move in missing:
        clear(move)
    for move in moves:

        @pl.when(jnp.logical_not(inside(move)))
        def _():
            clear(move)

    for copy in loads + turns:
        copy.wait()

    def scale(row, carry):
        for col in range(HALO, HALO + size_y):
            factor = jnp.broadcast_to(wide_k[row, col], (vecs, depth))
            one[row, col] = one[row, col] * factor
        return carry

    lax.fori_loop(HALO, HALO + size_x, scale, 0, unroll=2)
    pl.semaphore_wait(barrier, total)

    kinds = (wide_k, one, wide_c)

    def departure(kind, move):
        from_x, to_x = side(sides_x, move[0], size_x, HALO, False)
        from_y, to_y = side(sides_y, move[1], size_y, HALO, False)
        no = number(move)
        return pltpu.make_async_remote_copy(
            src_ref=kinds[kind].at[from_x, from_y], dst_ref=kinds[kind].at[to_x, to_y],
            send_sem=hsend.at[kind, no], recv_sem=hrecv.at[kind, no],
            device_id=device(move), device_id_type=MESH,
        )

    def arrival(kind, move):
        no = opposite(move)
        place = kinds[kind].at[
            hole(sides_x, move[0], size_x, HALO), hole(sides_y, move[1], size_y, HALO)
        ]
        return pltpu.make_async_remote_copy(
            src_ref=place, dst_ref=place, send_sem=hsend.at[kind, no], recv_sem=hrecv.at[kind, no],
            device_id=device(move), device_id_type=MESH,
        )

    def for_each(some, act):
        for move in some:
            if move in moves:

                @pl.when(inside(move))
                def _():
                    act(move)

    first = [(close, middle), (middle, close), (close, close)]
    second = [(far, middle), (far, close)]
    third = [(middle, far), (close, far), (far, far)]

    def leave(move):
        departure(0, move).start()
        departure(1, move).start()

    for_each(first[:1] + third[:1] + second[:1] + third[1:] + first[1:] + second[1:], leave)

    def start(low, sweep, wide, whole):
        if whole:
            return pick(low, HALO + sweep, sweep)
        return pick(low, sweep, wide - HALO - sweep)

    def region_rows(sweep, part):
        if part == 2:
            return sweep, wide_x - 2 * sweep
        if part == 1:
            return start(low_x, sweep, wide_x, False), HALO
        return start(low_x, sweep, wide_x, True), wide_x - HALO - 2 * sweep

    def region_cols(sweep, part):
        if part == 2:
            return start(low_y, sweep, wide_y, False), HALO
        return start(low_y, sweep, wide_y, True), wide_y - HALO - 2 * sweep

    def sweep_lines(sweep, part, act):
        row, rows = region_rows(sweep, part)
        col, cols = region_cols(sweep, part)
        if part == 2:

            def step(no, carry):
                act(lambda i, j: (row + j, col + no + i), rows, ANISOTROPY[1], ANISOTROPY[0])
                return carry

            lax.fori_loop(0, cols, step, 0, unroll=True)
        else:

            def step(no, carry):
                act(lambda i, j: (row + no + i, col + j), cols, ANISOTROPY[0], ANISOTROPY[1])
                return carry

            lax.fori_loop(0, rows, step, 0, unroll=True if part == 1 else 3)

    def gains(at, count, across, along):
        around = smear_line(lambda i, j: wide_k[at(i, j)], count, across, along)
        for no in range(count):
            mid = wide_k[at(0, no)]
            below = around[no] - (1.0 - SHIFT) * mid
            alive = mid > 0.0
            value = jnp.where(alive, OMEGA * mid / jnp.where(alive, below, 1.0), 0.0)
            gain[at(0, no)] = jnp.broadcast_to(value, (vecs, depth))

    def relax(source, target, at, count, across, along):
        around = smear_line(lambda i, j: source[at(i, j)], count, across, along)
        for no in range(count):
            factor = gain[at(0, no)]
            target(at(0, no), (1.0 - OMEGA - factor) * source[at(0, no)] + factor * around[no])

    def keep(ref):
        def store(at, value):
            ref[at] = value

        return store

    def final(at, value):
        out_ref[gv, at[0] - HALO + 1, at[1] - HALO + 1] = value

    def smooth(part):
        buffers = (one, two, three)
        for sweep in range(1, SWEEPS + 1):
            source = buffers[(sweep - 1) % 3]
            target = final if sweep == SWEEPS else keep(buffers[sweep % 3])
            sweep_lines(sweep, part, functools.partial(relax, source, target))

    def block_copy(step, part, half):
        row, rows = region_rows(SWEEPS, part)
        col, cols = region_cols(SWEEPS, part)
        place = out_ref.at[half, pl.ds(row - HALO + 1, rows), pl.ds(col - HALO + 1, cols)]
        return pltpu.make_async_remote_copy(
            src_ref=place, dst_ref=place,
            send_sem=fsend.at[step - 1, part], recv_sem=frecv.at[step - 1, part],
            device_id=device((0, 0), step), device_id_type=MESH,
        )

    def edge(sides, which, size):
        if which == middle:
            return pl.ds(1, size), pl.ds(1, size), pl.ds(1, size)
        low = sides[which] < 0
        return (
            pl.ds(pick(low, 1, size), 1), pl.ds(pick(low, size + 1, 0), 1),
            pl.ds(pick(low, 0, size + 1), 1),
        )

    def rim_span(piece):
        mx, my, part = piece
        over_x, over_y = edge(sides_x, mx, size_x), edge(sides_y, my, size_y)
        if my == middle:
            col, cols = region_cols(SWEEPS, part)
            over_y = (pl.ds(col - HALO + 1, cols),) * 3
        return over_x, over_y

    def rim_departure(step, piece):
        (from_x, to_x, _), (from_y, to_y, _) = rim_span(piece)
        no = number(piece)
        return pltpu.make_async_remote_copy(
            src_ref=out_ref.at[gv, from_x, from_y], dst_ref=out_ref.at[gv, to_x, to_y],
            send_sem=rsend.at[step, no, piece[2] // 2], recv_sem=rrecv.at[step, no, piece[2] // 2],
            device_id=device(piece, step), device_id_type=MESH,
        )

    def rim_arrival(step, piece):
        (_, _, at_x), (_, _, at_y) = rim_span(piece)
        no = opposite(piece)
        half = lax.rem(gv - step + nv, nv)
        place = out_ref.at[half, at_x, at_y]
        return pltpu.make_async_remote_copy(
            src_ref=place, dst_ref=place,
            send_sem=rsend.at[step, no, piece[2] // 2], recv_sem=rrecv.at[step, no, piece[2] // 2],
            device_id=device(piece, -step + nv), device_id_type=MESH,
        )

    rims = (
        [(close, middle, 0)],
        [(far, middle, 0)],
        [
            (far, far, 2), (close, far, 2), (middle, far, 2), (far, middle, 2), (close, middle, 2),
            (middle, close, 2), (close, close, 2), (far, close, 2),
        ],
    )

    def for_rims(pieces, act):
        for piece in pieces:
            if piece[:2] in moves:

                @pl.when(inside(piece))
                def _():
                    act(piece)

    for part, group in enumerate((first, second, third)):
        for_each(group, lambda move: arrival(0, move).wait_recv())
        sweep_lines(1, part, gains)
        for_each(group, lambda move: arrival(1, move).wait_recv())
        smooth(part)
        for step in range(1, nv):
            if part == 2:
                for_rims(rims[part], lambda piece: rim_departure(step, piece).start())
            block_copy(step, part, gv).start()
            if part < 2:
                for_rims(rims[part], lambda piece: rim_departure(step, piece).start())
        for_rims(rims[part], lambda piece: rim_departure(0, piece).start())
        if part == 0:
            for_each(moves, lambda move: departure(2, move).start())

    for_each(moves, lambda move: arrival(2, move).wait_recv())
    rim_x, rim_y = pl.ds(HALO - 1, size_x + 2), pl.ds(HALO - 1, size_y + 2)
    knots_ref[...] = wide_k[rim_x, rim_y]
    spots_ref[...] = wide_c[rim_x, rim_y]

    for step in range(1, nv):
        for part in range(3):
            block_copy(step, part, lax.rem(gv - step + nv, nv)).wait_recv()
    for step in range(nv):
        for part in range(3):
            for_rims(rims[part], lambda piece: rim_arrival(step, piece).wait_recv())
    for step in range(1, nv):
        for part in range(3):
            block_copy(step, part, gv).wait_send()
    for step in range(nv):
        for part in range(3):
            for_rims(rims[part], lambda piece: rim_departure(step, piece).wait_send())
    for kind in range(3):
        for_each(moves, lambda move: departure(kind, move).wait_send())


def split(x):
    high = x.astype(BF16)
    return high, (x - high.astype(F32)).astype(BF16)


NT = (((1,), (1,)), ((), ()))
NN = (((1,), (0,)), ((), ()))


def dot(a, b, dims):
    return lax.dot_general(a, b, dims, preferred_element_type=F32)


def dot3(a, b, dims):
    along = dims[0][1][0]
    both = dot(jnp.concatenate([a[0], a[0]], axis=1), jnp.concatenate(b, axis=along), dims)
    return both + dot(a[1], b[0], dims)


def coarse_kernel(
    size_x, size_y, slots, f_ref, k_ref, c_ref, interp_ref, coarse_ref,
    hot, right_h, right_l, gram_s, lh, ll, rh, rl, ch, tiles, leave,
):
    nv, cols, vecs, depth = f_ref.shape
    wide_y = size_y + 2
    rows = GROUP * slots
    members = GROUP * nv * vecs
    count = gram_s.shape[0]
    padded = -(-wide_y // GROUP) * GROUP
    band = size_y * slots

    def lanes(shape):
        return lax.broadcasted_iota(jnp.int32, shape, len(shape) - 1)

    def subs(shape):
        return lax.broadcasted_iota(jnp.int32, shape, len(shape) - 2)

    same = subs((rows, members)) // slots == lanes((rows, members)) // (nv * vecs)
    same_slots = subs((rows, rows)) // slots == lanes((rows, rows)) // slots
    own_lane = subs((rows, slots)) % slots == lanes((rows, slots))
    ones = jnp.ones((slots, depth), BF16)

    def start_of(no):
        return jnp.minimum(no * GROUP, cols - GROUP)

    def gather(batch):
        fields, spreads = [], []
        for no in batch:
            start = min(no * GROUP, cols - GROUP)
            knots = k_ref[pl.ds(start, GROUP)]
            alive = knots > 0.0
            inverse = jnp.where(alive, 1.0 / jnp.where(alive, knots, 1.0), 0.0)
            field = jnp.concatenate(
                [f_ref[half, pl.ds(start, GROUP)] * inverse for half in range(nv)], axis=1
            ).reshape(members, depth)
            fields.append(split(field))
            spots = jnp.broadcast_to(
                c_ref[pl.ds(start, GROUP)].astype(F32), (GROUP, slots, slots)
            ).reshape(rows, slots)
            spreads.append(dot(jnp.where(own_lane, spots, 0.0).astype(BF16), ones, NN))
        pairs = []
        for no, spread, (high, low) in zip(batch, spreads, fields):
            onehot = jnp.where(spread == lanes((rows, depth)).astype(F32), 1.0, 0.0).astype(BF16)
            hot[no] = onehot
            twice = jnp.concatenate([onehot, onehot], axis=1)
            pairs.append(dot(twice, jnp.concatenate([high, low], axis=1), NT))
        pairs = [split(jnp.where(same, cvals, 0.0)) for cvals in pairs]
        grams = [dot3(pair, pair, NT) for pair in pairs]
        rights = [dot3(pair, field, NN) for pair, field in zip(pairs, fields)]
        for no, gram, right in zip(batch, grams, rights):
            gram_s[no] = jnp.sum(gram.reshape(GROUP, slots, rows), axis=0)
            high, low = split(right)
            right_h[no] = high
            right_l[no] = low

    for first in range(0, count, BATCH):
        gather(range(first, min(first + BATCH, count)))

    shape = (count, slots, rows)
    lane = lanes(shape) % slots
    sub = subs(shape)
    system = gram_s[...]
    diagonal = jnp.sum(jnp.where(lane == sub, system, 0.0), axis=1)
    block = jnp.where(same_slots, 1.0, 0.0).astype(BF16)
    first = diagonal.astype(BF16)
    rest = diagonal - first.astype(F32)
    second = rest.astype(BF16)
    third = (rest - second.astype(F32)).astype(BF16)
    trace = dot(first, block, NN) + dot(second, block, NN) + dot(third, block, NN)
    ridge = RIDGE * trace / slots + 1e-06
    system = system + jnp.where(lane == sub, ridge[:, None, :], 0.0)
    flat = (count * slots, rows)
    base = lanes(flat) // slots * slots
    for pivot in range(slots):
        column = jnp.take_along_axis(
            system.reshape(flat), base + pivot, axis=1, mode="promise_in_bounds"
        ).reshape(shape)
        line = system[:, pivot : pivot + 1, :]
        here = lane[:, 0:1, :] == pivot
        line = jnp.where(here, 1.0, line) / column[:, pivot : pivot + 1, :]
        system = jnp.where(
            sub == pivot, line, jnp.where(lane == pivot, 0.0, system) - column * line
        )
    gram_s[...] = system

    def weigh(batch):
        inverses = [
            split(
                jnp.where(
                    same_slots,
                    jnp.broadcast_to(gram_s[no][None], (GROUP, slots, rows)).reshape(rows, rows),
                    0.0,
                )
            )
            for no in batch
        ]
        solved = [
            dot3(inverse, (right_h[no], right_l[no]), NN) for no, inverse in zip(batch, inverses)
        ]
        for no, weights in zip(batch, solved):
            here = pl.ds(min(no * GROUP, cols - GROUP), GROUP)
            onehot = hot[no].astype(F32).reshape(GROUP, slots, depth)
            crow = jnp.sum(onehot, axis=1, keepdims=True)
            value = weights.reshape(GROUP, slots, depth) * (1.0 - crow) + onehot
            ch[here] = value
            left = value * k_ref[here]
            high, low = split(left)
            lh[here] = high
            ll[here] = low
            high, low = split(smear_z(left.reshape(rows, depth)))
            rh[here] = high.reshape(GROUP, slots, depth)
            rl[here] = low.reshape(GROUP, slots, depth)

    for first in range(0, count, BATCH_2):
        weigh(range(first, min(first + BATCH_2, count)))

    half = GROUP * slots
    tall = (GROUP, half)
    lane_block, lane_in = lanes(tall) // slots, lanes(tall) % slots
    row_of = subs(tall)
    at_block = [lane_block == no for no in range(GROUP)]

    def lane_index(block):
        return block % GROUP * slots + lane_in

    skews = [lane_index(lane_block + row_of + shift) for shift in range(3)]
    sink = (row_of - lane_block + GROUP) % GROUP
    unskew = lane_index(row_of - lane_block + GROUP)

    def take(x, index, axis):
        return jnp.take_along_axis(x, index, axis=axis, mode="promise_in_bounds")

    def flat_tiles(origin, top, chunk, shift):
        parts = []
        for first in range(0, slots, GROUP):
            merged = None
            for no in range(GROUP):
                place = chunk + no + shift
                low = top + (chunk + no) * slots + first
                left_lane = place // GROUP * half
                values = origin[low : low + GROUP, left_lane : left_lane + half]
                here = at_block[place % GROUP]
                merged = values if merged is None else jnp.where(here, values, merged)
            parts.append(take(take(take(merged, skews[shift], 1), sink, 0), unskew, 1))
        return jnp.concatenate(parts, axis=1)

    def put(row, move_x, move_y, origin, top, shift):
        weight = 1.0
        if move_x != 0:
            weight = weight * ANISOTROPY[0]
        if move_y != 0:
            weight = weight * ANISOTROPY[1]
        for chunk in range(0, size_y, GROUP):
            tiles[row, 3 * (move_x + 1) + move_y + 1, chunk : chunk + GROUP, :] = (
                -weight * flat_tiles(origin, top, chunk, shift)
            )

    def mine(row):
        return pl.ds((row + 1) * wide_y + 1, size_y)

    def central(row):
        at = (row + 1) * wide_y
        across = k_ref[pl.ds(at, wide_y)] + ANISOTROPY[0] * (
            k_ref[pl.ds(at - wide_y, wide_y)] + k_ref[pl.ds(at + wide_y, wide_y)]
        )
        along = across[1 : size_y + 1] + ANISOTROPY[1] * (across[0:size_y] + across[2:])
        whole = smear_z(along.reshape(size_y, depth)).reshape(size_y, 1, depth)
        left = (lh[mine(row)].reshape(band, depth), ll[mine(row)].reshape(band, depth))
        right = rh[mine(row)].astype(F32) + rl[mine(row)].astype(F32)
        centre = right - ch[mine(row)] * (whole + SHIFT * k_ref[mine(row)])
        put(row, 0, 0, dot3(left, split(centre.reshape(band, depth)), NT), 0, 0)

    def galerkin(line):
        there = pl.ds(line * wide_y, padded)
        other = (
            rh[there].reshape(padded * slots, depth), rl[there].reshape(padded * slots, depth),
        )
        near_rows = [row for row in range(line - 2, line + 1) if 0 <= row < size_x]
        left = [
            jnp.concatenate([ref[mine(row)].reshape(band, depth) for row in near_rows], axis=0)
            for ref in (lh, ll)
        ]
        product = dot3(left, other, NT)
        for no, row in enumerate(near_rows):
            for move_y in (-1, 0, 1):
                if (row + 1, move_y) != (line, 0):
                    put(row, line - row - 1, move_y, product, no * band, 1 + move_y)

    away = [
        (
            pltpu.make_async_copy(
                ch.at[pl.ds((row + 1) * wide_y + 1, size_y)], interp_ref.at[row], leave.at[0, row]
            ),
            pltpu.make_async_copy(tiles.at[row], coarse_ref.at[row], leave.at[1, row]),
        )
        for row in range(size_x)
    ]
    for pair in away:
        pair[0].start()
    for line in range(size_x + 2):
        galerkin(line)
        if line < size_x:
            central(line)
        if line >= 2:
            away[line - 2][1].start()
    for pair in away:
        for copy in pair:
            copy.wait()


def stay(x):
    return pltpu.with_memory_space_constraint(x, pltpu.VMEM)


def body(nx, ny, nv, vectors, conductivity, c_points):
    vecs, size_x, size_y, depth = vectors.shape
    slots = c_points.shape[-1]
    wide_x, wide_y = size_x + 2 * HALO, size_y + 2 * HALO
    cols = (size_x + 2) * (size_y + 2)
    vmem = pl.BlockSpec(memory_space=pltpu.VMEM)
    hbm = pl.BlockSpec(memory_space=pl.ANY)
    dma = pltpu.SemaphoreType.DMA
    field, knots, spots = pl.pallas_call(
        functools.partial(smooth_kernel, nx, ny, nv),
        out_shape=(
            pltpu.VMEM((nv, size_x + 2, size_y + 2, vecs, depth), F32),
            pltpu.VMEM((size_x + 2, size_y + 2, 1, depth), F32),
            pltpu.VMEM((size_x + 2, size_y + 2, 1, slots), jnp.int32),
        ),
        in_specs=[hbm] * 3,
        out_specs=(vmem,) * 3,
        scratch_shapes=[
            pltpu.VMEM((wide_x, wide_y, vecs, depth), F32),
            pltpu.VMEM((wide_x, wide_y, vecs, depth), F32),
            pltpu.VMEM((wide_x, wide_y, vecs, depth), F32),
            pltpu.VMEM((wide_x, wide_y, vecs, depth), F32),
            pltpu.VMEM((wide_x, wide_y, 1, depth), F32),
            pltpu.VMEM((wide_x, wide_y, 1, slots), jnp.int32),
            dma((3, 9)), dma((3, 9)), dma((nv, 3)), dma((nv, 3)), dma((nv, 9, 2)), dma((nv, 9, 2)),
            dma((vecs,)), dma((2,)),
        ],
        compiler_params=pltpu.CompilerParams(collective_id=0, has_side_effects=True),
        name="smooth",
    )(vectors, conductivity[:, :, None, :], c_points[:, :, None, :])
    count = -(-cols // GROUP)
    rows = GROUP * slots
    more = cols + 2 * GROUP
    interp, coarse = pl.pallas_call(
        functools.partial(coarse_kernel, size_x, size_y, slots),
        out_shape=(
            jax.ShapeDtypeStruct((size_x, size_y, slots, depth), F32),
            jax.ShapeDtypeStruct((size_x, 9, size_y, slots * slots), F32),
        ),
        in_specs=[vmem] * 3,
        out_specs=(hbm, hbm),
        scratch_shapes=[
            pltpu.VMEM((count, rows, depth), BF16),
            pltpu.VMEM((count, rows, depth), BF16),
            pltpu.VMEM((count, rows, depth), BF16),
            pltpu.VMEM((count, slots, rows), F32),
            pltpu.VMEM((more, slots, depth), BF16),
            pltpu.VMEM((more, slots, depth), BF16),
            pltpu.VMEM((more, slots, depth), BF16),
            pltpu.VMEM((more, slots, depth), BF16),
            pltpu.VMEM((more, slots, depth), F32),
            pltpu.VMEM((size_x, 9, size_y, slots * slots), F32),
            dma((2, size_x)),
        ],
        name="coarse",
    )(
        stay(field.reshape(nv, cols, vecs, depth)),
        stay(knots.reshape(cols, 1, depth)),
        stay(spots.reshape(cols, 1, slots)),
    )
    return interp, jnp.transpose(coarse, (0, 2, 1, 3))


def solution(mesh):
    placed = (P("vert", "gx", "gy", None), P("gx", "gy", None), P("gx", "gy", None))
    return jax.shard_map(
        functools.partial(body, mesh.shape["gx"], mesh.shape["gy"], mesh.shape["vert"]),
        mesh=mesh,
        in_specs=placed,
        out_specs=(P("gx", "gy", None, None), P("gx", "gy", None, None)),
        check_vma=False,
    )
```

```python
import functools

import jax
import jax.numpy as jnp
from jax import lax
from jax.experimental import pallas as pl
from jax.experimental.pallas import tpu as pltpu
from jax.sharding import PartitionSpec as P

SWEEPS = 3
ANISOTROPY = (1.0, 0.6, 0.15)
OMEGA = 0.6
SHIFT = 0.5
RIDGE = 0.1
HALO = SWEEPS
GROUP = 8
BATCH_2 = 2
MESH = pl.DeviceIdType.MESH
F32 = jnp.float32
BF16 = jnp.bfloat16


def smear_z(x):
    axis = x.ndim - 1
    depth = x.shape[axis]
    lane = lax.broadcasted_iota(jnp.int32, x.shape, axis)
    below = jnp.where(lane == 0, 0.0, pltpu.roll(x, 1, axis))
    above = jnp.where(lane == depth - 1, 0.0, pltpu.roll(x, depth - 1, axis))
    return x + ANISOTROPY[2] * (below + above)


def smear_line(get, count, across, along):
    summed = [get(0, no) + across * (get(-1, no) + get(1, no)) for no in range(-1, count + 1)]
    return [
        smear_z(summed[no + 1] + along * (summed[no] + summed[no + 2])) for no in range(count)
    ]


def pick(low, first, second):
    return jnp.where(low, jnp.int32(first), jnp.int32(second))


def split(x):
    high = x.astype(BF16)
    return high, (x - high.astype(F32)).astype(BF16)


NT = (((1,), (1,)), ((), ()))
NN = (((1,), (0,)), ((), ()))


def dot(a, b, dims):
    return lax.dot_general(a, b, dims, preferred_element_type=F32)


def dot3(a, b, dims):
    along = dims[0][1][0]
    both = dot(jnp.concatenate([a[0], a[0]], axis=1), jnp.concatenate(b, axis=along), dims)
    return both + dot(a[1], b[0], dims)


def lanes(shape):
    return lax.broadcasted_iota(jnp.int32, shape, len(shape) - 1)


def subs(shape):
    return lax.broadcasted_iota(jnp.int32, shape, len(shape) - 2)


def solver(slots, depth, own):
    rows = GROUP * slots
    members = GROUP * own
    same = subs((rows, members)) // slots == lanes((rows, members)) // own
    same_slots = subs((rows, rows)) // slots == lanes((rows, rows)) // slots
    own_lane = subs((rows, slots)) % slots == lanes((rows, slots))
    ones = jnp.ones((slots, depth), BF16)

    def gather(cells, hot, right_h, right_l, gram_s):
        fields, spreads = [], []
        for field, knots, spots in cells:
            alive = knots > 0.0
            inverse = jnp.where(alive, 1.0 / jnp.where(alive, knots, 1.0), 0.0)
            fields.append(split((field * inverse).reshape(members, depth)))
            spots = jnp.broadcast_to(spots.astype(F32), (GROUP, slots, slots)).reshape(rows, slots)
            spreads.append(dot(jnp.where(own_lane, spots, 0.0).astype(BF16), ones, NN))
        pairs = []
        for no, (spread, (high, low)) in enumerate(zip(spreads, fields)):
            onehot = jnp.where(spread == lanes((rows, depth)).astype(F32), 1.0, 0.0).astype(BF16)
            hot[no] = onehot
            twice = jnp.concatenate([onehot, onehot], axis=1)
            pairs.append(dot(twice, jnp.concatenate([high, low], axis=1), NT))
        pairs = [split(jnp.where(same, cvals, 0.0)) for cvals in pairs]
        grams = [dot3(pair, pair, NT) for pair in pairs]
        rights = [dot3(pair, field, NN) for pair, field in zip(pairs, fields)]
        for no, (gram, right) in enumerate(zip(grams, rights)):
            gram_s[no] = jnp.sum(gram.reshape(GROUP, slots, rows), axis=0)
            high, low = split(right)
            right_h[no] = high
            right_l[no] = low

    def eliminate(system):
        shape = system.shape
        lane = lanes(shape) % slots
        sub = subs(shape)
        diagonal = jnp.sum(jnp.where(lane == sub, system, 0.0), axis=1)
        block = jnp.where(same_slots, 1.0, 0.0).astype(BF16)
        first = diagonal.astype(BF16)
        rest = diagonal - first.astype(F32)
        second = rest.astype(BF16)
        third = (rest - second.astype(F32)).astype(BF16)
        trace = dot(first, block, NN) + dot(second, block, NN) + dot(third, block, NN)
        ridge = RIDGE * trace / slots + 1e-06
        system = system + jnp.where(lane == sub, ridge[:, None, :], 0.0)
        flat = (shape[0] * slots, rows)
        base = lanes(flat) // slots * slots
        for pivot in range(slots):
            column = jnp.take_along_axis(
                system.reshape(flat), base + pivot, axis=1, mode="promise_in_bounds"
            ).reshape(shape)
            line = system[:, pivot : pivot + 1, :]
            here = lane[:, 0:1, :] == pivot
            line = jnp.where(here, 1.0, line) / column[:, pivot : pivot + 1, :]
            system = jnp.where(
                sub == pivot, line, jnp.where(lane == pivot, 0.0, system) - column * line
            )
        return system

    def weigh(inverses, rights, onehots, knots):
        blocks = [
            split(
                jnp.where(
                    same_slots,
                    jnp.broadcast_to(inverse[None], (GROUP, slots, rows)).reshape(rows, rows),
                    0.0,
                )
            )
            for inverse in inverses
        ]
        solved = [dot3(block, right, NN) for block, right in zip(blocks, rights)]
        result = []
        for weights, onehot, knot in zip(solved, onehots, knots):
            onehot = onehot.astype(F32).reshape(GROUP, slots, depth)
            crow = jnp.sum(onehot, axis=1, keepdims=True)
            value = weights.reshape(GROUP, slots, depth) * (1.0 - crow) + onehot
            left = value * knot
            smeared = smear_z(left.reshape(rows, depth)).reshape(GROUP, slots, depth)
            result.append((value,) + split(left) + split(smeared))
        return result

    return gather, eliminate, weigh


def smooth_kernel(
    nx, ny, nv, raw_ref, k_ref, c_ref, out_ref, knots_ref, spots_ref,
    ch_ref, lh_ref, ll_ref, rh_ref, rl_ref,
    one, two, three, gain, wide_k, wide_c, hsend, hrecv, fsend, frecv, rsend, rrecv, turn, load,
    hot, right_h, right_l, gram_s,
):
    size_x, size_y, depth = k_ref.shape[0], k_ref.shape[1], k_ref.shape[3]
    vecs = raw_ref.shape[0]
    wide_x, wide_y = size_x + 2 * HALO, size_y + 2 * HALO
    gx, gy, gv = lax.axis_index("gx"), lax.axis_index("gy"), lax.axis_index("vert")
    near = 1 - 2 * lax.rem(gx, 2)
    far_x = -near
    far_y = pick(gy > 0, -1, 1)
    low_x, low_y = far_x < 0, far_y < 0
    sides_x, sides_y = (0, near, far_x), (0, -far_y, far_y)
    middle, close, far = 0, 1, 2
    moves = [(mx, my) for mx in range(3) for my in range(3) if (mx, my) != (0, 0)]
    if ny <= 2:
        missing = [move for move in moves if move[1] == close]
        moves = [move for move in moves if move[1] != close]
    else:
        missing = []

    inner = pl.ds(HALO, size_x), pl.ds(HALO, size_y)
    loads = [
        pltpu.make_async_copy(source, target.at[inner], load.at[no])
        for no, (source, target) in enumerate(((k_ref, wide_k), (c_ref, wide_c)))
    ]
    turns = [
        pltpu.make_async_copy(raw_ref.at[vec], one.at[inner[0], inner[1], vec], turn.at[vec])
        for vec in range(vecs)
    ]
    for copy in loads + turns:
        copy.start()

    def inside(move):
        at_x, at_y = gx + sides_x[move[0]], gy + sides_y[move[1]]
        ok_x = jnp.logical_and(at_x >= 0, at_x < nx)
        return jnp.logical_and(ok_x, jnp.logical_and(at_y >= 0, at_y < ny))

    def device(move, step=0):
        return (gx + sides_x[move[0]], gy + sides_y[move[1]], lax.rem(gv + step, nv))

    def number(move):
        return 3 * (sides_x[move[0]] + 1) + sides_y[move[1]] + 1

    def opposite(move):
        return 3 * (1 - sides_x[move[0]]) + 1 - sides_y[move[1]]

    barrier = pltpu.get_barrier_semaphore()
    total = jnp.int32(nv - 1)
    for move in moves:
        here = inside(move)

        @pl.when(here)
        def _():
            pl.semaphore_signal(barrier, inc=1, device_id=device(move), device_id_type=MESH)

        total = total + here.astype(jnp.int32)
    for step in range(1, nv):
        pl.semaphore_signal(
            barrier, inc=1, device_id=device((0, 0), step), device_id_type=MESH
        )

    def side(sides, which, size, width, out):
        if which == middle:
            return pl.ds(0 if out else width, size), pl.ds(width, size)
        base = 0 if out else width
        low = sides[which] < 0
        return (
            pl.ds(base + pick(low, 0, size - width), width),
            pl.ds(pick(low, size + width, 0), width),
        )

    def hole(sides, which, size, width):
        if which == middle:
            return pl.ds(width, size)
        return pl.ds(pick(sides[which] < 0, 0, size + width), width)

    fills = ((wide_k, F32), (wide_c, jnp.int32), (one, F32))

    def clear(move):
        at_x, at_y = hole(sides_x, move[0], size_x, HALO), hole(sides_y, move[1], size_y, HALO)
        for target, kind in fills:
            target[at_x, at_y] = jnp.zeros((at_x.size, at_y.size) + target.shape[2:], kind)
        at_x, at_y = hole(sides_x, move[0], size_x, 1), hole(sides_y, move[1], size_y, 1)
        out_ref[:, at_x, at_y] = jnp.zeros((nv, at_x.size, at_y.size, vecs, depth), F32)

    for move in missing:
        clear(move)
    for move in moves:

        @pl.when(jnp.logical_not(inside(move)))
        def _():
            clear(move)

    for copy in loads + turns:
        copy.wait()

    def scale(row, carry):
        for col in range(HALO, HALO + size_y):
            factor = jnp.broadcast_to(wide_k[row, col], (vecs, depth))
            one[row, col] = one[row, col] * factor
        return carry

    lax.fori_loop(HALO, HALO + size_x, scale, 0, unroll=2)
    pl.semaphore_wait(barrier, total)

    kinds = (wide_k, one, wide_c)

    def departure(kind, move):
        from_x, to_x = side(sides_x, move[0], size_x, HALO, False)
        from_y, to_y = side(sides_y, move[1], size_y, HALO, False)
        no = number(move)
        return pltpu.make_async_remote_copy(
            src_ref=kinds[kind].at[from_x, from_y], dst_ref=kinds[kind].at[to_x, to_y],
            send_sem=hsend.at[kind, no], recv_sem=hrecv.at[kind, no],
            device_id=device(move), device_id_type=MESH,
        )

    def arrival(kind, move):
        no = opposite(move)
        place = kinds[kind].at[
            hole(sides_x, move[0], size_x, HALO), hole(sides_y, move[1], size_y, HALO)
        ]
        return pltpu.make_async_remote_copy(
            src_ref=place, dst_ref=place, send_sem=hsend.at[kind, no], recv_sem=hrecv.at[kind, no],
            device_id=device(move), device_id_type=MESH,
        )

    def for_each(some, act):
        for move in some:
            if move in moves:

                @pl.when(inside(move))
                def _():
                    act(move)

    first = [(close, middle), (middle, close), (close, close)]
    second = [(far, middle), (far, close)]
    third = [(middle, far), (close, far), (far, far)]

    def leave(move):
        departure(0, move).start()
        departure(1, move).start()

    for_each(first[:1] + third[:1] + second[:1] + third[1:] + first[1:] + second[1:], leave)

    def start(low, sweep, wide, whole):
        if whole:
            return pick(low, HALO + sweep, sweep)
        return pick(low, sweep, wide - HALO - sweep)

    def region_rows(sweep, part):
        if part == 2:
            return sweep, wide_x - 2 * sweep
        if part == 1:
            return start(low_x, sweep, wide_x, False), HALO
        return start(low_x, sweep, wide_x, True), wide_x - HALO - 2 * sweep

    def region_cols(sweep, part):
        if part == 2:
            return start(low_y, sweep, wide_y, False), HALO
        return start(low_y, sweep, wide_y, True), wide_y - HALO - 2 * sweep

    def sweep_lines(sweep, part, act):
        row, rows = region_rows(sweep, part)
        col, cols = region_cols(sweep, part)
        if part == 2:

            def step(no, carry):
                act(lambda i, j: (row + j, col + no + i), rows, ANISOTROPY[1], ANISOTROPY[0])
                return carry

            lax.fori_loop(0, cols, step, 0, unroll=True)
        else:

            def step(no, carry):
                act(lambda i, j: (row + no + i, col + j), cols, ANISOTROPY[0], ANISOTROPY[1])
                return carry

            lax.fori_loop(0, rows, step, 0, unroll=True if part == 1 else 3)

    def gains(at, count, across, along):
        around = smear_line(lambda i, j: wide_k[at(i, j)], count, across, along)
        for no in range(count):
            mid = wide_k[at(0, no)]
            below = around[no] - (1.0 - SHIFT) * mid
            alive = mid > 0.0
            value = jnp.where(alive, OMEGA * mid / jnp.where(alive, below, 1.0), 0.0)
            gain[at(0, no)] = jnp.broadcast_to(value, (vecs, depth))

    def relax(source, target, at, count, across, along):
        around = smear_line(lambda i, j: source[at(i, j)], count, across, along)
        for no in range(count):
            factor = gain[at(0, no)]
            target(at(0, no), (1.0 - OMEGA - factor) * source[at(0, no)] + factor * around[no])

    def keep(ref):
        def store(at, value):
            ref[at] = value

        return store

    def final(at, value):
        out_ref[gv, at[0] - HALO + 1, at[1] - HALO + 1] = value

    def smooth(part):
        buffers = (one, two, three)
        for sweep in range(1, SWEEPS + 1):
            source = buffers[(sweep - 1) % 3]
            target = final if sweep == SWEEPS else keep(buffers[sweep % 3])
            sweep_lines(sweep, part, functools.partial(relax, source, target))

    def block_copy(step, part, half):
        row, rows = region_rows(SWEEPS, part)
        col, cols = region_cols(SWEEPS, part)
        place = out_ref.at[half, pl.ds(row - HALO + 1, rows), pl.ds(col - HALO + 1, cols)]
        return pltpu.make_async_remote_copy(
            src_ref=place, dst_ref=place,
            send_sem=fsend.at[step - 1, part], recv_sem=frecv.at[step - 1, part],
            device_id=device((0, 0), step), device_id_type=MESH,
        )

    def edge(sides, which, size):
        if which == middle:
            return pl.ds(1, size), pl.ds(1, size), pl.ds(1, size)
        low = sides[which] < 0
        return (
            pl.ds(pick(low, 1, size), 1), pl.ds(pick(low, size + 1, 0), 1),
            pl.ds(pick(low, 0, size + 1), 1),
        )

    def rim_span(piece):
        mx, my, part = piece
        over_x, over_y = edge(sides_x, mx, size_x), edge(sides_y, my, size_y)
        if my == middle:
            col, cols = region_cols(SWEEPS, part)
            over_y = (pl.ds(col - HALO + 1, cols),) * 3
        return over_x, over_y

    def rim_departure(step, piece):
        (from_x, to_x, _), (from_y, to_y, _) = rim_span(piece)
        no = number(piece)
        return pltpu.make_async_remote_copy(
            src_ref=out_ref.at[gv, from_x, from_y], dst_ref=out_ref.at[gv, to_x, to_y],
            send_sem=rsend.at[step, no, piece[2] // 2], recv_sem=rrecv.at[step, no, piece[2] // 2],
            device_id=device(piece, step), device_id_type=MESH,
        )

    def rim_arrival(step, piece):
        (_, _, at_x), (_, _, at_y) = rim_span(piece)
        no = opposite(piece)
        half = lax.rem(gv - step + nv, nv)
        place = out_ref.at[half, at_x, at_y]
        return pltpu.make_async_remote_copy(
            src_ref=place, dst_ref=place,
            send_sem=rsend.at[step, no, piece[2] // 2], recv_sem=rrecv.at[step, no, piece[2] // 2],
            device_id=device(piece, -step + nv), device_id_type=MESH,
        )

    rims = (
        [(close, middle, 0)],
        [(far, middle, 0)],
        [
            (far, far, 2), (close, far, 2), (middle, far, 2), (far, middle, 2), (close, middle, 2),
            (middle, close, 2), (close, close, 2), (far, close, 2),
        ],
    )

    def for_rims(pieces, act):
        for piece in pieces:
            if piece[:2] in moves:

                @pl.when(inside(piece))
                def _():
                    act(piece)

    for part, group in enumerate((first, second, third)):
        for_each(group, lambda move: arrival(0, move).wait_recv())
        sweep_lines(1, part, gains)
        for_each(group, lambda move: arrival(1, move).wait_recv())
        smooth(part)
        for step in range(1, nv):
            if part == 2:
                for_rims(rims[part], lambda piece: rim_departure(step, piece).start())
            block_copy(step, part, gv).start()
            if part < 2:
                for_rims(rims[part], lambda piece: rim_departure(step, piece).start())
        for_rims(rims[part], lambda piece: rim_departure(0, piece).start())
        if part == 0:
            for_each(moves, lambda move: departure(2, move).start())

    slots = c_ref.shape[3]
    gather, eliminate, weigh = solver(slots, depth, nv * vecs)

    def early():
        col, cols = region_cols(SWEEPS, 0)
        col = col - HALO + 1
        groups = early_groups(size_x, cols, col)
        knots = [knots_ref[at] for at in groups]
        gather(
            [
                (
                    jnp.concatenate([out_ref[(half,) + at] for half in range(nv)], axis=1),
                    knot, spots_ref[at],
                )
                for at, knot in zip(groups, knots)
            ],
            hot, right_h, right_l, gram_s,
        )
        gram_s[...] = eliminate(gram_s[...])
        for no in range(len(groups)):
            results = weigh([gram_s[no]], [(right_h[no], right_l[no])], [hot[no]], [knots[no]])
            for ref, value in zip((ch_ref, lh_ref, ll_ref, rh_ref, rl_ref), results[0]):
                ref[no] = value

    for_each(moves, lambda move: arrival(2, move).wait_recv())
    rim_x, rim_y = pl.ds(HALO - 1, size_x + 2), pl.ds(HALO - 1, size_y + 2)
    knots_ref[...] = wide_k[rim_x, rim_y]
    spots_ref[...] = wide_c[rim_x, rim_y]

    for part in range(3):
        for step in range(1, nv):
            block_copy(step, part, lax.rem(gv - step + nv, nv)).wait_recv()
        if part == 1:
            early()
    for step in range(nv):
        for part in range(3):
            for_rims(rims[part], lambda piece: rim_arrival(step, piece).wait_recv())
    for step in range(1, nv):
        for part in range(3):
            block_copy(step, part, gv).wait_send()
    for step in range(nv):
        for part in range(3):
            for_rims(rims[part], lambda piece: rim_departure(step, piece).wait_send())
    for kind in range(3):
        for_each(moves, lambda move: departure(kind, move).wait_send())


def early_groups(size_x, cols, col):
    return [
        (pl.ds(first + 1, GROUP), col + no)
        for first in range(0, size_x, GROUP)
        for no in range(cols)
    ]


def late_groups(size_x, size_y, ny, low):
    groups = early_groups(size_x, HALO, pick(low, 1, size_y - HALO + 1))
    for row in (0, size_x + 1):
        groups += [(row, pl.ds(first + 1, GROUP)) for first in range(0, size_y, GROUP)]
    rims = (pick(low, 0, size_y + 1),) if ny <= 2 else (0, size_y + 1)
    for col in rims:
        groups += [(pl.ds(first + 1, GROUP), col) for first in range(0, size_x, GROUP)]
    corners = [(row, col) for row in (0, size_x + 1) for col in (0, size_y + 1)]
    return groups, [corners[no % len(corners)] for no in range(GROUP)]


def coarse_kernel(
    size_x, size_y, slots, ny, f_ref, k_ref, c_ref, ch_in, lh_in, ll_in, rh_in, rl_in,
    interp_ref, coarse_ref, hot, right_h, right_l, gram_s, lh, ll, rh, rl, ch, tiles, leave,
):
    nv, vecs, depth = f_ref.shape[0], f_ref.shape[3], f_ref.shape[4]
    wide_y = size_y + 2
    rows = GROUP * slots
    padded = -(-wide_y // GROUP) * GROUP
    band = size_y * slots
    low = lax.axis_index("gy") > 0
    gather, eliminate, weigh = solver(slots, depth, nv * vecs)
    places = (ch, lh, ll, rh, rl)

    groups, corners = late_groups(size_x, size_y, ny, low)
    if ny <= 2:
        blank = (pl.ds(1, size_x), pick(low, size_y + 1, 0))
        for ref in (rh, rl):
            ref[blank] = jnp.zeros((size_x, slots, depth), BF16)

    def fetch(ref, no, lead=()):
        if no < len(groups):
            return ref[lead + groups[no]]
        return jnp.stack([ref[lead + at] for at in corners], axis=0)

    def place(no, values):
        for ref, value in zip(places, values):
            if no < len(groups):
                ref[groups[no]] = value
            else:
                for corner in range(len(set(corners))):
                    ref[corners[corner]] = value[corner]

    count = len(groups) + 1
    knots = [fetch(k_ref, no) for no in range(count)]
    gather(
        [
            (
                jnp.concatenate([fetch(f_ref, no, (half,)) for half in range(nv)], axis=1),
                knots[no], fetch(c_ref, no),
            )
            for no in range(count)
        ],
        hot, right_h, right_l, gram_s,
    )
    done = early_groups(size_x, size_y - HALO, pick(low, HALO + 1, 1))
    for no, at in enumerate(done):
        for ref, source in zip(places, (ch_in, lh_in, ll_in, rh_in, rl_in)):
            ref[at] = source[no]
    gram_s[...] = eliminate(gram_s[...])
    for first in range(0, count, BATCH_2):
        batch = range(first, min(first + BATCH_2, count))
        results = weigh(
            [gram_s[no] for no in batch], [(right_h[no], right_l[no]) for no in batch],
            [hot[no] for no in batch], [knots[no] for no in batch],
        )
        for no, values in zip(batch, results):
            place(no, values)

    half = GROUP * slots
    tall = (GROUP, half)
    lane_block, lane_in = lanes(tall) // slots, lanes(tall) % slots
    row_of = subs(tall)
    at_block = [lane_block == no for no in range(GROUP)]

    def lane_index(block):
        return block % GROUP * slots + lane_in

    skews = [lane_index(lane_block + row_of + shift) for shift in range(3)]
    sink = (row_of - lane_block + GROUP) % GROUP
    unskew = lane_index(row_of - lane_block + GROUP)

    def take(x, index, axis):
        return jnp.take_along_axis(x, index, axis=axis, mode="promise_in_bounds")

    def flat_tiles(origin, top, chunk, shift):
        parts = []
        for first in range(0, slots, GROUP):
            merged = None
            for no in range(GROUP):
                place = chunk + no + shift
                low = top + (chunk + no) * slots + first
                left_lane = place // GROUP * half
                values = origin[low : low + GROUP, left_lane : left_lane + half]
                here = at_block[place % GROUP]
                merged = values if merged is None else jnp.where(here, values, merged)
            parts.append(take(take(take(merged, skews[shift], 1), sink, 0), unskew, 1))
        return jnp.concatenate(parts, axis=1)

    def put(row, move_x, move_y, origin, top, shift):
        weight = 1.0
        if move_x != 0:
            weight = weight * ANISOTROPY[0]
        if move_y != 0:
            weight = weight * ANISOTROPY[1]
        for chunk in range(0, size_y, GROUP):
            tiles[row, 3 * (move_x + 1) + move_y + 1, chunk : chunk + GROUP, :] = (
                -weight * flat_tiles(origin, top, chunk, shift)
            )

    def mine(row):
        return row + 1, pl.ds(1, size_y)

    def central(row):
        across = k_ref[row + 1] + ANISOTROPY[0] * (k_ref[row] + k_ref[row + 2])
        along = across[1 : size_y + 1] + ANISOTROPY[1] * (across[0:size_y] + across[2:])
        whole = smear_z(along.reshape(size_y, depth)).reshape(size_y, 1, depth)
        left = (lh[mine(row)].reshape(band, depth), ll[mine(row)].reshape(band, depth))
        right = rh[mine(row)].astype(F32) + rl[mine(row)].astype(F32)
        centre = right - ch[mine(row)] * (whole + SHIFT * k_ref[mine(row)])
        put(row, 0, 0, dot3(left, split(centre.reshape(band, depth)), NT), 0, 0)

    def galerkin(line):
        other = (
            rh[line].reshape(padded * slots, depth), rl[line].reshape(padded * slots, depth),
        )
        near_rows = [row for row in range(line - 2, line + 1) if 0 <= row < size_x]
        left = [
            jnp.concatenate([ref[mine(row)].reshape(band, depth) for row in near_rows], axis=0)
            for ref in (lh, ll)
        ]
        product = dot3(left, other, NT)
        for no, row in enumerate(near_rows):
            for move_y in (-1, 0, 1):
                if (row + 1, move_y) != (line, 0):
                    put(row, line - row - 1, move_y, product, no * band, 1 + move_y)

    away = [
        (
            pltpu.make_async_copy(
                ch.at[mine(row)], interp_ref.at[row], leave.at[0, row]
            ),
            pltpu.make_async_copy(tiles.at[row], coarse_ref.at[row], leave.at[1, row]),
        )
        for row in range(size_x)
    ]
    for pair in away:
        pair[0].start()
    for line in range(size_x + 2):
        galerkin(line)
        if line < size_x:
            central(line)
        if line >= 2:
            away[line - 2][1].start()
    for pair in away:
        for copy in pair:
            copy.wait()


def stay(x):
    return pltpu.with_memory_space_constraint(x, pltpu.VMEM)


def body(nx, ny, nv, vectors, conductivity, c_points):
    vecs, size_x, size_y, depth = vectors.shape
    slots = c_points.shape[-1]
    wide_x, wide_y = size_x + 2 * HALO, size_y + 2 * HALO
    rows = GROUP * slots
    early = (size_y - HALO) * size_x // GROUP
    made = [((early, GROUP, slots, depth), kind) for kind in (F32, BF16, BF16, BF16, BF16)]

    def work(count):
        return [
            pltpu.VMEM((count, rows, depth), BF16),
            pltpu.VMEM((count, rows, depth), BF16),
            pltpu.VMEM((count, rows, depth), BF16),
            pltpu.VMEM((count, slots, rows), F32),
        ]

    vmem = pl.BlockSpec(memory_space=pltpu.VMEM)
    hbm = pl.BlockSpec(memory_space=pl.ANY)
    dma = pltpu.SemaphoreType.DMA
    kept = pl.pallas_call(
        functools.partial(smooth_kernel, nx, ny, nv),
        out_shape=(
            pltpu.VMEM((nv, size_x + 2, size_y + 2, vecs, depth), F32),
            pltpu.VMEM((size_x + 2, size_y + 2, 1, depth), F32),
            pltpu.VMEM((size_x + 2, size_y + 2, 1, slots), jnp.int32),
            *(pltpu.VMEM(*one) for one in made),
        ),
        in_specs=[hbm] * 3,
        out_specs=(vmem,) * 8,
        scratch_shapes=[
            pltpu.VMEM((wide_x, wide_y, vecs, depth), F32),
            pltpu.VMEM((wide_x, wide_y, vecs, depth), F32),
            pltpu.VMEM((wide_x, wide_y, vecs, depth), F32),
            pltpu.VMEM((wide_x, wide_y, vecs, depth), F32),
            pltpu.VMEM((wide_x, wide_y, 1, depth), F32),
            pltpu.VMEM((wide_x, wide_y, 1, slots), jnp.int32),
            dma((3, 9)), dma((3, 9)), dma((nv, 3)), dma((nv, 3)), dma((nv, 9, 2)), dma((nv, 9, 2)),
            dma((vecs,)), dma((2,)), *work(early),
        ],
        compiler_params=pltpu.CompilerParams(collective_id=0, has_side_effects=True),
        name="smooth",
    )(vectors, conductivity[:, :, None, :], c_points[:, :, None, :])
    groups, _ = late_groups(size_x, size_y, ny, True)
    grid = (size_x + 2, -(-(size_y + 2) // GROUP) * GROUP, slots, depth)
    interp, coarse = pl.pallas_call(
        functools.partial(coarse_kernel, size_x, size_y, slots, ny),
        out_shape=(
            jax.ShapeDtypeStruct((size_x, size_y, slots, depth), F32),
            jax.ShapeDtypeStruct((size_x, 9, size_y, slots * slots), F32),
        ),
        in_specs=[vmem] * 8,
        out_specs=(hbm, hbm),
        scratch_shapes=[
            *work(len(groups) + 1),
            pltpu.VMEM(grid, BF16), pltpu.VMEM(grid, BF16), pltpu.VMEM(grid, BF16),
            pltpu.VMEM(grid, BF16), pltpu.VMEM(grid, F32),
            pltpu.VMEM((size_x, 9, size_y, slots * slots), F32),
            dma((2, size_x)),
        ],
        name="coarse",
    )(*(stay(one) for one in kept))
    return interp, jnp.transpose(coarse, (0, 2, 1, 3))


def solution(mesh):
    placed = (P("vert", "gx", "gy", None), P("gx", "gy", None), P("gx", "gy", None))
    return jax.shard_map(
        functools.partial(body, mesh.shape["gx"], mesh.shape["gy"], mesh.shape["vert"]),
        mesh=mesh,
        in_specs=placed,
        out_specs=(P("gx", "gy", None, None), P("gx", "gy", None, None)),
        check_vma=False,
    )
```

```python
import functools

import jax
import jax.numpy as jnp
from jax import lax
from jax.experimental import pallas as pl
from jax.experimental.pallas import tpu as pltpu
from jax.sharding import PartitionSpec as P

SWEEPS = 3
ANISOTROPY = (1.0, 0.6, 0.15)
OMEGA = 0.6
SHIFT = 0.5
RIDGE = 0.1
HALO = SWEEPS
GROUP = 8
BATCH_2 = 2
MESH = pl.DeviceIdType.MESH
F32 = jnp.float32
BF16 = jnp.bfloat16


def smear_z(x):
    axis = x.ndim - 1
    depth = x.shape[axis]
    lane = lax.broadcasted_iota(jnp.int32, x.shape, axis)
    below = jnp.where(lane == 0, 0.0, pltpu.roll(x, 1, axis))
    above = jnp.where(lane == depth - 1, 0.0, pltpu.roll(x, depth - 1, axis))
    return x + ANISOTROPY[2] * (below + above)


def smear_line(get, count, across, along):
    summed = [get(0, no) + across * (get(-1, no) + get(1, no)) for no in range(-1, count + 1)]
    return [
        smear_z(summed[no + 1] + along * (summed[no] + summed[no + 2])) for no in range(count)
    ]


def pick(low, first, second):
    if isinstance(low, bool):
        return first if low else second
    return jnp.where(low, jnp.int32(first), jnp.int32(second))


def split(x):
    high = x.astype(BF16)
    return high, (x - high.astype(F32)).astype(BF16)


NT = (((1,), (1,)), ((), ()))
NN = (((1,), (0,)), ((), ()))


def dot(a, b, dims):
    return lax.dot_general(a, b, dims, preferred_element_type=F32)


def dot3(a, b, dims):
    along = dims[0][1][0]
    both = dot(jnp.concatenate([a[0], a[0]], axis=1), jnp.concatenate(b, axis=along), dims)
    return both + dot(a[1], b[0], dims)


def lanes(shape):
    return lax.broadcasted_iota(jnp.int32, shape, len(shape) - 1)


def subs(shape):
    return lax.broadcasted_iota(jnp.int32, shape, len(shape) - 2)


def solver(slots, depth, own):
    rows = GROUP * slots
    members = GROUP * own
    same = subs((rows, members)) // slots == lanes((rows, members)) // own
    same_slots = subs((rows, rows)) // slots == lanes((rows, rows)) // slots
    own_lane = subs((rows, slots)) % slots == lanes((rows, slots))
    ones = jnp.ones((slots, depth), BF16)

    def gather(cells, hot, right_h, right_l, gram_s):
        fields, spreads = [], []
        for field, knots, spots in cells:
            alive = knots > 0.0
            inverse = jnp.where(alive, 1.0 / jnp.where(alive, knots, 1.0), 0.0)
            fields.append(split((field * inverse).reshape(members, depth)))
            spots = jnp.broadcast_to(spots.astype(F32), (GROUP, slots, slots)).reshape(rows, slots)
            spreads.append(dot(jnp.where(own_lane, spots, 0.0).astype(BF16), ones, NN))
        pairs = []
        for no, (spread, (high, low)) in enumerate(zip(spreads, fields)):
            onehot = jnp.where(spread == lanes((rows, depth)).astype(F32), 1.0, 0.0).astype(BF16)
            hot[no] = onehot
            twice = jnp.concatenate([onehot, onehot], axis=1)
            pairs.append(dot(twice, jnp.concatenate([high, low], axis=1), NT))
        pairs = [split(jnp.where(same, cvals, 0.0)) for cvals in pairs]
        grams = [dot3(pair, pair, NT) for pair in pairs]
        rights = [dot3(pair, field, NN) for pair, field in zip(pairs, fields)]
        for no, (gram, right) in enumerate(zip(grams, rights)):
            gram_s[no] = jnp.sum(gram.reshape(GROUP, slots, rows), axis=0)
            high, low = split(right)
            right_h[no] = high
            right_l[no] = low

    def eliminate(system):
        shape = system.shape
        lane = lanes(shape) % slots
        sub = subs(shape)
        diagonal = jnp.sum(jnp.where(lane == sub, system, 0.0), axis=1)
        block = jnp.where(same_slots, 1.0, 0.0).astype(BF16)
        first = diagonal.astype(BF16)
        rest = diagonal - first.astype(F32)
        second = rest.astype(BF16)
        third = (rest - second.astype(F32)).astype(BF16)
        trace = dot(first, block, NN) + dot(second, block, NN) + dot(third, block, NN)
        ridge = RIDGE * trace / slots + 1e-06
        system = system + jnp.where(lane == sub, ridge[:, None, :], 0.0)
        flat = (shape[0] * slots, rows)
        base = lanes(flat) // slots * slots

        def column(values, no):
            return jnp.take_along_axis(
                values.reshape(flat), base + no, axis=1, mode="promise_in_bounds"
            ).reshape(shape)

        now, ahead, pending = (column(system, no) for no in range(3))
        for pivot in range(slots):
            line = slice(pivot, pivot + 1)
            mine = sub == pivot
            inverse = 1.0 / now[:, line]
            scaled = jnp.where(lane[:, 0:1] == pivot, 1.0, system[:, line]) * inverse

            def advance(values):
                step = values[:, line] * inverse
                return jnp.where(mine, step, values - now * step)

            system = jnp.where(mine, scaled, jnp.where(lane == pivot, 0.0, system) - now * scaled)
            now, ahead = advance(ahead), advance(pending)
            pending = column(system, min(pivot + 3, slots - 1))
        return system

    def weigh(inverses, rights, onehots, knots):
        blocks = [
            split(
                jnp.where(
                    same_slots,
                    jnp.broadcast_to(inverse[None], (GROUP, slots, rows)).reshape(rows, rows),
                    0.0,
                )
            )
            for inverse in inverses
        ]
        solved = [dot3(block, right, NN) for block, right in zip(blocks, rights)]
        result = []
        for weights, onehot, knot in zip(solved, onehots, knots):
            onehot = onehot.astype(F32).reshape(GROUP, slots, depth)
            crow = jnp.sum(onehot, axis=1, keepdims=True)
            value = weights.reshape(GROUP, slots, depth) * (1.0 - crow) + onehot
            left = value * knot
            smeared = smear_z(left.reshape(rows, depth)).reshape(GROUP, slots, depth)
            result.append((value,) + split(left) + split(smeared))
        return result

    return gather, eliminate, weigh


def column_groups(size_x, cols, col):
    return [
        (pl.ds(first + 1, GROUP), col + no)
        for first in range(0, size_x, GROUP)
        for no in range(cols)
    ]


def packed(cells):
    groups = [cells[first : first + GROUP] for first in range(0, len(cells), GROUP)]
    return [group + group[:1] * (GROUP - len(group)) for group in groups]


def early_groups(size_x, size_y, low_x, low_y):
    cols, col = size_y - HALO, pick(low_y, HALO + 1, 1)
    rows = (pick(low_x, size_x + 1, 0), pick(low_x, 0, size_x + 1))
    return column_groups(size_x, cols, col) + packed(
        [(row, col + no) for row in rows for no in range(cols)]
    )


def late_groups(size_x, size_y, ny, low_y):
    col = pick(low_y, 1, size_y - HALO + 1)
    rims = [pick(low_y, 0, size_y + 1)] + ([] if ny <= 2 else [pick(low_y, size_y + 1, 0)])
    groups = column_groups(size_x, HALO, col)
    for rim in rims:
        groups += column_groups(size_x, 1, rim)
    cols = [col + no for no in range(HALO)] + rims
    return groups + packed([(row, at) for row in (0, size_x + 1) for at in cols])


def fetch(ref, group, lead=()):
    if isinstance(group, tuple):
        return ref[lead + group]
    return jnp.stack([ref[lead + at] for at in group], axis=0)


def place(ref, group, value):
    if isinstance(group, tuple):
        ref[group] = value
    else:
        for no, at in enumerate(group):
            if no == 0 or at is not group[0]:
                ref[at] = value[no]


def smooth_kernel(
    nx, ny, nv, raw_ref, k_ref, c_ref, out_ref, knots_ref, spots_ref,
    ch_ref, lh_ref, ll_ref, rh_ref, rl_ref,
    one, two, three, gain, wide_k, wide_c, hsend, hrecv, fsend, frecv, rsend, rrecv, turn, load,
    hot, right_h, right_l, gram_s,
):
    size_x, size_y, depth = k_ref.shape[0], k_ref.shape[1], k_ref.shape[3]
    vecs = raw_ref.shape[0]
    wide_x, wide_y = size_x + 2 * HALO, size_y + 2 * HALO
    gx, gy, gv = lax.axis_index("gx"), lax.axis_index("gy"), lax.axis_index("vert")
    near = 1 - 2 * lax.rem(gx, 2)
    far_x = -near
    far_y = pick(gy > 0, -1, 1)
    low_x, low_y = far_x < 0, far_y < 0
    sides_x, sides_y = (0, near, far_x), (0, -far_y, far_y)
    middle, close, far = 0, 1, 2
    moves = [(mx, my) for mx in range(3) for my in range(3) if (mx, my) != (0, 0)]
    if ny <= 2:
        missing = [move for move in moves if move[1] == close]
        moves = [move for move in moves if move[1] != close]
    else:
        missing = []

    inner = pl.ds(HALO, size_x), pl.ds(HALO, size_y)
    loads = [
        pltpu.make_async_copy(source, target.at[inner], load.at[no])
        for no, (source, target) in enumerate(((k_ref, wide_k), (c_ref, wide_c)))
    ]
    turns = [
        pltpu.make_async_copy(raw_ref.at[vec], one.at[inner[0], inner[1], vec], turn.at[vec])
        for vec in range(vecs)
    ]
    for copy in loads + turns:
        copy.start()

    def inside(move):
        at_x, at_y = gx + sides_x[move[0]], gy + sides_y[move[1]]
        ok_x = jnp.logical_and(at_x >= 0, at_x < nx)
        return jnp.logical_and(ok_x, jnp.logical_and(at_y >= 0, at_y < ny))

    def device(move, step=0):
        return (gx + sides_x[move[0]], gy + sides_y[move[1]], lax.rem(gv + step, nv))

    def number(move):
        return 3 * (sides_x[move[0]] + 1) + sides_y[move[1]] + 1

    def opposite(move):
        return 3 * (1 - sides_x[move[0]]) + 1 - sides_y[move[1]]

    barrier = pltpu.get_barrier_semaphore()
    total = jnp.int32(nv - 1)
    for move in moves:
        here = inside(move)

        @pl.when(here)
        def _():
            pl.semaphore_signal(barrier, inc=1, device_id=device(move), device_id_type=MESH)

        total = total + here.astype(jnp.int32)
    for step in range(1, nv):
        pl.semaphore_signal(
            barrier, inc=1, device_id=device((0, 0), step), device_id_type=MESH
        )

    def side(sides, which, size, width, out):
        if which == middle:
            return pl.ds(0 if out else width, size), pl.ds(width, size)
        base = 0 if out else width
        low = sides[which] < 0
        return (
            pl.ds(base + pick(low, 0, size - width), width),
            pl.ds(pick(low, size + width, 0), width),
        )

    def hole(sides, which, size, width):
        if which == middle:
            return pl.ds(width, size)
        return pl.ds(pick(sides[which] < 0, 0, size + width), width)

    fills = ((wide_k, F32), (wide_c, jnp.int32), (one, F32))

    def clear(move):
        at_x, at_y = hole(sides_x, move[0], size_x, HALO), hole(sides_y, move[1], size_y, HALO)
        for target, kind in fills:
            target[at_x, at_y] = jnp.zeros((at_x.size, at_y.size) + target.shape[2:], kind)
        at_x, at_y = hole(sides_x, move[0], size_x, 1), hole(sides_y, move[1], size_y, 1)
        out_ref[:, at_x, at_y] = jnp.zeros((nv, at_x.size, at_y.size, vecs, depth), F32)

    for move in missing:
        clear(move)
    for move in moves:

        @pl.when(jnp.logical_not(inside(move)))
        def _():
            clear(move)

    for copy in loads + turns:
        copy.wait()

    def scale(row, carry):
        for col in range(HALO, HALO + size_y):
            factor = jnp.broadcast_to(wide_k[row, col], (vecs, depth))
            one[row, col] = one[row, col] * factor
        return carry

    lax.fori_loop(HALO, HALO + size_x, scale, 0, unroll=2)
    pl.semaphore_wait(barrier, total)

    kinds = (wide_k, one, wide_c)

    def departure(kind, move):
        from_x, to_x = side(sides_x, move[0], size_x, HALO, False)
        from_y, to_y = side(sides_y, move[1], size_y, HALO, False)
        no = number(move)
        return pltpu.make_async_remote_copy(
            src_ref=kinds[kind].at[from_x, from_y], dst_ref=kinds[kind].at[to_x, to_y],
            send_sem=hsend.at[kind, no], recv_sem=hrecv.at[kind, no],
            device_id=device(move), device_id_type=MESH,
        )

    def arrival(kind, move):
        no = opposite(move)
        place = kinds[kind].at[
            hole(sides_x, move[0], size_x, HALO), hole(sides_y, move[1], size_y, HALO)
        ]
        return pltpu.make_async_remote_copy(
            src_ref=place, dst_ref=place, send_sem=hsend.at[kind, no], recv_sem=hrecv.at[kind, no],
            device_id=device(move), device_id_type=MESH,
        )

    def for_each(some, act):
        for move in some:
            if move in moves:

                @pl.when(inside(move))
                def _():
                    act(move)

    first = [(close, middle), (middle, close), (close, close)]
    second = [(far, middle), (far, close)]
    third = [(middle, far), (close, far), (far, far)]

    def leave(move):
        departure(0, move).start()
        departure(1, move).start()

    for_each(first[:1] + third[:1] + second[:1] + third[1:] + first[1:] + second[1:], leave)

    def start(low, sweep, wide, whole):
        if whole:
            return pick(low, HALO + sweep, sweep)
        return pick(low, sweep, wide - HALO - sweep)

    def region_rows(sweep, part):
        if part == 2:
            return sweep, wide_x - 2 * sweep
        if part == 1:
            return start(low_x, sweep, wide_x, False), HALO
        return start(low_x, sweep, wide_x, True), wide_x - HALO - 2 * sweep

    def region_cols(sweep, part):
        if part == 2:
            return start(low_y, sweep, wide_y, False), HALO
        return start(low_y, sweep, wide_y, True), wide_y - HALO - 2 * sweep

    def sweep_lines(sweep, part, act):
        row, rows = region_rows(sweep, part)
        col, cols = region_cols(sweep, part)
        if part == 2:

            def step(no, carry):
                act(lambda i, j: (row + j, col + no + i), rows, ANISOTROPY[1], ANISOTROPY[0])
                return carry

            lax.fori_loop(0, cols, step, 0, unroll=True)
        else:

            def step(no, carry):
                act(lambda i, j: (row + no + i, col + j), cols, ANISOTROPY[0], ANISOTROPY[1])
                return carry

            lax.fori_loop(0, rows, step, 0, unroll=True if part == 1 else 3)

    def gains(at, count, across, along):
        around = smear_line(lambda i, j: wide_k[at(i, j)], count, across, along)
        for no in range(count):
            mid = wide_k[at(0, no)]
            below = around[no] - (1.0 - SHIFT) * mid
            alive = mid > 0.0
            value = jnp.where(alive, OMEGA * mid / jnp.where(alive, below, 1.0), 0.0)
            gain[at(0, no)] = jnp.broadcast_to(value, (vecs, depth))

    def relax(source, target, at, count, across, along):
        around = smear_line(lambda i, j: source[at(i, j)], count, across, along)
        for no in range(count):
            factor = gain[at(0, no)]
            target(at(0, no), (1.0 - OMEGA - factor) * source[at(0, no)] + factor * around[no])

    def keep(ref):
        def store(at, value):
            ref[at] = value

        return store

    def final(at, value):
        out_ref[gv, at[0] - HALO + 1, at[1] - HALO + 1] = value

    def smooth(part):
        buffers = (one, two, three)
        for sweep in range(1, SWEEPS + 1):
            source = buffers[(sweep - 1) % 3]
            target = final if sweep == SWEEPS else keep(buffers[sweep % 3])
            sweep_lines(sweep, part, functools.partial(relax, source, target))

    def block_copy(step, part, half):
        row, rows = region_rows(SWEEPS, part)
        col, cols = region_cols(SWEEPS, part)
        place = out_ref.at[half, pl.ds(row - HALO + 1, rows), pl.ds(col - HALO + 1, cols)]
        return pltpu.make_async_remote_copy(
            src_ref=place, dst_ref=place,
            send_sem=fsend.at[step - 1, part], recv_sem=frecv.at[step - 1, part],
            device_id=device((0, 0), step), device_id_type=MESH,
        )

    def edge(sides, which, size):
        if which == middle:
            return pl.ds(1, size), pl.ds(1, size), pl.ds(1, size)
        low = sides[which] < 0
        return (
            pl.ds(pick(low, 1, size), 1), pl.ds(pick(low, size + 1, 0), 1),
            pl.ds(pick(low, 0, size + 1), 1),
        )

    def rim_span(piece):
        mx, my, part = piece
        over_x, over_y = edge(sides_x, mx, size_x), edge(sides_y, my, size_y)
        if my == middle:
            col, cols = region_cols(SWEEPS, part)
            over_y = (pl.ds(col - HALO + 1, cols),) * 3
        return over_x, over_y

    def rim_departure(step, piece):
        (from_x, to_x, _), (from_y, to_y, _) = rim_span(piece)
        no = number(piece)
        return pltpu.make_async_remote_copy(
            src_ref=out_ref.at[gv, from_x, from_y], dst_ref=out_ref.at[gv, to_x, to_y],
            send_sem=rsend.at[step, no, piece[2] // 2], recv_sem=rrecv.at[step, no, piece[2] // 2],
            device_id=device(piece, step), device_id_type=MESH,
        )

    def rim_arrival(step, piece):
        (_, _, at_x), (_, _, at_y) = rim_span(piece)
        no = opposite(piece)
        half = lax.rem(gv - step + nv, nv)
        place = out_ref.at[half, at_x, at_y]
        return pltpu.make_async_remote_copy(
            src_ref=place, dst_ref=place,
            send_sem=rsend.at[step, no, piece[2] // 2], recv_sem=rrecv.at[step, no, piece[2] // 2],
            device_id=device(piece, -step + nv), device_id_type=MESH,
        )

    rims = (
        [(close, middle, 0)],
        [(far, middle, 0)],
        [
            (far, far, 2), (close, far, 2), (middle, far, 2), (far, middle, 2), (close, middle, 2),
            (middle, close, 2), (close, close, 2), (far, close, 2),
        ],
    )

    def for_rims(pieces, act):
        for piece in pieces:
            if piece[:2] in moves:

                @pl.when(inside(piece))
                def _():
                    act(piece)

    for part, group in enumerate((first, second, third)):
        for_each(group, lambda move: arrival(0, move).wait_recv())
        sweep_lines(1, part, gains)
        for_each(group, lambda move: arrival(1, move).wait_recv())
        smooth(part)
        for step in range(1, nv):
            if part == 2:
                for_rims(rims[part], lambda piece: rim_departure(step, piece).start())
            block_copy(step, part, gv).start()
            if part < 2:
                for_rims(rims[part], lambda piece: rim_departure(step, piece).start())
        for_rims(rims[part], lambda piece: rim_departure(0, piece).start())
        if part == 0:
            for_each(moves, lambda move: departure(2, move).start())

    slots = c_ref.shape[3]
    gather, eliminate, weigh = solver(slots, depth, nv * vecs)

    def early():
        groups = early_groups(size_x, size_y, low_x, low_y)
        knots = [fetch(knots_ref, group) for group in groups]
        gather(
            [
                (
                    jnp.concatenate([fetch(out_ref, group, (half,)) for half in range(nv)], axis=1),
                    knot, fetch(spots_ref, group),
                )
                for group, knot in zip(groups, knots)
            ],
            hot, right_h, right_l, gram_s,
        )
        gram_s[...] = eliminate(gram_s[...])
        for no in range(len(groups)):
            results = weigh([gram_s[no]], [(right_h[no], right_l[no])], [hot[no]], [knots[no]])
            for ref, value in zip((ch_ref, lh_ref, ll_ref, rh_ref, rl_ref), results[0]):
                ref[no] = value

    for_each(moves, lambda move: arrival(2, move).wait_recv())
    rim_x, rim_y = pl.ds(HALO - 1, size_x + 2), pl.ds(HALO - 1, size_y + 2)
    knots_ref[...] = wide_k[rim_x, rim_y]
    spots_ref[...] = wide_c[rim_x, rim_y]

    def wait_blocks(part):
        for step in range(1, nv):
            block_copy(step, part, lax.rem(gv - step + nv, nv)).wait_recv()

    def wait_rims(part):
        for step in range(nv):
            for_rims(rims[part], lambda piece: rim_arrival(step, piece).wait_recv())

    for part in range(2):
        wait_blocks(part)
        wait_rims(part)
    early()
    for part in range(3):
        for step in range(1, nv):
            block_copy(step, part, gv).wait_send()
        for step in range(nv):
            for_rims(rims[part], lambda piece: rim_departure(step, piece).wait_send())
    for kind in range(3):
        for_each(moves, lambda move: departure(kind, move).wait_send())
    wait_blocks(2)
    wait_rims(2)


def coarse_kernel(
    size_x, size_y, slots, ny, f_ref, k_ref, c_ref, ch_in, lh_in, ll_in, rh_in, rl_in,
    interp_ref, coarse_ref, hot, right_h, right_l, gram_s, lh, ll, rh, rl, ch, tiles, leave,
):
    nv, vecs, depth = f_ref.shape[0], f_ref.shape[3], f_ref.shape[4]
    wide_y = size_y + 2
    rows = GROUP * slots
    padded = -(-wide_y // GROUP) * GROUP
    band = size_y * slots
    low_x, low_y = lax.rem(lax.axis_index("gx"), 2) == 0, lax.axis_index("gy") > 0
    gather, eliminate, weigh = solver(slots, depth, nv * vecs)
    places = (ch, lh, ll, rh, rl)

    groups = late_groups(size_x, size_y, ny, low_y)
    if ny <= 2:
        blank = (pl.ds(0, size_x + 2), pick(low_y, size_y + 1, 0))
        for ref in (rh, rl):
            ref[blank] = jnp.zeros((size_x + 2, slots, depth), BF16)

    knots = [fetch(k_ref, group) for group in groups]
    gather(
        [
            (
                jnp.concatenate([fetch(f_ref, group, (half,)) for half in range(nv)], axis=1),
                knot, fetch(c_ref, group),
            )
            for group, knot in zip(groups, knots)
        ],
        hot, right_h, right_l, gram_s,
    )
    for no, group in enumerate(early_groups(size_x, size_y, low_x, low_y)):
        for ref, source in zip(places, (ch_in, lh_in, ll_in, rh_in, rl_in)):
            place(ref, group, source[no])
    gram_s[...] = eliminate(gram_s[...])
    for first in range(0, len(groups), BATCH_2):
        batch = range(first, min(first + BATCH_2, len(groups)))
        results = weigh(
            [gram_s[no] for no in batch], [(right_h[no], right_l[no]) for no in batch],
            [hot[no] for no in batch], [knots[no] for no in batch],
        )
        for no, values in zip(batch, results):
            for ref, value in zip(places, values):
                place(ref, groups[no], value)

    half = GROUP * slots
    tall = (GROUP, half)
    lane_block, lane_in = lanes(tall) // slots, lanes(tall) % slots
    row_of = subs(tall)
    at_block = [lane_block == no for no in range(GROUP)]

    def lane_index(block):
        return block % GROUP * slots + lane_in

    skews = [lane_index(lane_block + row_of + shift) for shift in range(3)]
    sink = (row_of - lane_block + GROUP) % GROUP
    unskew = lane_index(row_of - lane_block + GROUP)

    def take(x, index, axis):
        return jnp.take_along_axis(x, index, axis=axis, mode="promise_in_bounds")

    def flat_tiles(origin, top, chunk, shift):
        parts = []
        for first in range(0, slots, GROUP):
            merged = None
            for no in range(GROUP):
                place = chunk + no + shift
                low = top + (chunk + no) * slots + first
                left_lane = place // GROUP * half
                values = origin[low : low + GROUP, left_lane : left_lane + half]
                here = at_block[place % GROUP]
                merged = values if merged is None else jnp.where(here, values, merged)
            parts.append(take(take(take(merged, skews[shift], 1), sink, 0), unskew, 1))
        return jnp.concatenate(parts, axis=1)

    def put(row, move_x, move_y, origin, top, shift):
        weight = 1.0
        if move_x != 0:
            weight = weight * ANISOTROPY[0]
        if move_y != 0:
            weight = weight * ANISOTROPY[1]
        for chunk in range(0, size_y, GROUP):
            tiles[row, 3 * (move_x + 1) + move_y + 1, chunk : chunk + GROUP, :] = (
                -weight * flat_tiles(origin, top, chunk, shift)
            )

    def mine(row):
        return row + 1, pl.ds(1, size_y)

    def central(row):
        across = k_ref[row + 1] + ANISOTROPY[0] * (k_ref[row] + k_ref[row + 2])
        along = across[1 : size_y + 1] + ANISOTROPY[1] * (across[0:size_y] + across[2:])
        whole = smear_z(along.reshape(size_y, depth)).reshape(size_y, 1, depth)
        left = (lh[mine(row)].reshape(band, depth), ll[mine(row)].reshape(band, depth))
        right = rh[mine(row)].astype(F32) + rl[mine(row)].astype(F32)
        centre = right - ch[mine(row)] * (whole + SHIFT * k_ref[mine(row)])
        put(row, 0, 0, dot3(left, split(centre.reshape(band, depth)), NT), 0, 0)

    def galerkin(line):
        other = (
            rh[line].reshape(padded * slots, depth), rl[line].reshape(padded * slots, depth),
        )
        near_rows = [row for row in range(line - 2, line + 1) if 0 <= row < size_x]
        left = [
            jnp.concatenate([ref[mine(row)].reshape(band, depth) for row in near_rows], axis=0)
            for ref in (lh, ll)
        ]
        product = dot3(left, other, NT)
        for no, row in enumerate(near_rows):
            for move_y in (-1, 0, 1):
                if (row + 1, move_y) != (line, 0):
                    put(row, line - row - 1, move_y, product, no * band, 1 + move_y)

    away = [
        (
            pltpu.make_async_copy(
                ch.at[mine(row)], interp_ref.at[row], leave.at[0, row]
            ),
            pltpu.make_async_copy(tiles.at[row], coarse_ref.at[row], leave.at[1, row]),
        )
        for row in range(size_x)
    ]
    for pair in away:
        pair[0].start()
    for line in range(size_x + 2):
        galerkin(line)
        if line < size_x:
            central(line)
        if line >= 2:
            away[line - 2][1].start()
    for pair in away:
        for copy in pair:
            copy.wait()


def stay(x):
    return pltpu.with_memory_space_constraint(x, pltpu.VMEM)


def body(nx, ny, nv, vectors, conductivity, c_points):
    vecs, size_x, size_y, depth = vectors.shape
    slots = c_points.shape[-1]
    wide_x, wide_y = size_x + 2 * HALO, size_y + 2 * HALO
    rows = GROUP * slots
    early = len(early_groups(size_x, size_y, True, True))
    made = [((early, GROUP, slots, depth), kind) for kind in (F32, BF16, BF16, BF16, BF16)]

    def work(count):
        return [
            pltpu.VMEM((count, rows, depth), BF16),
            pltpu.VMEM((count, rows, depth), BF16),
            pltpu.VMEM((count, rows, depth), BF16),
            pltpu.VMEM((count, slots, rows), F32),
        ]

    vmem = pl.BlockSpec(memory_space=pltpu.VMEM)
    hbm = pl.BlockSpec(memory_space=pl.ANY)
    dma = pltpu.SemaphoreType.DMA
    kept = pl.pallas_call(
        functools.partial(smooth_kernel, nx, ny, nv),
        out_shape=(
            pltpu.VMEM((nv, size_x + 2, size_y + 2, vecs, depth), F32),
            pltpu.VMEM((size_x + 2, size_y + 2, 1, depth), F32),
            pltpu.VMEM((size_x + 2, size_y + 2, 1, slots), jnp.int32),
            *(pltpu.VMEM(*one) for one in made),
        ),
        in_specs=[hbm] * 3,
        out_specs=(vmem,) * 8,
        scratch_shapes=[
            pltpu.VMEM((wide_x, wide_y, vecs, depth), F32),
            pltpu.VMEM((wide_x, wide_y, vecs, depth), F32),
            pltpu.VMEM((wide_x, wide_y, vecs, depth), F32),
            pltpu.VMEM((wide_x, wide_y, vecs, depth), F32),
            pltpu.VMEM((wide_x, wide_y, 1, depth), F32),
            pltpu.VMEM((wide_x, wide_y, 1, slots), jnp.int32),
            dma((3, 9)), dma((3, 9)), dma((nv, 3)), dma((nv, 3)), dma((nv, 9, 2)), dma((nv, 9, 2)),
            dma((vecs,)), dma((2,)), *work(early),
        ],
        compiler_params=pltpu.CompilerParams(collective_id=0, has_side_effects=True),
        name="smooth",
    )(vectors, conductivity[:, :, None, :], c_points[:, :, None, :])
    late = len(late_groups(size_x, size_y, ny, True))
    grid = (size_x + 2, -(-(size_y + 2) // GROUP) * GROUP, slots, depth)
    interp, coarse = pl.pallas_call(
        functools.partial(coarse_kernel, size_x, size_y, slots, ny),
        out_shape=(
            jax.ShapeDtypeStruct((size_x, size_y, slots, depth), F32),
            jax.ShapeDtypeStruct((size_x, 9, size_y, slots * slots), F32),
        ),
        in_specs=[vmem] * 8,
        out_specs=(hbm, hbm),
        scratch_shapes=[
            *work(late),
            pltpu.VMEM(grid, BF16), pltpu.VMEM(grid, BF16), pltpu.VMEM(grid, BF16),
            pltpu.VMEM(grid, BF16), pltpu.VMEM(grid, F32),
            pltpu.VMEM((size_x, 9, size_y, slots * slots), F32),
            dma((2, size_x)),
        ],
        name="coarse",
    )(*(stay(one) for one in kept))
    return interp, jnp.transpose(coarse, (0, 2, 1, 3))


def solution(mesh):
    placed = (P("vert", "gx", "gy", None), P("gx", "gy", None), P("gx", "gy", None))
    return jax.shard_map(
        functools.partial(body, mesh.shape["gx"], mesh.shape["gy"], mesh.shape["vert"]),
        mesh=mesh,
        in_specs=placed,
        out_specs=(P("gx", "gy", None, None), P("gx", "gy", None, None)),
        check_vma=False,
    )
```

```python
import functools

import jax
import jax.numpy as jnp
from jax import lax
from jax.experimental import pallas as pl
from jax.experimental.pallas import tpu as pltpu
from jax.sharding import PartitionSpec as P

SWEEPS = 3
ANISOTROPY = (1.0, 0.6, 0.15)
OMEGA = 0.6
SHIFT = 0.5
RIDGE = 0.1
HALO = SWEEPS
GROUP = 8
BATCH_2 = 2
MESH = pl.DeviceIdType.MESH
F32 = jnp.float32
BF16 = jnp.bfloat16


def smear_z(x):
    axis = x.ndim - 1
    depth = x.shape[axis]
    lane = lax.broadcasted_iota(jnp.int32, x.shape, axis)
    below = jnp.where(lane == 0, 0.0, pltpu.roll(x, 1, axis))
    above = jnp.where(lane == depth - 1, 0.0, pltpu.roll(x, depth - 1, axis))
    return x + ANISOTROPY[2] * (below + above)


def smear_line(get, count, across, along):
    summed = [get(0, no) + across * (get(-1, no) + get(1, no)) for no in range(-1, count + 1)]
    return [
        smear_z(summed[no + 1] + along * (summed[no] + summed[no + 2])) for no in range(count)
    ]


def pick(low, first, second):
    if isinstance(low, bool):
        return first if low else second
    return jnp.where(low, jnp.int32(first), jnp.int32(second))


def split(x):
    high = x.astype(BF16)
    return high, (x - high.astype(F32)).astype(BF16)


NT = (((1,), (1,)), ((), ()))
NN = (((1,), (0,)), ((), ()))


def dot(a, b, dims):
    return lax.dot_general(a, b, dims, preferred_element_type=F32)


def dot3(a, b, dims):
    along = dims[0][1][0]
    both = dot(jnp.concatenate([a[0], a[0]], axis=1), jnp.concatenate(b, axis=along), dims)
    return both + dot(a[1], b[0], dims)


def lanes(shape):
    return lax.broadcasted_iota(jnp.int32, shape, len(shape) - 1)


def subs(shape):
    return lax.broadcasted_iota(jnp.int32, shape, len(shape) - 2)


def solver(slots, depth, own):
    rows = GROUP * slots
    members = GROUP * own
    same = subs((rows, members)) // slots == lanes((rows, members)) // own
    same_slots = subs((rows, rows)) // slots == lanes((rows, rows)) // slots
    own_lane = subs((rows, slots)) % slots == lanes((rows, slots))
    ones = jnp.ones((slots, depth), BF16)

    def mark(places):
        onehots = []
        for spots in places:
            spots = jnp.broadcast_to(spots.astype(F32), (GROUP, slots, slots)).reshape(rows, slots)
            spread = dot(jnp.where(own_lane, spots, 0.0).astype(BF16), ones, NN)
            onehots.append(
                jnp.where(spread == lanes((rows, depth)).astype(F32), 1.0, 0.0).astype(BF16)
            )
        return onehots

    def inverted(knots):
        alive = knots > 0.0
        return jnp.where(alive, 1.0 / jnp.where(alive, knots, 1.0), 0.0)

    def gather(cells, hot, right_h, right_l, gram_s):
        fields = [split((field * inverse).reshape(members, depth)) for field, inverse in cells]
        pairs = []
        for no, (high, low) in enumerate(fields):
            onehot = hot[no]
            twice = jnp.concatenate([onehot, onehot], axis=1)
            pairs.append(dot(twice, jnp.concatenate([high, low], axis=1), NT))
        pairs = [split(jnp.where(same, cvals, 0.0)) for cvals in pairs]
        grams = [dot3(pair, pair, NT) for pair in pairs]
        rights = [dot3(pair, field, NN) for pair, field in zip(pairs, fields)]
        for no, (gram, right) in enumerate(zip(grams, rights)):
            gram_s[no] = jnp.sum(gram.reshape(GROUP, slots, rows), axis=0)
            high, low = split(right)
            right_h[no] = high
            right_l[no] = low

    def eliminate(system):
        shape = system.shape
        lane = lanes(shape) % slots
        sub = subs(shape)
        diagonal = jnp.sum(jnp.where(lane == sub, system, 0.0), axis=1)
        block = jnp.where(same_slots, 1.0, 0.0).astype(BF16)
        first = diagonal.astype(BF16)
        rest = diagonal - first.astype(F32)
        second = rest.astype(BF16)
        third = (rest - second.astype(F32)).astype(BF16)
        trace = dot(first, block, NN) + dot(second, block, NN) + dot(third, block, NN)
        ridge = RIDGE * trace / slots + 1e-06
        system = system + jnp.where(lane == sub, ridge[:, None, :], 0.0)
        flat = (shape[0] * slots, rows)
        base = lanes(flat) // slots * slots

        def column(values, no):
            return jnp.take_along_axis(
                values.reshape(flat), base + no, axis=1, mode="promise_in_bounds"
            ).reshape(shape)

        now, ahead, pending = (column(system, no) for no in range(3))
        for pivot in range(slots):
            line = slice(pivot, pivot + 1)
            mine = sub == pivot
            inverse = 1.0 / now[:, line]
            scaled = jnp.where(lane[:, 0:1] == pivot, 1.0, system[:, line]) * inverse

            def advance(values):
                step = values[:, line] * inverse
                return jnp.where(mine, step, values - now * step)

            system = jnp.where(mine, scaled, jnp.where(lane == pivot, 0.0, system) - now * scaled)
            now, ahead = advance(ahead), advance(pending)
            pending = column(system, min(pivot + 3, slots - 1))
        return system

    def weigh(inverses, rights, onehots, knots):
        blocks = [
            split(
                jnp.where(
                    same_slots,
                    jnp.broadcast_to(inverse[None], (GROUP, slots, rows)).reshape(rows, rows),
                    0.0,
                )
            )
            for inverse in inverses
        ]
        solved = [dot3(block, right, NN) for block, right in zip(blocks, rights)]
        result = []
        for weights, onehot, knot in zip(solved, onehots, knots):
            onehot = onehot.astype(F32).reshape(GROUP, slots, depth)
            crow = jnp.sum(onehot, axis=1, keepdims=True)
            value = weights.reshape(GROUP, slots, depth) * (1.0 - crow) + onehot
            left = value * knot
            smeared = smear_z(left.reshape(rows, depth)).reshape(GROUP, slots, depth)
            result.append((value,) + split(left) + split(smeared))
        return result

    return mark, inverted, gather, eliminate, weigh


def column_groups(size_x, cols, col):
    return [
        (pl.ds(first + 1, GROUP), col + no)
        for first in range(0, size_x, GROUP)
        for no in range(cols)
    ]


def packed(cells):
    groups = [cells[first : first + GROUP] for first in range(0, len(cells), GROUP)]
    return [group + group[:1] * (GROUP - len(group)) for group in groups]


def early_groups(size_x, size_y, low_x, low_y):
    cols, col = size_y - HALO, pick(low_y, HALO + 1, 1)
    rows = (pick(low_x, size_x + 1, 0), pick(low_x, 0, size_x + 1))
    return column_groups(size_x, cols, col) + packed(
        [(row, col + no) for row in rows for no in range(cols)]
    )


def late_groups(size_x, size_y, ny, low_y):
    col = pick(low_y, 1, size_y - HALO + 1)
    rims = [pick(low_y, 0, size_y + 1)] + ([] if ny <= 2 else [pick(low_y, size_y + 1, 0)])
    groups = column_groups(size_x, HALO, col)
    for rim in rims:
        groups += column_groups(size_x, 1, rim)
    cols = [col + no for no in range(HALO)] + rims
    return groups + packed([(row, at) for row in (0, size_x + 1) for at in cols])


def fetch(ref, group, lead=()):
    if isinstance(group, tuple):
        return ref[lead + group]
    return jnp.stack([ref[lead + at] for at in group], axis=0)


def place(ref, group, value):
    if isinstance(group, tuple):
        ref[group] = value
    else:
        for no, at in enumerate(group):
            if no == 0 or at is not group[0]:
                ref[at] = value[no]


def smooth_kernel(
    nx, ny, nv, raw_ref, k_ref, c_ref, out_ref, knots_ref, spots_ref,
    ch_ref, lh_ref, ll_ref, rh_ref, rl_ref, full_ref, late_hot,
    one, two, three, gain, wide_k, wide_c, hsend, hrecv, fsend, frecv, rsend, rrecv, turn, load,
    hot, right_h, right_l, gram_s,
):
    size_x, size_y, depth = k_ref.shape[0], k_ref.shape[1], k_ref.shape[3]
    vecs = raw_ref.shape[0]
    wide_x, wide_y = size_x + 2 * HALO, size_y + 2 * HALO
    gx, gy, gv = lax.axis_index("gx"), lax.axis_index("gy"), lax.axis_index("vert")
    near = 1 - 2 * lax.rem(gx, 2)
    far_x = -near
    far_y = pick(gy > 0, -1, 1)
    low_x, low_y = far_x < 0, far_y < 0
    sides_x, sides_y = (0, near, far_x), (0, -far_y, far_y)
    middle, close, far = 0, 1, 2
    moves = [(mx, my) for mx in range(3) for my in range(3) if (mx, my) != (0, 0)]
    if ny <= 2:
        missing = [move for move in moves if move[1] == close]
        moves = [move for move in moves if move[1] != close]
    else:
        missing = []

    inner = pl.ds(HALO, size_x), pl.ds(HALO, size_y)
    loads = [
        pltpu.make_async_copy(source, target.at[inner], load.at[no])
        for no, (source, target) in enumerate(((k_ref, wide_k), (c_ref, wide_c)))
    ]
    turns = [
        pltpu.make_async_copy(raw_ref.at[vec], one.at[inner[0], inner[1], vec], turn.at[vec])
        for vec in range(vecs)
    ]
    for copy in loads + turns:
        copy.start()

    def inside(move):
        at_x, at_y = gx + sides_x[move[0]], gy + sides_y[move[1]]
        ok_x = jnp.logical_and(at_x >= 0, at_x < nx)
        return jnp.logical_and(ok_x, jnp.logical_and(at_y >= 0, at_y < ny))

    def device(move, step=0):
        return (gx + sides_x[move[0]], gy + sides_y[move[1]], lax.rem(gv + step, nv))

    def number(move):
        return 3 * (sides_x[move[0]] + 1) + sides_y[move[1]] + 1

    def opposite(move):
        return 3 * (1 - sides_x[move[0]]) + 1 - sides_y[move[1]]

    barrier = pltpu.get_barrier_semaphore()
    total = jnp.int32(nv - 1)
    for move in moves:
        here = inside(move)

        @pl.when(here)
        def _():
            pl.semaphore_signal(barrier, inc=1, device_id=device(move), device_id_type=MESH)

        total = total + here.astype(jnp.int32)
    for step in range(1, nv):
        pl.semaphore_signal(
            barrier, inc=1, device_id=device((0, 0), step), device_id_type=MESH
        )

    def side(sides, which, size, width, out):
        if which == middle:
            return pl.ds(0 if out else width, size), pl.ds(width, size)
        base = 0 if out else width
        low = sides[which] < 0
        return (
            pl.ds(base + pick(low, 0, size - width), width),
            pl.ds(pick(low, size + width, 0), width),
        )

    def hole(sides, which, size, width):
        if which == middle:
            return pl.ds(width, size)
        return pl.ds(pick(sides[which] < 0, 0, size + width), width)

    fills = ((wide_k, F32), (wide_c, jnp.int32), (one, F32))

    def clear(move):
        at_x, at_y = hole(sides_x, move[0], size_x, HALO), hole(sides_y, move[1], size_y, HALO)
        for target, kind in fills:
            target[at_x, at_y] = jnp.zeros((at_x.size, at_y.size) + target.shape[2:], kind)
        at_x, at_y = hole(sides_x, move[0], size_x, 1), hole(sides_y, move[1], size_y, 1)
        out_ref[:, at_x, at_y] = jnp.zeros((nv, at_x.size, at_y.size, vecs, depth), F32)

    for move in missing:
        clear(move)
    for move in moves:

        @pl.when(jnp.logical_not(inside(move)))
        def _():
            clear(move)

    for copy in loads + turns:
        copy.wait()

    def scale(row, carry):
        for col in range(HALO, HALO + size_y):
            factor = jnp.broadcast_to(wide_k[row, col], (vecs, depth))
            one[row, col] = one[row, col] * factor
        return carry

    lax.fori_loop(HALO, HALO + size_x, scale, 0, unroll=2)
    pl.semaphore_wait(barrier, total)

    kinds = (wide_k, one, wide_c)

    def departure(kind, move):
        from_x, to_x = side(sides_x, move[0], size_x, HALO, False)
        from_y, to_y = side(sides_y, move[1], size_y, HALO, False)
        no = number(move)
        return pltpu.make_async_remote_copy(
            src_ref=kinds[kind].at[from_x, from_y], dst_ref=kinds[kind].at[to_x, to_y],
            send_sem=hsend.at[kind, no], recv_sem=hrecv.at[kind, no],
            device_id=device(move), device_id_type=MESH,
        )

    def arrival(kind, move):
        no = opposite(move)
        place = kinds[kind].at[
            hole(sides_x, move[0], size_x, HALO), hole(sides_y, move[1], size_y, HALO)
        ]
        return pltpu.make_async_remote_copy(
            src_ref=place, dst_ref=place, send_sem=hsend.at[kind, no], recv_sem=hrecv.at[kind, no],
            device_id=device(move), device_id_type=MESH,
        )

    def for_each(some, act):
        for move in some:
            if move in moves:

                @pl.when(inside(move))
                def _():
                    act(move)

    first = [(close, middle), (middle, close), (close, close)]
    second = [(far, middle), (far, close)]
    third = [(middle, far), (close, far), (far, far)]

    def leave(move):
        departure(0, move).start()
        departure(1, move).start()

    for_each(first[:1] + third[:1] + second[:1] + third[1:] + first[1:] + second[1:], leave)

    def start(low, sweep, wide, whole):
        if whole:
            return pick(low, HALO + sweep, sweep)
        return pick(low, sweep, wide - HALO - sweep)

    def region_rows(sweep, part):
        if part == 2:
            return sweep, wide_x - 2 * sweep
        if part == 1:
            return start(low_x, sweep, wide_x, False), HALO
        return start(low_x, sweep, wide_x, True), wide_x - HALO - 2 * sweep

    def region_cols(sweep, part):
        if part == 2:
            return start(low_y, sweep, wide_y, False), HALO
        return start(low_y, sweep, wide_y, True), wide_y - HALO - 2 * sweep

    def sweep_lines(sweep, part, act):
        row, rows = region_rows(sweep, part)
        col, cols = region_cols(sweep, part)
        if part == 2:

            def step(no, carry):
                act(lambda i, j: (row + j, col + no + i), rows, ANISOTROPY[1], ANISOTROPY[0])
                return carry

            lax.fori_loop(0, cols, step, 0, unroll=True)
        else:

            def step(no, carry):
                act(lambda i, j: (row + no + i, col + j), cols, ANISOTROPY[0], ANISOTROPY[1])
                return carry

            lax.fori_loop(0, rows, step, 0, unroll=True)

    def gains(at, count, across, along):
        around = smear_line(lambda i, j: wide_k[at(i, j)], count, across, along)
        for no in range(count):
            mid = wide_k[at(0, no)]
            below = around[no] - (1.0 - SHIFT) * mid
            alive = mid > 0.0
            value = jnp.where(alive, OMEGA * mid / jnp.where(alive, below, 1.0), 0.0)
            gain[at(0, no)] = jnp.broadcast_to(value, (vecs, depth))

    def relax(source, target, at, count, across, along):
        around = smear_line(lambda i, j: source[at(i, j)], count, across, along)
        for no in range(count):
            factor = gain[at(0, no)]
            target(at(0, no), (1.0 - OMEGA - factor) * source[at(0, no)] + factor * around[no])

    def keep(ref):
        def store(at, value):
            ref[at] = value

        return store

    def final(at, value):
        out_ref[gv, at[0] - HALO + 1, at[1] - HALO + 1] = value

    def smooth(part):
        buffers = (one, two, three)
        for sweep in range(1, SWEEPS + 1):
            source = buffers[(sweep - 1) % 3]
            target = final if sweep == SWEEPS else keep(buffers[sweep % 3])
            sweep_lines(sweep, part, functools.partial(relax, source, target))

    def block_copy(step, part, half):
        row, rows = region_rows(SWEEPS, part)
        col, cols = region_cols(SWEEPS, part)
        place = out_ref.at[half, pl.ds(row - HALO + 1, rows), pl.ds(col - HALO + 1, cols)]
        return pltpu.make_async_remote_copy(
            src_ref=place, dst_ref=place,
            send_sem=fsend.at[step - 1, part], recv_sem=frecv.at[step - 1, part],
            device_id=device((0, 0), step), device_id_type=MESH,
        )

    def edge(sides, which, size):
        if which == middle:
            return pl.ds(1, size), pl.ds(1, size), pl.ds(1, size)
        low = sides[which] < 0
        return (
            pl.ds(pick(low, 1, size), 1), pl.ds(pick(low, size + 1, 0), 1),
            pl.ds(pick(low, 0, size + 1), 1),
        )

    def rim_span(piece):
        mx, my, part = piece
        over_x, over_y = edge(sides_x, mx, size_x), edge(sides_y, my, size_y)
        if my == middle:
            col, cols = region_cols(SWEEPS, part)
            over_y = (pl.ds(col - HALO + 1, cols),) * 3
        return over_x, over_y

    def rim_departure(step, piece):
        (from_x, to_x, _), (from_y, to_y, _) = rim_span(piece)
        no = number(piece)
        return pltpu.make_async_remote_copy(
            src_ref=out_ref.at[gv, from_x, from_y], dst_ref=out_ref.at[gv, to_x, to_y],
            send_sem=rsend.at[step, no, piece[2] // 2], recv_sem=rrecv.at[step, no, piece[2] // 2],
            device_id=device(piece, step), device_id_type=MESH,
        )

    def rim_arrival(step, piece):
        (_, _, at_x), (_, _, at_y) = rim_span(piece)
        no = opposite(piece)
        half = lax.rem(gv - step + nv, nv)
        place = out_ref.at[half, at_x, at_y]
        return pltpu.make_async_remote_copy(
            src_ref=place, dst_ref=place,
            send_sem=rsend.at[step, no, piece[2] // 2], recv_sem=rrecv.at[step, no, piece[2] // 2],
            device_id=device(piece, -step + nv), device_id_type=MESH,
        )

    rims = (
        [(close, middle, 0)],
        [(far, middle, 0)],
        [
            (far, far, 2), (close, far, 2), (middle, far, 2), (far, middle, 2), (close, middle, 2),
            (middle, close, 2), (close, close, 2), (far, close, 2),
        ],
    )

    def for_rims(pieces, act):
        for piece in pieces:
            if piece[:2] in moves:

                @pl.when(inside(piece))
                def _():
                    act(piece)

    def totals(row, carry):
        around = smear_line(
            lambda i, j: wide_k[HALO + row + i, HALO + j], size_y, ANISOTROPY[0], ANISOTROPY[1]
        )
        for no in range(size_y):
            full_ref[row, no] = around[no] + SHIFT * wide_k[HALO + row, HALO + no]
        return carry

    mark, inverted, gather, eliminate, weigh = solver(c_ref.shape[3], depth, nv * vecs)

    def mark_own(cols, col, target):
        groups = column_groups(size_x, cols, col + HALO - 1)
        spots = [wide_c[pl.ds(rows.start + HALO - 1, GROUP), at] for rows, at in groups]
        for no, onehot in enumerate(mark(spots)):
            target[no] = onehot

    for part, group in enumerate((first, second, third)):
        for_each(group, lambda move: arrival(0, move).wait_recv())
        sweep_lines(1, part, gains)
        if part == 2:
            lax.fori_loop(0, size_x, totals, 0, unroll=2)
        for_each(group, lambda move: arrival(1, move).wait_recv())
        smooth(part)
        for step in range(1, nv):
            if part == 2:
                for_rims(rims[part], lambda piece: rim_departure(step, piece).start())
            block_copy(step, part, gv).start()
            if part < 2:
                for_rims(rims[part], lambda piece: rim_departure(step, piece).start())
        for_rims(rims[part], lambda piece: rim_departure(0, piece).start())
        if part == 0:
            for_each(moves, lambda move: departure(2, move).start())
            mark_own(size_y - HALO, pick(low_y, HALO + 1, 1), hot)
            mark_own(HALO, pick(low_y, 1, size_y - HALO + 1), late_hot)


    def early():
        groups = early_groups(size_x, size_y, low_x, low_y)
        knots = [fetch(knots_ref, group) for group in groups]
        inner_count = (size_y - HALO) * size_x // GROUP
        rim_groups = groups[inner_count:]
        onehots = mark([fetch(spots_ref, group) for group in rim_groups])
        for no, onehot in enumerate(onehots):
            hot[inner_count + no] = onehot
        gather(
            [
                (
                    jnp.concatenate([fetch(out_ref, group, (half,)) for half in range(nv)], axis=1),
                    inverted(knot),
                )
                for group, knot in zip(groups, knots)
            ],
            hot, right_h, right_l, gram_s,
        )
        gram_s[...] = eliminate(gram_s[...])
        for no in range(len(groups)):
            results = weigh([gram_s[no]], [(right_h[no], right_l[no])], [hot[no]], [knots[no]])
            for ref, value in zip((ch_ref, lh_ref, ll_ref, rh_ref, rl_ref), results[0]):
                ref[no] = value

    for_each(moves, lambda move: arrival(2, move).wait_recv())
    rim_x, rim_y = pl.ds(HALO - 1, size_x + 2), pl.ds(HALO - 1, size_y + 2)
    knots_ref[...] = wide_k[rim_x, rim_y]
    spots_ref[...] = wide_c[rim_x, rim_y]

    def wait_blocks(part):
        for step in range(1, nv):
            block_copy(step, part, lax.rem(gv - step + nv, nv)).wait_recv()

    def wait_rims(part):
        for step in range(nv):
            for_rims(rims[part], lambda piece: rim_arrival(step, piece).wait_recv())

    for part in range(2):
        wait_blocks(part)
        wait_rims(part)
    early()

    for part in range(3):
        for step in range(1, nv):
            block_copy(step, part, gv).wait_send()
        for step in range(nv):
            for_rims(rims[part], lambda piece: rim_departure(step, piece).wait_send())
    for kind in range(3):
        for_each(moves, lambda move: departure(kind, move).wait_send())
    wait_blocks(2)
    wait_rims(2)


def coarse_kernel(
    size_x, size_y, slots, ny, f_ref, k_ref, c_ref, ch_in, lh_in, ll_in, rh_in, rl_in, full_ref, own_hot,
    interp_ref, coarse_ref, hot, right_h, right_l, gram_s, lh, ll, rh, rl, ch, tiles, leave,
):
    nv, vecs, depth = f_ref.shape[0], f_ref.shape[3], f_ref.shape[4]
    wide_y = size_y + 2
    rows = GROUP * slots
    padded = -(-wide_y // GROUP) * GROUP
    band = size_y * slots
    low_x, low_y = lax.rem(lax.axis_index("gx"), 2) == 0, lax.axis_index("gy") > 0
    mark, inverted, gather, eliminate, weigh = solver(slots, depth, nv * vecs)
    places = (ch, lh, ll, rh, rl)

    groups = late_groups(size_x, size_y, ny, low_y)
    if ny <= 2:
        blank = (pl.ds(0, size_x + 2), pick(low_y, size_y + 1, 0))
        for ref in (rh, rl):
            ref[blank] = jnp.zeros((size_x + 2, slots, depth), BF16)

    knots = [fetch(k_ref, group) for group in groups]
    own_count = own_hot.shape[0]
    rim_hot = mark([fetch(c_ref, group) for group in groups[own_count:]])
    for no in range(len(groups)):
        hot[no] = own_hot[no] if no < own_count else rim_hot[no - own_count]
    gather(
        [
            (
                jnp.concatenate([fetch(f_ref, group, (half,)) for half in range(nv)], axis=1),
                inverted(knot),
            )
            for group, knot in zip(groups, knots)
        ],
        hot, right_h, right_l, gram_s,
    )
    for no, group in enumerate(early_groups(size_x, size_y, low_x, low_y)):
        for ref, source in zip(places, (ch_in, lh_in, ll_in, rh_in, rl_in)):
            place(ref, group, source[no])
    gram_s[...] = eliminate(gram_s[...])
    for first in range(0, len(groups), BATCH_2):
        batch = range(first, min(first + BATCH_2, len(groups)))
        results = weigh(
            [gram_s[no] for no in batch], [(right_h[no], right_l[no]) for no in batch],
            [hot[no] for no in batch], [knots[no] for no in batch],
        )
        for no, values in zip(batch, results):
            for ref, value in zip(places, values):
                place(ref, groups[no], value)

    half = GROUP * slots
    tall = (GROUP, half)
    lane_block, lane_in = lanes(tall) // slots, lanes(tall) % slots
    row_of = subs(tall)
    at_block = [lane_block == no for no in range(GROUP)]

    def lane_index(block):
        return block % GROUP * slots + lane_in

    skews = [lane_index(lane_block + row_of + shift) for shift in range(3)]
    sink = (row_of - lane_block + GROUP) % GROUP
    unskew = lane_index(row_of - lane_block + GROUP)

    def take(x, index, axis):
        return jnp.take_along_axis(x, index, axis=axis, mode="promise_in_bounds")

    def flat_tiles(origin, top, chunk, shift):
        parts = []
        for first in range(0, slots, GROUP):
            merged = None
            for no in range(GROUP):
                place = chunk + no + shift
                low = top + (chunk + no) * slots + first
                left_lane = place // GROUP * half
                values = origin[low : low + GROUP, left_lane : left_lane + half]
                here = at_block[place % GROUP]
                merged = values if merged is None else jnp.where(here, values, merged)
            parts.append(take(take(take(merged, skews[shift], 1), sink, 0), unskew, 1))
        return jnp.concatenate(parts, axis=1)

    def put(row, move_x, move_y, origin, top, shift):
        weight = 1.0
        if move_x != 0:
            weight = weight * ANISOTROPY[0]
        if move_y != 0:
            weight = weight * ANISOTROPY[1]
        for chunk in range(0, size_y, GROUP):
            tiles[row, 3 * (move_x + 1) + move_y + 1, chunk : chunk + GROUP, :] = (
                -weight * flat_tiles(origin, top, chunk, shift)
            )

    def mine(row):
        return row + 1, pl.ds(1, size_y)

    def central(row):
        left = (lh[mine(row)].reshape(band, depth), ll[mine(row)].reshape(band, depth))
        right = rh[mine(row)].astype(F32) + rl[mine(row)].astype(F32)
        centre = right - ch[mine(row)] * full_ref[row]
        put(row, 0, 0, dot3(left, split(centre.reshape(band, depth)), NT), 0, 0)

    def galerkin(line):
        other = (
            rh[line].reshape(padded * slots, depth), rl[line].reshape(padded * slots, depth),
        )
        near_rows = [row for row in range(line - 2, line + 1) if 0 <= row < size_x]
        left = [
            jnp.concatenate([ref[mine(row)].reshape(band, depth) for row in near_rows], axis=0)
            for ref in (lh, ll)
        ]
        product = dot3(left, other, NT)
        for no, row in enumerate(near_rows):
            for move_y in (-1, 0, 1):
                if (row + 1, move_y) != (line, 0):
                    put(row, line - row - 1, move_y, product, no * band, 1 + move_y)

    away = [
        (
            pltpu.make_async_copy(
                ch.at[mine(row)], interp_ref.at[row], leave.at[0, row]
            ),
            pltpu.make_async_copy(tiles.at[row], coarse_ref.at[row], leave.at[1, row]),
        )
        for row in range(size_x)
    ]
    for pair in away:
        pair[0].start()
    for line in range(size_x + 2):
        galerkin(line)
        if line < size_x:
            central(line)
        if line >= 2:
            away[line - 2][1].start()
    for pair in away:
        for copy in pair:
            copy.wait()


def stay(x):
    return pltpu.with_memory_space_constraint(x, pltpu.VMEM)


def body(nx, ny, nv, vectors, conductivity, c_points):
    vecs, size_x, size_y, depth = vectors.shape
    slots = c_points.shape[-1]
    wide_x, wide_y = size_x + 2 * HALO, size_y + 2 * HALO
    rows = GROUP * slots
    early = len(early_groups(size_x, size_y, True, True))
    made = [((early, GROUP, slots, depth), kind) for kind in (F32, BF16, BF16, BF16, BF16)]

    def work(count):
        return [
            pltpu.VMEM((count, rows, depth), BF16),
            pltpu.VMEM((count, rows, depth), BF16),
            pltpu.VMEM((count, slots, rows), F32),
        ]

    late = len(late_groups(size_x, size_y, ny, True))
    vmem = pl.BlockSpec(memory_space=pltpu.VMEM)
    hbm = pl.BlockSpec(memory_space=pl.ANY)
    dma = pltpu.SemaphoreType.DMA
    kept = pl.pallas_call(
        functools.partial(smooth_kernel, nx, ny, nv),
        out_shape=(
            pltpu.VMEM((nv, size_x + 2, size_y + 2, vecs, depth), F32),
            pltpu.VMEM((size_x + 2, size_y + 2, 1, depth), F32),
            pltpu.VMEM((size_x + 2, size_y + 2, 1, slots), jnp.int32),
            *(pltpu.VMEM(*one) for one in made),
            pltpu.VMEM((size_x, size_y, 1, depth), F32),
            pltpu.VMEM((HALO * size_x // GROUP, rows, depth), BF16),
        ),
        in_specs=[hbm] * 3,
        out_specs=(vmem,) * 10,
        scratch_shapes=[
            pltpu.VMEM((wide_x, wide_y, vecs, depth), F32),
            pltpu.VMEM((wide_x, wide_y, vecs, depth), F32),
            pltpu.VMEM((wide_x, wide_y, vecs, depth), F32),
            pltpu.VMEM((wide_x, wide_y, vecs, depth), F32),
            pltpu.VMEM((wide_x, wide_y, 1, depth), F32),
            pltpu.VMEM((wide_x, wide_y, 1, slots), jnp.int32),
            dma((3, 9)), dma((3, 9)), dma((nv, 3)), dma((nv, 3)), dma((nv, 9, 2)), dma((nv, 9, 2)),
            dma((vecs,)), dma((2,)), pltpu.VMEM((early, rows, depth), BF16),
            *work(early),
        ],
        compiler_params=pltpu.CompilerParams(collective_id=0, has_side_effects=True),
        name="smooth",
    )(vectors, conductivity[:, :, None, :], c_points[:, :, None, :])
    grid = (size_x + 2, -(-(size_y + 2) // GROUP) * GROUP, slots, depth)
    interp, coarse = pl.pallas_call(
        functools.partial(coarse_kernel, size_x, size_y, slots, ny),
        out_shape=(
            jax.ShapeDtypeStruct((size_x, size_y, slots, depth), F32),
            jax.ShapeDtypeStruct((size_x, 9, size_y, slots * slots), F32),
        ),
        in_specs=[vmem] * 10,
        out_specs=(hbm, hbm),
        scratch_shapes=[
            pltpu.VMEM((late, rows, depth), BF16), *work(late),
            pltpu.VMEM(grid, BF16), pltpu.VMEM(grid, BF16), pltpu.VMEM(grid, BF16),
            pltpu.VMEM(grid, BF16), pltpu.VMEM(grid, F32),
            pltpu.VMEM((size_x, 9, size_y, slots * slots), F32),
            dma((2, size_x)),
        ],
        name="coarse",
    )(*(stay(one) for one in kept))
    return interp, jnp.transpose(coarse, (0, 2, 1, 3))


def solution(mesh):
    placed = (P("vert", "gx", "gy", None), P("gx", "gy", None), P("gx", "gy", None))
    return jax.shard_map(
        functools.partial(body, mesh.shape["gx"], mesh.shape["gy"], mesh.shape["vert"]),
        mesh=mesh,
        in_specs=placed,
        out_specs=(P("gx", "gy", None, None), P("gx", "gy", None, None)),
        check_vma=False,
    )
```

```python
import functools

import jax
import jax.numpy as jnp
from jax import lax
from jax.experimental import pallas as pl
from jax.experimental.pallas import tpu as pltpu
from jax.sharding import PartitionSpec as P

SWEEPS = 3
ANISOTROPY = (1.0, 0.6, 0.15)
OMEGA = 0.6
SHIFT = 0.5
RIDGE = 0.1
HALO = SWEEPS
INNER, BESIDE = -1, -2
GROUP = 8
BATCH_2 = 5
MESH = pl.DeviceIdType.MESH
F32 = jnp.float32
BF16 = jnp.bfloat16


def smear_z(x):
    axis = x.ndim - 1
    depth = x.shape[axis]
    lane = lax.broadcasted_iota(jnp.int32, x.shape, axis)
    below = jnp.where(lane == 0, 0.0, pltpu.roll(x, 1, axis))
    above = jnp.where(lane == depth - 1, 0.0, pltpu.roll(x, depth - 1, axis))
    return x + ANISOTROPY[2] * (below + above)


def smear_line(get, count, across, along):
    summed = [get(0, no) + across * (get(-1, no) + get(1, no)) for no in range(-1, count + 1)]
    return [
        smear_z(summed[no + 1] + along * (summed[no] + summed[no + 2])) for no in range(count)
    ]


def pick(low, first, second):
    if isinstance(low, bool):
        return first if low else second
    return jnp.where(low, jnp.int32(first), jnp.int32(second))


def split(x):
    high = x.astype(BF16)
    return high, (x - high.astype(F32)).astype(BF16)


NT = (((1,), (1,)), ((), ()))
NN = (((1,), (0,)), ((), ()))


def dot(a, b, dims):
    return lax.dot_general(a, b, dims, preferred_element_type=F32)


def dot3(a, b, dims):
    along = dims[0][1][0]
    both = dot(jnp.concatenate([a[0], a[0]], axis=1), jnp.concatenate(b, axis=along), dims)
    return both + dot(a[1], b[0], dims)


def lanes(shape):
    return lax.broadcasted_iota(jnp.int32, shape, len(shape) - 1)


def subs(shape):
    return lax.broadcasted_iota(jnp.int32, shape, len(shape) - 2)


def solver(slots, depth, own):
    rows = GROUP * slots
    members = GROUP * own
    same = subs((rows, members)) // slots == lanes((rows, members)) // own
    same_slots = subs((rows, rows)) // slots == lanes((rows, rows)) // slots
    own_lane = subs((rows, slots)) % slots == lanes((rows, slots))
    ones = jnp.ones((slots, depth), BF16)

    def mark(places):
        onehots = []
        for spots in places:
            spots = jnp.broadcast_to(spots.astype(F32), (GROUP, slots, slots)).reshape(rows, slots)
            spread = dot(jnp.where(own_lane, spots, 0.0).astype(BF16), ones, NN)
            onehots.append(
                jnp.where(spread == lanes((rows, depth)).astype(F32), 1.0, 0.0).astype(BF16)
            )
        return onehots

    def inverted(knots):
        alive = knots > 0.0
        return jnp.where(alive, 1.0 / jnp.where(alive, knots, 1.0), 0.0)

    def gather(cells, hot, right_h, right_l, gram_s):
        fields = [split((field * inverse).reshape(members, depth)) for field, inverse in cells]
        pairs = []
        for no, (high, low) in enumerate(fields):
            onehot = hot[no]
            twice = jnp.concatenate([onehot, onehot], axis=1)
            pairs.append(dot(twice, jnp.concatenate([high, low], axis=1), NT))
        pairs = [split(jnp.where(same, cvals, 0.0)) for cvals in pairs]
        grams = [dot3(pair, pair, NT) for pair in pairs]
        rights = [dot3(pair, field, NN) for pair, field in zip(pairs, fields)]
        for no, (gram, right) in enumerate(zip(grams, rights)):
            gram_s[no] = jnp.sum(gram.reshape(GROUP, slots, rows), axis=0)
            high, low = split(right)
            right_h[no] = high
            right_l[no] = low

    def eliminate(system):
        shape = system.shape
        lane = lanes(shape) % slots
        sub = subs(shape)
        diagonal = jnp.sum(jnp.where(lane == sub, system, 0.0), axis=1)
        block = jnp.where(same_slots, 1.0, 0.0).astype(BF16)
        first = diagonal.astype(BF16)
        rest = diagonal - first.astype(F32)
        second = rest.astype(BF16)
        third = (rest - second.astype(F32)).astype(BF16)
        trace = dot(first, block, NN) + dot(second, block, NN) + dot(third, block, NN)
        ridge = RIDGE * trace / slots + 1e-06
        system = system + jnp.where(lane == sub, ridge[:, None, :], 0.0)
        flat = (shape[0] * slots, rows)
        base = lanes(flat) // slots * slots

        def column(values, no):
            return jnp.take_along_axis(
                values.reshape(flat), base + no, axis=1, mode="promise_in_bounds"
            ).reshape(shape)

        now, ahead, pending = (column(system, no) for no in range(3))
        for pivot in range(slots):
            line = slice(pivot, pivot + 1)
            mine = sub == pivot
            inverse = 1.0 / now[:, line]
            scaled = jnp.where(lane[:, 0:1] == pivot, 1.0, system[:, line]) * inverse

            def advance(values):
                step = values[:, line] * inverse
                return jnp.where(mine, step, values - now * step)

            system = jnp.where(mine, scaled, jnp.where(lane == pivot, 0.0, system) - now * scaled)
            now, ahead = advance(ahead), advance(pending)
            pending = column(system, min(pivot + 3, slots - 1))
        return system

    def weigh(inverses, rights, onehots, knots):
        blocks = [
            split(
                jnp.where(
                    same_slots,
                    jnp.broadcast_to(inverse[None], (GROUP, slots, rows)).reshape(rows, rows),
                    0.0,
                )
            )
            for inverse in inverses
        ]
        solved = [dot3(block, right, NN) for block, right in zip(blocks, rights)]
        result = []
        for weights, onehot, knot in zip(solved, onehots, knots):
            onehot = onehot.astype(F32).reshape(GROUP, slots, depth)
            crow = jnp.sum(onehot, axis=1, keepdims=True)
            value = weights.reshape(GROUP, slots, depth) * (1.0 - crow) + onehot
            left = value * knot
            smeared = smear_z(left.reshape(rows, depth)).reshape(GROUP, slots, depth)
            result.append((value,) + split(left) + split(smeared))
        return result

    return mark, inverted, gather, eliminate, weigh


def column_groups(size_x, cols, col):
    return [
        (pl.ds(first + 1, GROUP), col + no)
        for first in range(0, size_x, GROUP)
        for no in range(cols)
    ]


def packed(cells):
    groups = [cells[first : first + GROUP] for first in range(0, len(cells), GROUP)]
    return [group + group[:1] * (GROUP - len(group)) for group in groups]


def early_groups(size_x, size_y, low_x, low_y):
    cols, col = size_y - HALO, pick(low_y, HALO + 1, 1)
    rows = (pick(low_x, size_x + 1, 0), pick(low_x, 0, size_x + 1))
    return column_groups(size_x, cols, col) + packed(
        [(row, col + no) for row in rows for no in range(cols)]
    )


def late_groups(size_x, size_y, ny, low_y):
    col = pick(low_y, 1, size_y - HALO + 1)
    rims = [pick(low_y, 0, size_y + 1)] + ([] if ny <= 2 else [pick(low_y, size_y + 1, 0)])
    groups = column_groups(size_x, HALO, col)
    for rim in rims:
        groups += column_groups(size_x, 1, rim)
    cols = [col + no for no in range(HALO)] + rims
    return groups + packed([(row, at) for row in (0, size_x + 1) for at in cols])


def fetch(ref, group, lead=()):
    if isinstance(group, tuple):
        return ref[lead + group]
    return jnp.stack([ref[lead + at] for at in group], axis=0)


def place(ref, group, value):
    if isinstance(group, tuple):
        ref[group] = value
    else:
        for no, at in enumerate(group):
            if no == 0 or at is not group[0]:
                ref[at] = value[no]


def smooth_kernel(
    nx, ny, nv, raw_ref, k_ref, c_ref, out_ref, knots_ref, spots_ref,
    ch_ref, lh_ref, ll_ref, rh_ref, rl_ref, full_ref, late_hot,
    one, two, three, gain, wide_k, wide_c, hsend, hrecv, fsend, frecv, rsend, rrecv, turn, load,
    hot, right_h, right_l, gram_s,
):
    size_x, size_y, depth = k_ref.shape[0], k_ref.shape[1], k_ref.shape[3]
    vecs = raw_ref.shape[0]
    wide_x, wide_y = size_x + 2 * HALO, size_y + 2 * HALO
    gx, gy, gv = lax.axis_index("gx"), lax.axis_index("gy"), lax.axis_index("vert")
    near = 1 - 2 * lax.rem(gx, 2)
    far_x = -near
    far_y = pick(gy > 0, -1, 1)
    low_x, low_y = far_x < 0, far_y < 0
    sides_x, sides_y = (0, near, far_x), (0, -far_y, far_y)
    middle, close, far = 0, 1, 2
    moves = [(mx, my) for mx in range(3) for my in range(3) if (mx, my) != (0, 0)]
    if ny <= 2:
        missing = [move for move in moves if move[1] == close]
        moves = [move for move in moves if move[1] != close]
    else:
        missing = []

    inner = pl.ds(HALO, size_x), pl.ds(HALO, size_y)
    loads = [
        pltpu.make_async_copy(source, target.at[inner], load.at[no])
        for no, (source, target) in enumerate(((k_ref, wide_k), (c_ref, wide_c)))
    ]
    turns = [
        pltpu.make_async_copy(raw_ref.at[vec], one.at[inner[0], inner[1], vec], turn.at[vec])
        for vec in range(vecs)
    ]
    for copy in loads + turns:
        copy.start()

    def inside(move):
        at_x, at_y = gx + sides_x[move[0]], gy + sides_y[move[1]]
        ok_x = jnp.logical_and(at_x >= 0, at_x < nx)
        return jnp.logical_and(ok_x, jnp.logical_and(at_y >= 0, at_y < ny))

    def device(move, step=0):
        return (gx + sides_x[move[0]], gy + sides_y[move[1]], lax.rem(gv + step, nv))

    def number(move):
        return 3 * (sides_x[move[0]] + 1) + sides_y[move[1]] + 1

    def opposite(move):
        return 3 * (1 - sides_x[move[0]]) + 1 - sides_y[move[1]]

    barrier = pltpu.get_barrier_semaphore()
    total = jnp.int32(nv - 1)
    for move in moves:
        here = inside(move)

        @pl.when(here)
        def _():
            pl.semaphore_signal(barrier, inc=1, device_id=device(move), device_id_type=MESH)

        total = total + here.astype(jnp.int32)
    for step in range(1, nv):
        pl.semaphore_signal(
            barrier, inc=1, device_id=device((0, 0), step), device_id_type=MESH
        )

    def side(sides, which, size, width, out):
        if which == middle:
            return pl.ds(0 if out else width, size), pl.ds(width, size)
        base = 0 if out else width
        low = sides[which] < 0
        return (
            pl.ds(base + pick(low, 0, size - width), width),
            pl.ds(pick(low, size + width, 0), width),
        )

    def hole(sides, which, size, width):
        if which == middle:
            return pl.ds(width, size)
        return pl.ds(pick(sides[which] < 0, 0, size + width), width)

    fills = ((wide_k, F32), (wide_c, jnp.int32), (one, F32))

    def clear(move):
        at_x, at_y = hole(sides_x, move[0], size_x, HALO), hole(sides_y, move[1], size_y, HALO)
        for target, kind in fills:
            target[at_x, at_y] = jnp.zeros((at_x.size, at_y.size) + target.shape[2:], kind)
        at_x, at_y = hole(sides_x, move[0], size_x, 1), hole(sides_y, move[1], size_y, 1)
        out_ref[:, at_x, at_y] = jnp.zeros((nv, at_x.size, at_y.size, vecs, depth), F32)

    for move in missing:
        clear(move)
    for move in moves:

        @pl.when(jnp.logical_not(inside(move)))
        def _():
            clear(move)

    for copy in loads + turns:
        copy.wait()

    def scale(row, carry):
        for col in range(HALO, HALO + size_y):
            factor = jnp.broadcast_to(wide_k[row, col], (vecs, depth))
            one[row, col] = one[row, col] * factor
        return carry

    lax.fori_loop(HALO, HALO + size_x, scale, 0, unroll=2)
    pl.semaphore_wait(barrier, total)

    kinds = (wide_k, one, wide_c)

    def departure(kind, move):
        from_x, to_x = side(sides_x, move[0], size_x, HALO, False)
        from_y, to_y = side(sides_y, move[1], size_y, HALO, False)
        no = number(move)
        return pltpu.make_async_remote_copy(
            src_ref=kinds[kind].at[from_x, from_y], dst_ref=kinds[kind].at[to_x, to_y],
            send_sem=hsend.at[kind, no], recv_sem=hrecv.at[kind, no],
            device_id=device(move), device_id_type=MESH,
        )

    def arrival(kind, move):
        no = opposite(move)
        place = kinds[kind].at[
            hole(sides_x, move[0], size_x, HALO), hole(sides_y, move[1], size_y, HALO)
        ]
        return pltpu.make_async_remote_copy(
            src_ref=place, dst_ref=place, send_sem=hsend.at[kind, no], recv_sem=hrecv.at[kind, no],
            device_id=device(move), device_id_type=MESH,
        )

    def for_each(some, act):
        for move in some:
            if move in moves:

                @pl.when(inside(move))
                def _():
                    act(move)

    first = [(close, middle), (middle, close), (close, close)]
    second = [(far, middle), (far, close)]
    third = [(middle, far), (close, far), (far, far)]

    def leave(move):
        departure(0, move).start()
        departure(1, move).start()

    for_each(first[:1] + third[:1] + second[:1] + third[1:] + first[1:] + second[1:], leave)

    def start(low, sweep, wide, whole):
        if whole:
            return pick(low, HALO + sweep, sweep)
        return pick(low, sweep, wide - HALO - sweep)

    def region_rows(sweep, part):
        if part == INNER:
            return HALO + sweep, size_x - 2 * sweep
        if part == BESIDE:
            return pick(low_x, HALO + size_x - sweep, sweep), HALO
        if part == 2:
            return sweep, wide_x - 2 * sweep
        if part == 1:
            return start(low_x, sweep, wide_x, False), HALO
        return start(low_x, sweep, wide_x, True), wide_x - HALO - 2 * sweep

    def region_cols(sweep, part):
        if part == 2:
            return start(low_y, sweep, wide_y, False), HALO
        return start(low_y, sweep, wide_y, True), wide_y - HALO - 2 * sweep

    def sweep_lines(sweep, part, act):
        row, rows = region_rows(sweep, part)
        col, cols = region_cols(sweep, part)
        if part == 2:

            def step(no, carry):
                act(lambda i, j: (row + j, col + no + i), rows, ANISOTROPY[1], ANISOTROPY[0])
                return carry

            lax.fori_loop(0, cols, step, 0, unroll=True)
        else:

            def step(no, carry):
                act(lambda i, j: (row + no + i, col + j), cols, ANISOTROPY[0], ANISOTROPY[1])
                return carry

            lax.fori_loop(0, rows, step, 0, unroll=True)

    def gains(at, count, across, along):
        around = smear_line(lambda i, j: wide_k[at(i, j)], count, across, along)
        for no in range(count):
            mid = wide_k[at(0, no)]
            below = around[no] - (1.0 - SHIFT) * mid
            alive = mid > 0.0
            value = jnp.where(alive, OMEGA * mid / jnp.where(alive, below, 1.0), 0.0)
            gain[at(0, no)] = jnp.broadcast_to(value, (vecs, depth))

    def relax(source, target, at, count, across, along):
        around = smear_line(lambda i, j: source[at(i, j)], count, across, along)
        for no in range(count):
            factor = gain[at(0, no)]
            target(at(0, no), (1.0 - OMEGA - factor) * source[at(0, no)] + factor * around[no])

    def keep(ref):
        def store(at, value):
            ref[at] = value

        return store

    def final(at, value):
        out_ref[gv, at[0] - HALO + 1, at[1] - HALO + 1] = value

    def smooth(part):
        buffers = (one, two, three)
        for sweep in range(1, SWEEPS + 1):
            source = buffers[(sweep - 1) % 3]
            target = final if sweep == SWEEPS else keep(buffers[sweep % 3])
            sweep_lines(sweep, part, functools.partial(relax, source, target))

    def block_copy(step, part, half):
        row, rows = region_rows(SWEEPS, part)
        col, cols = region_cols(SWEEPS, part)
        place = out_ref.at[half, pl.ds(row - HALO + 1, rows), pl.ds(col - HALO + 1, cols)]
        return pltpu.make_async_remote_copy(
            src_ref=place, dst_ref=place,
            send_sem=fsend.at[step - 1, part], recv_sem=frecv.at[step - 1, part],
            device_id=device((0, 0), step), device_id_type=MESH,
        )

    def edge(sides, which, size):
        if which == middle:
            return pl.ds(1, size), pl.ds(1, size), pl.ds(1, size)
        low = sides[which] < 0
        return (
            pl.ds(pick(low, 1, size), 1), pl.ds(pick(low, size + 1, 0), 1),
            pl.ds(pick(low, 0, size + 1), 1),
        )

    def rim_span(piece):
        mx, my, part = piece
        over_x, over_y = edge(sides_x, mx, size_x), edge(sides_y, my, size_y)
        if my == middle:
            col, cols = region_cols(SWEEPS, part)
            over_y = (pl.ds(col - HALO + 1, cols),) * 3
        return over_x, over_y

    def rim_departure(step, piece):
        (from_x, to_x, _), (from_y, to_y, _) = rim_span(piece)
        no = number(piece)
        return pltpu.make_async_remote_copy(
            src_ref=out_ref.at[gv, from_x, from_y], dst_ref=out_ref.at[gv, to_x, to_y],
            send_sem=rsend.at[step, no, piece[2] // 2], recv_sem=rrecv.at[step, no, piece[2] // 2],
            device_id=device(piece, step), device_id_type=MESH,
        )

    def rim_arrival(step, piece):
        (_, _, at_x), (_, _, at_y) = rim_span(piece)
        no = opposite(piece)
        half = lax.rem(gv - step + nv, nv)
        place = out_ref.at[half, at_x, at_y]
        return pltpu.make_async_remote_copy(
            src_ref=place, dst_ref=place,
            send_sem=rsend.at[step, no, piece[2] // 2], recv_sem=rrecv.at[step, no, piece[2] // 2],
            device_id=device(piece, -step + nv), device_id_type=MESH,
        )

    rims = (
        [(close, middle, 0)],
        [(far, middle, 0)],
        [
            (far, far, 2), (close, far, 2), (middle, far, 2), (far, middle, 2), (close, middle, 2),
            (middle, close, 2), (close, close, 2), (far, close, 2),
        ],
    )

    def for_rims(pieces, act):
        for piece in pieces:
            if piece[:2] in moves:

                @pl.when(inside(piece))
                def _():
                    act(piece)

    def totals(row, carry):
        around = smear_line(
            lambda i, j: wide_k[HALO + row + i, HALO + j], size_y, ANISOTROPY[0], ANISOTROPY[1]
        )
        for no in range(size_y):
            full_ref[row, no] = around[no] + SHIFT * wide_k[HALO + row, HALO + no]
        return carry

    mark, inverted, gather, eliminate, weigh = solver(c_ref.shape[3], depth, nv * vecs)

    def mark_own(cols, col, target):
        groups = column_groups(size_x, cols, col + HALO - 1)
        spots = [wide_c[pl.ds(rows.start + HALO - 1, GROUP), at] for rows, at in groups]
        for no, onehot in enumerate(mark(spots)):
            target[no] = onehot

    for part, group in enumerate((first, second, third)):
        if part == 0 and ny <= 2:
            sweep_lines(1, INNER, gains)
            smooth(INNER)
        for_each(group, lambda move: arrival(0, move).wait_recv())
        sweep_lines(1, BESIDE if part == 0 and ny <= 2 else part, gains)
        if part == 2:
            lax.fori_loop(0, size_x, totals, 0, unroll=2)
        for_each(group, lambda move: arrival(1, move).wait_recv())
        smooth(BESIDE if part == 0 and ny <= 2 else part)
        for step in range(1, nv):
            if part == 2:
                for_rims(rims[part], lambda piece: rim_departure(step, piece).start())
            block_copy(step, part, gv).start()
            if part < 2:
                for_rims(rims[part], lambda piece: rim_departure(step, piece).start())
        for_rims(rims[part], lambda piece: rim_departure(0, piece).start())
        if part == 0:
            for_each(moves, lambda move: departure(2, move).start())
            mark_own(size_y - HALO, pick(low_y, HALO + 1, 1), hot)
            mark_own(HALO, pick(low_y, 1, size_y - HALO + 1), late_hot)


    def early():
        groups = early_groups(size_x, size_y, low_x, low_y)
        knots = [fetch(knots_ref, group) for group in groups]
        inner_count = (size_y - HALO) * size_x // GROUP
        rim_groups = groups[inner_count:]
        onehots = mark([fetch(spots_ref, group) for group in rim_groups])
        for no, onehot in enumerate(onehots):
            hot[inner_count + no] = onehot
        gather(
            [
                (
                    jnp.concatenate([fetch(out_ref, group, (half,)) for half in range(nv)], axis=1),
                    inverted(knot),
                )
                for group, knot in zip(groups, knots)
            ],
            hot, right_h, right_l, gram_s,
        )
        gram_s[...] = eliminate(gram_s[...])
        for no in range(len(groups)):
            results = weigh([gram_s[no]], [(right_h[no], right_l[no])], [hot[no]], [knots[no]])
            for ref, value in zip((ch_ref, lh_ref, ll_ref, rh_ref, rl_ref), results[0]):
                ref[no] = value

    for_each(moves, lambda move: arrival(2, move).wait_recv())
    rim_x, rim_y = pl.ds(HALO - 1, size_x + 2), pl.ds(HALO - 1, size_y + 2)
    knots_ref[...] = wide_k[rim_x, rim_y]
    spots_ref[...] = wide_c[rim_x, rim_y]

    def wait_blocks(part):
        for step in range(1, nv):
            block_copy(step, part, lax.rem(gv - step + nv, nv)).wait_recv()

    def wait_rims(part):
        for step in range(nv):
            for_rims(rims[part], lambda piece: rim_arrival(step, piece).wait_recv())

    for part in range(2):
        wait_blocks(part)
        wait_rims(part)
    early()

    for part in range(3):
        for step in range(1, nv):
            block_copy(step, part, gv).wait_send()
        for step in range(nv):
            for_rims(rims[part], lambda piece: rim_departure(step, piece).wait_send())
    for kind in range(3):
        for_each(moves, lambda move: departure(kind, move).wait_send())
    wait_blocks(2)
    wait_rims(2)


def coarse_kernel(
    size_x, size_y, slots, ny, f_ref, k_ref, c_ref, ch_in, lh_in, ll_in, rh_in, rl_in, full_ref, own_hot,
    interp_ref, coarse_ref, hot, right_h, right_l, gram_s, lh, ll, rh, rl, ch, tiles, leave,
):
    nv, vecs, depth = f_ref.shape[0], f_ref.shape[3], f_ref.shape[4]
    wide_y = size_y + 2
    rows = GROUP * slots
    padded = -(-wide_y // GROUP) * GROUP
    band = size_y * slots
    low_x, low_y = lax.rem(lax.axis_index("gx"), 2) == 0, lax.axis_index("gy") > 0
    mark, inverted, gather, eliminate, weigh = solver(slots, depth, nv * vecs)
    places = (ch, lh, ll, rh, rl)

    groups = late_groups(size_x, size_y, ny, low_y)
    if ny <= 2:
        blank = (pl.ds(0, size_x + 2), pick(low_y, size_y + 1, 0))
        for ref in (rh, rl):
            ref[blank] = jnp.zeros((size_x + 2, slots, depth), BF16)

    knots = [fetch(k_ref, group) for group in groups]
    own_count = own_hot.shape[0]
    rim_hot = mark([fetch(c_ref, group) for group in groups[own_count:]])
    for no in range(len(groups)):
        hot[no] = own_hot[no] if no < own_count else rim_hot[no - own_count]
    gather(
        [
            (
                jnp.concatenate([fetch(f_ref, group, (half,)) for half in range(nv)], axis=1),
                inverted(knot),
            )
            for group, knot in zip(groups, knots)
        ],
        hot, right_h, right_l, gram_s,
    )
    for no, group in enumerate(early_groups(size_x, size_y, low_x, low_y)):
        for ref, source in zip(places, (ch_in, lh_in, ll_in, rh_in, rl_in)):
            place(ref, group, source[no])
    gram_s[...] = eliminate(gram_s[...])
    for first in range(0, len(groups), BATCH_2):
        batch = range(first, min(first + BATCH_2, len(groups)))
        results = weigh(
            [gram_s[no] for no in batch], [(right_h[no], right_l[no]) for no in batch],
            [hot[no] for no in batch], [knots[no] for no in batch],
        )
        for no, values in zip(batch, results):
            for ref, value in zip(places, values):
                place(ref, groups[no], value)

    half = GROUP * slots
    tall = (GROUP, half)
    lane_block, lane_in = lanes(tall) // slots, lanes(tall) % slots
    row_of = subs(tall)
    at_block = [lane_block == no for no in range(GROUP)]

    def lane_index(block):
        return block % GROUP * slots + lane_in

    skews = [lane_index(lane_block + row_of + shift) for shift in range(3)]
    sink = (row_of - lane_block + GROUP) % GROUP
    unskew = lane_index(row_of - lane_block + GROUP)

    def take(x, index, axis):
        return jnp.take_along_axis(x, index, axis=axis, mode="promise_in_bounds")

    def flat_tiles(origin, top, chunk, shift):
        parts = []
        for first in range(0, slots, GROUP):
            merged = None
            for no in range(GROUP):
                place = chunk + no + shift
                low = top + (chunk + no) * slots + first
                left_lane = place // GROUP * half
                values = origin[low : low + GROUP, left_lane : left_lane + half]
                here = at_block[place % GROUP]
                merged = values if merged is None else jnp.where(here, values, merged)
            parts.append(take(take(take(merged, skews[shift], 1), sink, 0), unskew, 1))
        return jnp.concatenate(parts, axis=1)

    def put(row, move_x, move_y, origin, top, shift):
        weight = 1.0
        if move_x != 0:
            weight = weight * ANISOTROPY[0]
        if move_y != 0:
            weight = weight * ANISOTROPY[1]
        for chunk in range(0, size_y, GROUP):
            tiles[row, 3 * (move_x + 1) + move_y + 1, chunk : chunk + GROUP, :] = (
                -weight * flat_tiles(origin, top, chunk, shift)
            )

    def mine(row):
        return row + 1, pl.ds(1, size_y)

    def central(row):
        left = (lh[mine(row)].reshape(band, depth), ll[mine(row)].reshape(band, depth))
        right = rh[mine(row)].astype(F32) + rl[mine(row)].astype(F32)
        centre = right - ch[mine(row)] * full_ref[row]
        put(row, 0, 0, dot3(left, split(centre.reshape(band, depth)), NT), 0, 0)

    def galerkin(line):
        other = (
            rh[line].reshape(padded * slots, depth), rl[line].reshape(padded * slots, depth),
        )
        near_rows = [row for row in range(line - 2, line + 1) if 0 <= row < size_x]
        left = [
            jnp.concatenate([ref[mine(row)].reshape(band, depth) for row in near_rows], axis=0)
            for ref in (lh, ll)
        ]
        product = dot3(left, other, NT)
        for no, row in enumerate(near_rows):
            for move_y in (-1, 0, 1):
                if (row + 1, move_y) != (line, 0):
                    put(row, line - row - 1, move_y, product, no * band, 1 + move_y)

    away = [
        (
            pltpu.make_async_copy(
                ch.at[mine(row)], interp_ref.at[row], leave.at[0, row]
            ),
            pltpu.make_async_copy(tiles.at[row], coarse_ref.at[row], leave.at[1, row]),
        )
        for row in range(size_x)
    ]
    for pair in away:
        pair[0].start()
    for line in range(size_x + 2):
        galerkin(line)
        if line < size_x:
            central(line)
        if line >= 2:
            away[line - 2][1].start()
    for pair in away:
        for copy in pair:
            copy.wait()


def stay(x):
    return pltpu.with_memory_space_constraint(x, pltpu.VMEM)


def body(nx, ny, nv, vectors, conductivity, c_points):
    vecs, size_x, size_y, depth = vectors.shape
    slots = c_points.shape[-1]
    wide_x, wide_y = size_x + 2 * HALO, size_y + 2 * HALO
    rows = GROUP * slots
    early = len(early_groups(size_x, size_y, True, True))
    made = [((early, GROUP, slots, depth), kind) for kind in (F32, BF16, BF16, BF16, BF16)]

    def work(count):
        return [
            pltpu.VMEM((count, rows, depth), BF16),
            pltpu.VMEM((count, rows, depth), BF16),
            pltpu.VMEM((count, slots, rows), F32),
        ]

    late = len(late_groups(size_x, size_y, ny, True))
    vmem = pl.BlockSpec(memory_space=pltpu.VMEM)
    hbm = pl.BlockSpec(memory_space=pl.ANY)
    dma = pltpu.SemaphoreType.DMA
    kept = pl.pallas_call(
        functools.partial(smooth_kernel, nx, ny, nv),
        out_shape=(
            pltpu.VMEM((nv, size_x + 2, size_y + 2, vecs, depth), F32),
            pltpu.VMEM((size_x + 2, size_y + 2, 1, depth), F32),
            pltpu.VMEM((size_x + 2, size_y + 2, 1, slots), jnp.int32),
            *(pltpu.VMEM(*one) for one in made),
            pltpu.VMEM((size_x, size_y, 1, depth), F32),
            pltpu.VMEM((HALO * size_x // GROUP, rows, depth), BF16),
        ),
        in_specs=[hbm] * 3,
        out_specs=(vmem,) * 10,
        scratch_shapes=[
            pltpu.VMEM((wide_x, wide_y, vecs, depth), F32),
            pltpu.VMEM((wide_x, wide_y, vecs, depth), F32),
            pltpu.VMEM((wide_x, wide_y, vecs, depth), F32),
            pltpu.VMEM((wide_x, wide_y, vecs, depth), F32),
            pltpu.VMEM((wide_x, wide_y, 1, depth), F32),
            pltpu.VMEM((wide_x, wide_y, 1, slots), jnp.int32),
            dma((3, 9)), dma((3, 9)), dma((nv, 3)), dma((nv, 3)), dma((nv, 9, 2)), dma((nv, 9, 2)),
            dma((vecs,)), dma((2,)), pltpu.VMEM((early, rows, depth), BF16),
            *work(early),
        ],
        compiler_params=pltpu.CompilerParams(collective_id=0, has_side_effects=True),
        name="smooth",
    )(vectors, conductivity[:, :, None, :], c_points[:, :, None, :])
    grid = (size_x + 2, -(-(size_y + 2) // GROUP) * GROUP, slots, depth)
    interp, coarse = pl.pallas_call(
        functools.partial(coarse_kernel, size_x, size_y, slots, ny),
        out_shape=(
            jax.ShapeDtypeStruct((size_x, size_y, slots, depth), F32),
            jax.ShapeDtypeStruct((size_x, 9, size_y, slots * slots), F32),
        ),
        in_specs=[vmem] * 10,
        out_specs=(hbm, hbm),
        scratch_shapes=[
            pltpu.VMEM((late, rows, depth), BF16), *work(late),
            pltpu.VMEM(grid, BF16), pltpu.VMEM(grid, BF16), pltpu.VMEM(grid, BF16),
            pltpu.VMEM(grid, BF16), pltpu.VMEM(grid, F32),
            pltpu.VMEM((size_x, 9, size_y, slots * slots), F32),
            dma((2, size_x)),
        ],
        name="coarse",
    )(*(stay(one) for one in kept))
    return interp, jnp.transpose(coarse, (0, 2, 1, 3))


def solution(mesh):
    placed = (P("vert", "gx", "gy", None), P("gx", "gy", None), P("gx", "gy", None))
    return jax.shard_map(
        functools.partial(body, mesh.shape["gx"], mesh.shape["gy"], mesh.shape["vert"]),
        mesh=mesh,
        in_specs=placed,
        out_specs=(P("gx", "gy", None, None), P("gx", "gy", None, None)),
        check_vma=False,
    )
```
